256 devices in a mesh: seq: 32 (over y, z), dp: 2 (over core), head: 4 (over x).
Axes of the slice: x: 4, y: 4, z: 8, core: 2. Of those that a mesh axis runs over, the one named last changes fastest.
Arguments:
- inputs: bfloat16 [2, 12288, 3072], P('dp', 'seq'), may hold values from -40 to 40
- w_query: bfloat16 [3072, 2048], P(None, 'head'), may hold values from -0.21650635 to 0.21650635
- w_key: bfloat16 [3072, 2048], P(None, 'head'), may hold values from -0.07216878 to 0.07216878
- w_value: bfloat16 [3072, 2048], P(None, 'head'), may hold values from -0.108253175 to 0.108253175
- gate_bias: float32 [8], P('head'), may hold values from 0 to 2.5
- cotangent: bfloat16 [2, 12288, 2048], P('dp', 'seq', 'head'), may hold values from -8 to 8
Outputs:
- blended: bfloat16 [2, 12288, 2048], P('dp', 'seq', 'head')
- grad_weights: float32 [3072, 3, 2048], P(('seq', 'dp'), None, 'head')
The draws below stay inside these ranges and needn't reach their ends.
All inputs are finite; a program needn't handle non-finite values.
Results may differ from the reference program's by a relative error of at most 0.012.
Values may be sent and summed in bfloat16 or wider, within the bound.
A program may use at most 128 MiB of HBM per device.

```python
import math
import jax
import jax.numpy as jnp
from jax import lax

D = 3072
HEADS = 8
HDIM = 256
SEG = 384
BATCH = 2
LENGTH = 12288


def shared_mean(key):
    raw = jax.random.normal(jax.random.fold_in(key, 101), (D,), jnp.float32)
    return jnp.clip(raw, -4.0, 4.0)


def remove_mean(matrix, mean_row):
    along = jnp.dot(mean_row, matrix, precision=lax.Precision.HIGHEST) / jnp.sum(mean_row * mean_row)
    return matrix - mean_row[:, None] * along[None, :]


def key_basis(key):
    mean_row = shared_mean(key)
    raw = jnp.clip(jax.random.normal(jax.random.fold_in(key, 202), (D, HEADS * HDIM), jnp.float32), -6.0, 6.0)
    return remove_mean(raw, mean_row) / math.sqrt(D)


def draw_inputs(key, part):
    subkeys = jax.random.split(jax.random.fold_in(key, 11), 2)
    segments = LENGTH // SEG
    mean_row = shared_mean(key)
    common = jax.random.normal(subkeys[1], (BATCH, segments, 1, D), jnp.float32)
    noise_part = jax.random.normal(subkeys[0], (BATCH, segments, SEG, D), jnp.float32)
    mixed_rows = mean_row + 0.5 * common + noise_part
    return jnp.clip(mixed_rows.reshape(BATCH, LENGTH, D), -40.0, 40.0).astype(jnp.bfloat16)


def draw_w_query(key, part):
    mean_row = shared_mean(key)
    raw = jnp.clip(jax.random.normal(jax.random.fold_in(key, 303), (D, HEADS * HDIM), jnp.float32), -6.0, 6.0)
    offsets = jax.random.uniform(jax.random.fold_in(key, 404), (HEADS * HDIM,), jnp.float32, -5.0, -3.0)
    weight = 1.8 * remove_mean(raw, mean_row) / math.sqrt(D)
    weight = weight + mean_row[:, None] * offsets[None, :] / jnp.sum(mean_row * mean_row)
    limit = 12.0 / math.sqrt(D)
    return jnp.clip(weight, -limit, limit).astype(jnp.bfloat16)


def draw_w_key(key, part):
    weight = 0.58 * key_basis(key)
    limit = 4.0 / math.sqrt(D)
    return jnp.clip(weight, -limit, limit).astype(jnp.bfloat16)


def draw_w_value(key, part):
    basis = key_basis(key).reshape(D, HEADS, HDIM)
    mixer = jax.random.normal(jax.random.fold_in(key, 505), (HEADS, HDIM, HDIM), jnp.float32) / math.sqrt(HDIM)
    linked = jnp.einsum('chd,hde->che', basis, mixer, precision=lax.Precision.HIGHEST).reshape(D, HEADS * HDIM)
    mean_row = shared_mean(key)
    raw = jnp.clip(jax.random.normal(jax.random.fold_in(key, 606), (D, HEADS * HDIM), jnp.float32), -6.0, 6.0)
    weight = 0.9 * linked + 0.436 * remove_mean(raw, mean_row) / math.sqrt(D)
    limit = 6.0 / math.sqrt(D)
    return jnp.clip(weight, -limit, limit).astype(jnp.bfloat16)


def steps_of(stream_key, shape, cuts, low, largest):
    level = 1.0
    for axis_at, blocks in cuts:
        steps = jax.random.uniform(jax.random.fold_in(jax.random.fold_in(stream_key, 6), axis_at), (blocks,), jnp.float32, low / len(cuts), largest / len(cuts))
        level = level * jnp.repeat(jnp.exp(steps), shape[axis_at] // blocks).reshape((-1,) + (1,) * (len(shape) - 1 - axis_at))
    return level


def normal_values(rng, extent, width, reach, cuts=(), held_as=jnp.bfloat16):
    values = width * jax.random.normal(rng, extent, jnp.float32)
    if cuts:
        values = values * steps_of(rng, extent, cuts, -0.22, 0.18)
    return jnp.clip(values, -reach, reach).astype(held_as)


def setup_inputs(seed: int = 0) -> dict:
    key_of = jax.random.split(jax.random.key(seed), 7)
    return {
        "inputs": draw_inputs(jax.random.fold_in(key_of[6], 71), 0),
        "w_query": draw_w_query(jax.random.fold_in(key_of[6], 71), 0),
        "w_key": draw_w_key(jax.random.fold_in(key_of[6], 71), 0),
        "w_value": draw_w_value(jax.random.fold_in(key_of[6], 71), 0),
        "gate_bias": jnp.clip(2.5 * jax.random.uniform(key_of[4], (HEADS,), jnp.float32) ** steps_of(key_of[4], (HEADS,), ((0, 4),), -0.2, 0.2), 0.0, 2.5),
        "cotangent": normal_values(key_of[5], (BATCH, LENGTH, HEADS * HDIM), 1.0, 8.0, ((0, 2), (1, 32), (2, 4))),
    }


exact_mode = lax.Precision.HIGHEST

def product(form, left, right):
    return jnp.einsum(form, left.astype(jnp.float32), right.astype(jnp.float32))

def feature(values_in):
    return jnp.where(values_in > 0, values_in + 1.0, jnp.exp(jnp.minimum(values_in, 0.0)))

def feature_slope(values_in):
    return jnp.where(values_in > 0, 1.0, jnp.exp(jnp.minimum(values_in, 0.0)))

def write_memory(keys_own, values_own):
    phi_key = feature(keys_own.astype(jnp.float32))
    memory = jnp.einsum('shd,she->hde', phi_key, values_own.astype(jnp.float32), precision=exact_mode)
    return (memory, lax.optimization_barrier(jnp.sum(phi_key, axis=0)))

def write_grads(keys_own, values_own, grad_memory, grad_norm):
    key_float = keys_own.astype(jnp.float32)
    phi_key = feature(key_float)
    grad_phi = jnp.einsum('hde,she->shd', grad_memory, values_own.astype(jnp.float32), precision=exact_mode) + grad_norm[None]
    grad_value = jnp.einsum('shd,hde->she', phi_key, grad_memory, precision=exact_mode)
    return (grad_phi * feature_slope(key_float), grad_value)

def attend(queries, keys_own, values_own, keys_prev, values_prev, has_prev, memory, normaliser, gate_bias):
    seg_len, head_count, head_dim = queries.shape
    all_keys = jnp.concatenate([keys_prev, keys_own], 0)
    all_values = jnp.concatenate([values_prev, values_own], 0)
    score_scale = head_dim ** (-0.5)
    scores = product('shd,thd->hst', queries, all_keys) * score_scale
    row_ids = lax.broadcasted_iota(jnp.int32, (seg_len, 2 * seg_len), 0)
    col_ids = lax.broadcasted_iota(jnp.int32, (seg_len, 2 * seg_len), 1)
    allowed = (col_ids <= row_ids + seg_len) & ((col_ids >= seg_len) | has_prev)
    scores = jnp.where(allowed[None], scores, -1e+30)
    row_max = lax.optimization_barrier(jnp.max(scores, axis=2, keepdims=True))
    weights = jnp.exp(scores - row_max)
    softmax = weights / lax.optimization_barrier(jnp.sum(weights, axis=2, keepdims=True))
    soft_bf = softmax.astype(jnp.bfloat16)
    local_out = product('hst,thd->shd', soft_bf, all_values)
    phi_query = feature(queries.astype(jnp.float32))
    numerator = jnp.einsum('shd,hde->she', phi_query, memory, precision=exact_mode)
    denominator = jnp.einsum('shd,hd->sh', phi_query, normaliser, precision=exact_mode) + 1.0
    retrieved = numerator / denominator[:, :, None]
    mixing = jax.nn.sigmoid(gate_bias)[None, :, None]
    blended = mixing * retrieved + (1.0 - mixing) * local_out
    stored = (all_keys, all_values, softmax, soft_bf, phi_query, retrieved, denominator)
    return (blended.astype(jnp.bfloat16), stored)

def backprop(cotangent, queries, memory, normaliser, gate_bias, stored):
    all_keys, all_values, softmax, soft_bf, phi_query, retrieved, denominator = stored
    head_dim = queries.shape[2]
    mixing = jax.nn.sigmoid(gate_bias)[None, :, None]
    upstream = cotangent.astype(jnp.float32)
    grad_ret = mixing * upstream
    grad_local = ((1.0 - mixing) * upstream).astype(jnp.bfloat16)
    grad_soft = product('shd,thd->hst', grad_local, all_values)
    grad_values = product('hst,shd->thd', soft_bf, grad_local)
    row_dot = lax.optimization_barrier(jnp.sum(softmax * grad_soft, axis=2, keepdims=True))
    grad_scores = (softmax * (grad_soft - row_dot) * head_dim ** (-0.5)).astype(jnp.bfloat16)
    grad_query = product('hst,thd->shd', grad_scores, all_keys)
    grad_keys = product('hst,shd->thd', grad_scores, queries)
    grad_num = grad_ret / denominator[:, :, None]
    grad_den = -lax.optimization_barrier(jnp.sum(grad_ret * retrieved, axis=2)) / denominator
    grad_phi = jnp.einsum('she,hde->shd', grad_num, memory, precision=exact_mode) + grad_den[:, :, None] * normaliser[None]
    grad_memory = jnp.einsum('shd,she->hde', phi_query, grad_num, precision=exact_mode)
    grad_norm = jnp.einsum('shd,sh->hd', phi_query, grad_den, precision=exact_mode)
    grad_query = grad_query + grad_phi * feature_slope(queries.astype(jnp.float32))
    return (grad_query, grad_keys, grad_values, grad_memory, grad_norm)

def prefix_before(stacked):
    running = jnp.cumsum(stacked, axis=0)
    return jnp.concatenate([jnp.zeros_like(running[:1]), running[:-1]], 0)

def suffix_after(stacked):
    running = jnp.cumsum(stacked[::-1], axis=0)[::-1]
    return jnp.concatenate([running[1:], jnp.zeros_like(running[:1])], 0)

def one_sequence(tokens, w_query, w_key, w_value, gate_bias, cotangent):
    length = tokens.shape[0]
    head_count = gate_bias.shape[0]
    columns = w_query.shape[1]
    head_dim = columns // head_count
    blocks = length // SEG

    def project(weight):
        flat = jnp.dot(tokens, weight, preferred_element_type=jnp.float32).astype(jnp.bfloat16)
        return flat.reshape(blocks, SEG, head_count, head_dim)
    queries = project(w_query)
    keys_all = project(w_key)
    values_all = project(w_value)
    memories, norms_all = jax.vmap(write_memory)(keys_all, values_all)
    memory_prev = prefix_before(memories)
    norm_prev = prefix_before(norms_all)
    keys_prev = jnp.concatenate([jnp.zeros_like(keys_all[:1]), keys_all[:-1]], 0)
    values_prev = jnp.concatenate([jnp.zeros_like(values_all[:1]), values_all[:-1]], 0)
    has_prev = jnp.arange(blocks) > 0
    cot_blocks = cotangent.reshape(blocks, SEG, head_count, head_dim)

    def segment(pieces):
        query_block, key_block, value_block, key_before, value_before, flag_prev, memory_in, normaliser_in, cot_block = pieces
        out_block, stored = attend(query_block, key_block, value_block, key_before, value_before, flag_prev, memory_in, normaliser_in, gate_bias)
        grads = backprop(cot_block, query_block, memory_in, normaliser_in, gate_bias, stored)
        return (out_block,) + grads
    outputs, grad_query, grad_keys, grad_values, grad_memory, grad_norm = lax.map(segment, (queries, keys_all, values_all, keys_prev, values_prev, has_prev, memory_prev, norm_prev, cot_blocks))
    grad_mem_seg = suffix_after(grad_memory)
    grad_norm_seg = suffix_after(grad_norm)
    write_key, write_value = jax.vmap(write_grads)(keys_all, values_all, grad_mem_seg, grad_norm_seg)
    halo_keys = grad_keys[:, :SEG].astype(jnp.bfloat16)
    halo_values = grad_values[:, :SEG].astype(jnp.bfloat16)
    next_keys = jnp.concatenate([halo_keys[1:], jnp.zeros_like(halo_keys[:1])], 0)
    next_values = jnp.concatenate([halo_values[1:], jnp.zeros_like(halo_values[:1])], 0)
    grad_key = (grad_keys[:, SEG:] + next_keys.astype(jnp.float32) + write_key).astype(jnp.bfloat16)
    grad_value = (grad_values[:, SEG:] + next_values.astype(jnp.float32) + write_value).astype(jnp.bfloat16)
    grad_all = jnp.concatenate([grad_query.astype(jnp.bfloat16).reshape(length, columns), grad_key.reshape(length, columns), grad_value.reshape(length, columns)], 1)
    weight_term = jnp.dot(tokens.T, grad_all, preferred_element_type=jnp.float32)
    return (outputs.reshape(length, columns), weight_term)

def reference(inputs, w_query, w_key, w_value, gate_bias, cotangent):
    results = []
    grad_total = None
    for batch_index in range(BATCH):
        output_one, weight_term = one_sequence(inputs[batch_index], w_query, w_key, w_value, gate_bias, cotangent[batch_index])
        results.append(output_one)
        grad_total = weight_term if grad_total is None else grad_total + weight_term
    grad_scale = 1.0 / math.sqrt(BATCH * LENGTH)
    grad_weights = (grad_total * grad_scale).reshape(D, 3, HEADS * HDIM)
    return (jnp.stack(results, 0), grad_weights)
```

```python
import functools
import math

import jax
import jax.numpy as jnp
from jax import lax
from jax.experimental import pallas as pl
from jax.experimental.pallas import tpu as pltpu
from jax.sharding import Mesh
from jax.sharding import PartitionSpec as P

SEQ = ("y", "z")
SEQ_DP = ("y", "z", "dp")
MESH = pl.DeviceIdType.MESH


def ring_chains(n):
    chains, first = [], 0
    for sub in (0, 1):
        for way in (1, -1):
            length = n // 2 if (way > 0) == (sub == 0) else n - 1 - n // 2
            chains.append((sub, way, length, first))
            first += length
    return chains


class RingSum:
    def __init__(self, axis, mine, send, recv, send_sem, recv_sem):
        self.axis, self.mine = axis, mine
        self.n, self.position = lax.axis_size(axis), lax.axis_index(axis)
        self.send, self.recv, self.send_sem, self.recv_sem = send, recv, send_sem, recv_sem
        self.chains = ring_chains(self.n)

    def copy(self, slot, way):
        return pltpu.make_async_remote_copy(
            src_ref=self.send.at[slot],
            dst_ref=self.recv.at[slot],
            send_sem=self.send_sem.at[slot],
            recv_sem=self.recv_sem.at[slot],
            device_id={self.axis: lax.rem(self.position + way + self.n, self.n)},
            device_id_type=MESH,
        )

    def step(self, t, ahead=None):
        for sub, way, length, first in self.chains:
            if t >= length:
                continue
            if ahead is not None and (way * (length - t)) % self.n != ahead % self.n:
                continue
            target = lax.rem(self.position + way * (length - t) + self.n, self.n)
            value = self.mine(target, sub)
            if t:
                self.copy(first + t - 1, way).wait_recv()
                value = value + self.recv[first + t - 1].astype(jnp.float32)
            self.send[first + t] = value.astype(jnp.bfloat16)
            self.copy(first + t, way).start()

    def total(self, sub):
        value = self.mine(self.position, sub)
        for chain_sub, way, length, first in self.chains:
            if chain_sub == sub and length:
                self.copy(first + length - 1, way).wait_recv()
                value = value + self.recv[first + length - 1].astype(jnp.float32)
        return value

    def drain(self):
        for _, way, length, first in self.chains:
            for t in range(length):
                self.copy(first + t, way).wait_send()


def weight_kernel(
    scale, x_ref, g_ref, out_ref, x_all, g_all, dw, a_sum, b_sum, fin, swap,
    a1_send, a1_recv, b1_send, b1_recv, a2_send, a2_recv, b2_send, b2_recv,
    local_sem, pair_sem, z1_sem, y1_sem, y2_sem, z2_sem,
):
    ny, nz = lax.axis_size("y"), lax.axis_size("z")
    y, dp = lax.axis_index("y"), lax.axis_index("dp")
    other = {"dp": 1 - dp}
    tokens = x_ref.shape[0]
    half = g_ref.shape[2] // 2
    wide = dw.shape[1]
    block = wide // nz
    rows = block // 2

    barrier = pltpu.get_barrier_semaphore()
    pl.semaphore_signal(barrier, inc=1, device_id=other, device_id_type=MESH)
    for axis, n in (("y", ny), ("z", nz)):
        for way in (1, -1):
            seat = lax.rem(lax.axis_index(axis) + way + n, n)
            pl.semaphore_signal(barrier, inc=1, device_id={axis: seat}, device_id_type=MESH)
    x_in = pltpu.make_async_copy(x_ref, x_all.at[pl.ds(0, tokens)], local_sem.at[0])
    g_in = pltpu.make_async_copy(g_ref.at[dp], g_all.at[pl.ds(0, tokens)], local_sem.at[1])
    x_in.start()
    g_in.start()
    pl.semaphore_wait(barrier, 5)

    def pair_copy(src, dst, slot):
        return pltpu.make_async_remote_copy(
            src_ref=src, dst_ref=dst, send_sem=pair_sem.at[0, slot], recv_sem=pair_sem.at[1, slot],
            device_id=other, device_id_type=MESH,
        )

    g_out = pair_copy(g_ref.at[1 - dp], g_all.at[pl.ds(tokens, tokens)], 0)
    x_out = pair_copy(x_ref, x_all.at[pl.ds(tokens, tokens)], 1)
    g_out.start()
    x_out.start()
    x_in.wait()
    g_in.wait()
    g_out.wait_recv()
    x_out.wait_recv()

    tile = min(wide, 256)

    def products(target):
        def body(i, carry):
            start = pl.multiple_of(target * wide + i * tile, 128)
            dw[target, pl.ds(pl.multiple_of(i * tile, 8), tile), :] = lax.dot_general(
                x_all[:, pl.ds(start, tile)], g_all[...], (((0,), (0,)), ((), ())),
                preferred_element_type=jnp.float32,
            )
            return carry
        lax.fori_loop(0, wide // tile, body, 0)

    def a1_mine(target, sub):
        return dw[:, pl.ds(pl.multiple_of(target * block + sub * rows, 8), rows), :half]

    def b1_mine(target, sub):
        return dw[target, sub * (wide // 2):(sub + 1) * (wide // 2), half:]

    def b2_mine(target, sub):
        return b_sum[pl.ds(pl.multiple_of(target * block + sub * rows, 8), rows), :]

    a1 = RingSum("z", a1_mine, a1_send, a1_recv, z1_sem.at[0], z1_sem.at[1])
    b1 = RingSum("y", b1_mine, b1_send, b1_recv, y1_sem.at[0], y1_sem.at[1])
    a2 = RingSum("y", lambda k, sub: a_sum[sub, k], a2_send, a2_recv, y2_sem.at[0], y2_sem.at[1])
    b2 = RingSum("z", b2_mine, b2_send, b2_recv, z2_sem.at[0], z2_sem.at[1])

    for step in range(ny):
        ahead = ny // 2 - step
        products(lax.rem(y + ahead + ny, ny))
        b1.step(0, ahead)
    a1.step(0)
    a1.step(1)
    b1.step(1)
    for t in range(2, nz // 2):
        a1.step(t)
    for sub in (0, 1):
        b_sum[sub * (wide // 2):(sub + 1) * (wide // 2), :] = b1.total(sub)
    b2.step(0)
    for sub in (0, 1):
        a_sum[sub] = a1.total(sub)
    for t in range(max(ny, nz) // 2):
        a2.step(t)
        b2.step(t + 1)
    for sub in (0, 1):
        fin[sub, :, :half] = a2.total(sub) * scale
        fin[sub, :, half:] = b2.total(sub) * scale
    swap_out = pair_copy(fin.at[1 - dp], swap, 2)
    swap_out.start()
    out_ref[dp] = fin[dp]
    for ring in (a1, b1, a2, b2):
        ring.drain()
    g_out.wait_send()
    x_out.wait_send()
    swap_out.wait()
    out_ref[1 - dp] = swap[...]


def weight_sum(x, g, scale):
    tokens, depth = x.shape
    cols = g.shape[2]
    ny, nz = lax.axis_size("y"), lax.axis_size("z")
    wide = depth // ny
    rows = wide // nz // 2
    half = cols // 2
    zs, ys = 2 * (nz - 1), 2 * (ny - 1)
    wire = lambda *shape: pltpu.VMEM(shape, jnp.bfloat16)
    real = lambda *shape: pltpu.VMEM(shape, jnp.float32)
    dma = lambda *shape: pltpu.SemaphoreType.DMA(shape)
    a1, b1, last = (zs, ny, rows, half), (ys, wide // 2, half), (rows, half)
    return pl.pallas_call(
        functools.partial(weight_kernel, scale),
        out_shape=jax.ShapeDtypeStruct((2, rows, cols), jnp.float32),
        in_specs=[pl.BlockSpec(memory_space=pl.ANY)] * 2,
        out_specs=pl.BlockSpec(memory_space=pltpu.VMEM),
        scratch_shapes=[
            wire(2 * tokens, depth), wire(2 * tokens, cols), real(ny, wide, cols),
            real(2, ny, rows, half), real(wide, half), real(2, rows, cols), real(rows, cols),
            wire(*a1), wire(*a1), wire(*b1), wire(*b1),
            wire(ys, *last), wire(ys, *last), wire(zs, *last), wire(zs, *last),
            dma(2), dma(2, 3), dma(2, zs), dma(2, ys), dma(2, ys), dma(2, zs),
        ],
        compiler_params=pltpu.CompilerParams(
            collective_id=1, has_side_effects=True, vmem_limit_bytes=60 * 1024 * 1024
        ),
    )(x, g)


def filled_with(x, identity):
    return jax.tree.map(
        lambda a, e: jnp.broadcast_to(jnp.asarray(e, a.dtype), a.shape), x, identity
    )


def prefix_by_axis(x, axes, combine, identity, reverse):
    before = start = filled_with(x, identity)
    subtotal = x
    for axis in reversed(axes):
        devices, position = (lax.axis_size(axis), lax.axis_index(axis))
        pieces = jax.tree.map(lambda part: lax.all_gather(part, axis), subtotal)
        inside, subtotal = (start, start)
        for k in reversed(range(devices)) if reverse else range(devices):
            passed = k > position if reverse else k < position
            subtotal = combine(subtotal, jax.tree.map(lambda part: part[k], pieces))
            inside = jax.tree.map(lambda new, old: jnp.where(passed, new, old), subtotal, inside)
        before = combine(inside, before)
    return before


def passed_along(x, axis, by):
    devices = lax.axis_size(axis)
    pairs = [(i, i + by) for i in range(devices) if 0 <= i + by < devices]
    return lax.ppermute(x, axis, pairs)


def product(form, left, right):
    return jnp.einsum(form, left, right, preferred_element_type=jnp.float32)


def feature(values_in):
    return jnp.where(values_in > 0, values_in + 1.0, jnp.exp(jnp.minimum(values_in, 0.0)))


def feature_slope(values_in):
    return jnp.where(values_in > 0, 1.0, jnp.exp(jnp.minimum(values_in, 0.0)))


def add_pair(earlier, latter):
    return (earlier[0] + latter[0], earlier[1] + latter[1])


def write_memory(keys_own, values_own):
    phi_key = feature(keys_own.astype(jnp.float32))
    memory = jnp.einsum("shd,she->hde", phi_key, values_own.astype(jnp.float32))
    return (memory, jnp.sum(phi_key, axis=0))


def write_grads(keys_own, values_own, grad_memory, grad_norm):
    key_float = keys_own.astype(jnp.float32)
    phi_key = feature(key_float)
    grad_phi = (
        jnp.einsum("hde,she->shd", grad_memory, values_own.astype(jnp.float32)) + grad_norm[None]
    )
    grad_value = jnp.einsum("shd,hde->she", phi_key, grad_memory)
    return (grad_phi * feature_slope(key_float), grad_value)


def attend(
    queries, keys_own, values_own, keys_prev, values_prev, has_prev, memory, normaliser, gate_bias
):
    seg_len, head_count, head_dim = queries.shape
    all_keys = jnp.concatenate([keys_prev, keys_own], 0)
    all_values = jnp.concatenate([values_prev, values_own], 0)
    score_scale = head_dim ** (-0.5)
    scores = product("shd,thd->hst", queries, all_keys) * score_scale
    row_ids = lax.broadcasted_iota(jnp.int32, (seg_len, 2 * seg_len), 0)
    col_ids = lax.broadcasted_iota(jnp.int32, (seg_len, 2 * seg_len), 1)
    allowed = (col_ids <= row_ids + seg_len) & ((col_ids >= seg_len) | has_prev)
    scores = jnp.where(allowed[None], scores, -1e30)
    row_max = jnp.max(scores, axis=2, keepdims=True)
    weights = jnp.exp(scores - row_max)
    softmax = weights / jnp.sum(weights, axis=2, keepdims=True)
    soft_bf = softmax.astype(jnp.bfloat16)
    local_out = product("hst,thd->shd", soft_bf, all_values)
    phi_query = feature(queries.astype(jnp.float32))
    numerator = jnp.einsum("shd,hde->she", phi_query, memory)
    denominator = jnp.einsum("shd,hd->sh", phi_query, normaliser) + 1.0
    retrieved = numerator / denominator[:, :, None]
    mixing = jax.nn.sigmoid(gate_bias)[None, :, None]
    blended = mixing * retrieved + (1.0 - mixing) * local_out
    stored = (all_keys, all_values, softmax, soft_bf, phi_query, retrieved, denominator)
    return (blended.astype(jnp.bfloat16), stored)


def backprop(cotangent, queries, memory, normaliser, gate_bias, stored):
    all_keys, all_values, softmax, soft_bf, phi_query, retrieved, denominator = stored
    head_dim = queries.shape[2]
    mixing = jax.nn.sigmoid(gate_bias)[None, :, None]
    upstream = cotangent.astype(jnp.float32)
    grad_ret = mixing * upstream
    grad_local = ((1.0 - mixing) * upstream).astype(jnp.bfloat16)
    grad_soft = product("shd,thd->hst", grad_local, all_values)
    grad_values = product("hst,shd->thd", soft_bf, grad_local)
    row_dot = jnp.sum(softmax * grad_soft, axis=2, keepdims=True)
    grad_scores = (softmax * (grad_soft - row_dot) * head_dim ** (-0.5)).astype(jnp.bfloat16)
    grad_query = product("hst,thd->shd", grad_scores, all_keys)
    grad_keys = product("hst,shd->thd", grad_scores, queries)
    grad_num = grad_ret / denominator[:, :, None]
    grad_den = -jnp.sum(grad_ret * retrieved, axis=2) / denominator
    grad_phi = (
        jnp.einsum("she,hde->shd", grad_num, memory) + grad_den[:, :, None] * normaliser[None]
    )
    grad_memory = jnp.einsum("shd,she->hde", phi_query, grad_num)
    grad_norm = jnp.einsum("shd,sh->hd", phi_query, grad_den)
    grad_query = grad_query + grad_phi * feature_slope(queries.astype(jnp.float32))
    return (grad_query, grad_keys, grad_values, grad_memory, grad_norm)


def local(inputs, w_query, w_key, w_value, gate_bias, cotangent):
    tokens = inputs[0]
    seg_len, model_dim = tokens.shape
    head_count = gate_bias.shape[0]
    columns = w_query.shape[1]
    head_dim = columns // head_count

    def project(weight):
        return jnp.dot(tokens, weight, preferred_element_type=jnp.float32).astype(jnp.bfloat16)

    query_flat = project(w_query)
    key_flat = project(w_key)
    value_flat = project(w_value)
    queries = query_flat.reshape(seg_len, head_count, head_dim)
    keys_own = key_flat.reshape(seg_len, head_count, head_dim)
    values_own = value_flat.reshape(seg_len, head_count, head_dim)
    memory_own, norm_own = write_memory(keys_own, values_own)
    zero_pair = (jnp.zeros_like(memory_own), jnp.zeros_like(norm_own))
    memory_prev, norm_prev = prefix_by_axis((memory_own, norm_own), SEQ, add_pair, zero_pair, False)
    neighbour = passed_along(jnp.stack([key_flat, value_flat]), SEQ, 1)
    keys_prev = neighbour[0].reshape(seg_len, head_count, head_dim)
    values_prev = neighbour[1].reshape(seg_len, head_count, head_dim)
    has_prev = lax.axis_index(SEQ) > 0
    blended, stored = attend(
        queries,
        keys_own,
        values_own,
        keys_prev,
        values_prev,
        has_prev,
        memory_prev,
        norm_prev,
        gate_bias,
    )
    cot_local = cotangent[0].reshape(seg_len, head_count, head_dim)
    grad_query, grad_keys, grad_values, grad_memory, grad_norm = backprop(
        cot_local, queries, memory_prev, norm_prev, gate_bias, stored
    )
    grad_mem_seg, grad_norm_seg = prefix_by_axis(
        (grad_memory, grad_norm), SEQ, add_pair, zero_pair, True
    )
    outgoing = jnp.stack([grad_keys[:seg_len], grad_values[:seg_len]]).astype(jnp.bfloat16)
    incoming = passed_along(outgoing, SEQ, -1).astype(jnp.float32)
    write_key, write_value = write_grads(keys_own, values_own, grad_mem_seg, grad_norm_seg)
    grad_key = (grad_keys[seg_len:] + incoming[0] + write_key).astype(jnp.bfloat16)
    grad_value = (grad_values[seg_len:] + incoming[1] + write_value).astype(jnp.bfloat16)
    grad_all = jnp.concatenate(
        [grad_query.astype(jnp.bfloat16), grad_key, grad_value], 2
    ).transpose(1, 0, 2)
    scale = 1.0 / math.sqrt(lax.axis_size(SEQ) * lax.axis_size("dp") * seg_len)
    summed = weight_sum(tokens, grad_all, scale)
    rows = summed.shape[1]
    grad_weights = summed.reshape(2, rows, 3, head_dim).transpose(1, 2, 0, 3).reshape(rows, 3, columns)
    return (blended.reshape(1, seg_len, columns), grad_weights)


def solution(mesh):
    finer = Mesh(
        mesh.devices.reshape(4, 8, mesh.shape["dp"], mesh.shape["head"]),
        ("y", "z", "dp", "head"),
    )
    placed = (
        P("dp", SEQ, None),
        P(None, "head"),
        P(None, "head"),
        P(None, "head"),
        P("head"),
        P("dp", SEQ, "head"),
    )
    return jax.shard_map(
        local,
        mesh=finer,
        in_specs=placed,
        out_specs=(P("dp", SEQ, "head"), P(SEQ_DP, None, "head")),
        check_vma=False,
    )
```

```python
import functools
import math

import jax
import jax.numpy as jnp
from jax import lax
from jax.experimental import pallas as pl
from jax.experimental.pallas import tpu as pltpu
from jax.sharding import Mesh
from jax.sharding import PartitionSpec as P

SEQ = ("y", "z")
SEQ_DP = ("y", "z", "dp")
MESH = pl.DeviceIdType.MESH
MASKED = -1e30


def feature(u):
    return jnp.where(u > 0, u + 1.0, jnp.exp(jnp.minimum(u, 0.0)))


def feature_slope(u):
    return jnp.where(u > 0, 1.0, jnp.exp(jnp.minimum(u, 0.0)))


def contract(a, b, over_a, over_b):
    return lax.dot_general(
        a, b, (((over_a,), (over_b,)), ((), ())), preferred_element_type=jnp.float32
    )


def dot_nn(a, b):
    return contract(a, b, 1, 0)


def dot_nt(a, b):
    return contract(a, b, 1, 1)


def dot_tn(a, b):
    return contract(a, b, 0, 0)


def ring_chains(n):
    chains, first = [], 0
    for sub in (0, 1):
        for way in (1, -1):
            length = n // 2 if (way > 0) == (sub == 0) else n - 1 - n // 2
            chains.append((sub, way, length, first))
            first += length
    return chains


class RingSum:
    def __init__(self, axis, mine, send, recv, send_sem, recv_sem):
        self.axis, self.mine = axis, mine
        self.n, self.position = lax.axis_size(axis), lax.axis_index(axis)
        self.send, self.recv, self.send_sem, self.recv_sem = send, recv, send_sem, recv_sem
        self.chains = ring_chains(self.n)

    def copy(self, slot, way):
        return pltpu.make_async_remote_copy(
            src_ref=self.send.at[slot],
            dst_ref=self.recv.at[slot],
            send_sem=self.send_sem.at[slot],
            recv_sem=self.recv_sem.at[slot],
            device_id={self.axis: lax.rem(self.position + way + self.n, self.n)},
            device_id_type=MESH,
        )

    def step(self, t, ahead=None):
        for sub, way, length, first in self.chains:
            if t >= length:
                continue
            if ahead is not None and (way * (length - t)) % self.n != ahead % self.n:
                continue
            target = lax.rem(self.position + way * (length - t) + self.n, self.n)
            value = self.mine(target, sub)
            if t:
                self.copy(first + t - 1, way).wait_recv()
                value = value + self.recv[first + t - 1].astype(jnp.float32)
            self.send[first + t] = value.astype(jnp.bfloat16)
            self.copy(first + t, way).start()

    def total(self, sub):
        value = self.mine(self.position, sub)
        for chain_sub, way, length, first in self.chains:
            if chain_sub == sub and length:
                self.copy(first + length - 1, way).wait_recv()
                value = value + self.recv[first + length - 1].astype(jnp.float32)
        return value

    def drain(self):
        for _, way, length, first in self.chains:
            for t in range(length):
                self.copy(first + t, way).wait_send()


class Spread:
    def __init__(self, axis, got, sem):
        self.axis, self.got, self.sem = axis, got, sem
        self.n, self.position = lax.axis_size(axis), lax.axis_index(axis)

    def copy(self, src, j):
        return pltpu.make_async_remote_copy(
            src_ref=src,
            dst_ref=self.got.at[j],
            send_sem=self.sem.at[0, j],
            recv_sem=self.sem.at[1, j],
            device_id={self.axis: lax.rem(self.position + j, self.n)},
            device_id_type=MESH,
        )

    def start(self, src):
        self.src = src
        for j in range(1, self.n):
            self.copy(src, j).start()

    def sums(self, own, reverse):
        passed, total = jnp.zeros_like(own), own
        for j in range(1, self.n):
            self.copy(self.src, j).wait_recv()
            value = self.got[j]
            earlier = self.position < j if reverse else self.position >= j
            passed = passed + value * jnp.where(earlier, 1.0, 0.0)
            total = total + value
        return passed, total

    def drain(self):
        for j in range(1, self.n):
            self.copy(self.src, j).wait_send()


class VectorScan:
    def __init__(self, reverse, own, z_got, y_own, y_got, z_sem, y_sem):
        self.reverse, self.own, self.y_own = reverse, own, y_own
        self.z, self.y = Spread("z", z_got, z_sem), Spread("y", y_got, y_sem)

    def start(self):
        self.z.start(self.own)

    def across_rows(self):
        self.inside, total = self.z.sums(self.own[...], self.reverse)
        self.y_own[...] = total
        self.y.start(self.y_own)

    def result(self):
        passed, _ = self.y.sums(self.y_own[...], self.reverse)
        return passed + self.inside

    def drain(self):
        self.z.drain()
        self.y.drain()


class MemoryScan:
    def __init__(self, reverse, parts, got, inside, y_own, y_got, back, result, z_sem, y_sem, back_sem):
        self.reverse, self.parts, self.got, self.inside, self.y_own = reverse, parts, got, inside, y_own
        self.back, self.full, self.z_sem, self.back_sem = back, result, z_sem, back_sem
        self.n, self.position = lax.axis_size("z"), lax.axis_index("z")
        self.y = Spread("y", y_got, y_sem)

    def out_copy(self, j):
        target = lax.rem(self.position + j, self.n)
        return pltpu.make_async_remote_copy(
            src_ref=self.parts.at[target],
            dst_ref=self.got.at[j],
            send_sem=self.z_sem.at[0, j],
            recv_sem=self.z_sem.at[1, j],
            device_id={"z": target},
            device_id_type=MESH,
        )

    def back_copy(self, j):
        target = lax.rem(self.position + j, self.n)
        return pltpu.make_async_remote_copy(
            src_ref=self.back.at[target],
            dst_ref=self.full.at[self.position],
            send_sem=self.back_sem.at[0, j],
            recv_sem=self.back_sem.at[1, j],
            device_id={"z": target},
            device_id_type=MESH,
        )

    def start(self):
        for j in range(1, self.n):
            self.out_copy(j).start()

    def across_rows(self):
        for j in range(1, self.n):
            self.out_copy(j).wait_recv()
        self.got[0] = self.parts[self.position]
        run = jnp.zeros(self.y_own.shape, jnp.float32)
        for k in reversed(range(self.n)) if self.reverse else range(self.n):
            self.inside[k] = run
            run = run + self.got[lax.rem(self.position - k + self.n, self.n)].astype(jnp.float32)
        self.y_own[...] = run
        self.y.start(self.y_own)

    def give_back(self):
        passed, _ = self.y.sums(self.y_own[...], self.reverse)
        for k in range(self.n):
            self.back[k] = (self.inside[k] + passed).astype(jnp.bfloat16)
        for j in range(1, self.n):
            self.back_copy(j).start()
        self.full[self.position] = self.back[self.position]

    def finish(self):
        for j in range(1, self.n):
            self.back_copy(j).wait_recv()

    def head(self, h, heads):
        parts = self.n // heads
        block = self.full[pl.ds(h * parts, parts)]
        return block.reshape(parts * block.shape[1], block.shape[2])

    def drain(self):
        self.y.drain()
        for j in range(1, self.n):
            self.out_copy(j).wait_send()
            self.back_copy(j).wait_send()


def layer_kernel(
    scale, x_ref, wq_ref, wk_ref, wv_ref, gate_ref, cot_ref, blended_ref, out_ref,
    x_all, w_all, cot, kvq, prev, halo_out, halo_in, own_grads, dq_att, local_out,
    scores, soft_grads, grad_local, grad_num, den, grads, g_all,
    n1_own, n1_got, n1_yown, n1_ygot, n2_own, n2_got, n2_yown, n2_ygot, norms,
    m1_parts, m1_got, m1_inside, m1_yown, m1_ygot, m1_back, m1_full,
    m2_parts, m2_got, m2_inside, m2_yown, m2_ygot, m2_back, m2_full,
    dw, a_sum, b_sum, fin, swap,
    a1_send, a1_recv, b1_send, b1_recv, a2_send, a2_recv, b2_send, b2_recv,
    local_sem, halo_sem, pair_sem, nz_sem, ny_sem, mz_sem, my_sem, mb_sem, z1_sem, y1_sem, y2_sem, z2_sem,
):
    ny, nz = lax.axis_size("y"), lax.axis_size("z")
    y, z, dp = lax.axis_index("y"), lax.axis_index("z"), lax.axis_index("dp")
    other = {"dp": 1 - dp}
    tokens = x_ref.shape[0]
    heads, dim = kvq.shape[0] // 3, kvq.shape[2]
    half = grads.shape[2] // 2
    wide = dw.shape[1]
    block = wide // nz
    rows = block // 2
    up, down = z == nz - 1, z == 0
    after = {
        "y": lax.rem(y + jnp.where(up, 1, 0), ny), "z": lax.rem(z + 1, nz),
    }
    ahead_of = {
        "y": lax.rem(y - jnp.where(down, 1, 0) + ny, ny), "z": lax.rem(z - 1 + nz, nz),
    }
    score_scale = dim ** (-0.5)

    barrier = pltpu.get_barrier_semaphore()
    partners = [other, after, ahead_of]
    partners += [{"z": lax.rem(z + j, nz)} for j in range(1, nz)]
    partners += [{"y": lax.rem(y + j, ny)} for j in range(1, ny)]
    for device in partners:
        pl.semaphore_signal(barrier, inc=1, device_id=device, device_id_type=MESH)

    x_in = pltpu.make_async_copy(x_ref, x_all.at[pl.ds(0, tokens)], local_sem.at[0])
    cot_in = pltpu.make_async_copy(cot_ref, cot, local_sem.at[1])
    w_in = [
        pltpu.make_async_copy(w.at[:, pl.ds(h * dim, dim)], w_all.at[at * heads + h], local_sem.at[2 + at * heads + h])
        for at, w in enumerate((wk_ref, wv_ref, wq_ref)) for h in range(heads)
    ]
    x_in.start()
    for copy in w_in:
        copy.start()
    cot_in.start()

    def project(at):
        for h in range(heads):
            w_in[at * heads + h].wait()
        def body(h, carry):
            c = at * heads + h
            kvq[c] = dot_nn(x_all[pl.ds(0, tokens), :], w_all[c]).astype(jnp.bfloat16)
            return carry
        lax.fori_loop(0, heads, body, 0)

    def halo_copy(src, dst, slot, device):
        return pltpu.make_async_remote_copy(
            src_ref=src.at[pl.ds((slot % 2) * heads, heads)], dst_ref=dst.at[pl.ds((slot % 2) * heads, heads)],
            send_sem=halo_sem.at[0, slot], recv_sem=halo_sem.at[1, slot],
            device_id=device, device_id_type=MESH,
        )

    def pair_copy(src, dst, slot):
        return pltpu.make_async_remote_copy(
            src_ref=src, dst_ref=dst, send_sem=pair_sem.at[0, slot], recv_sem=pair_sem.at[1, slot],
            device_id=other, device_id_type=MESH,
        )

    def each_head(body):
        def step(h, carry):
            body(h)
            return carry
        lax.fori_loop(0, heads, step, 0)

    def columns(h):
        return pl.ds(pl.multiple_of(h * dim, dim), dim)

    norm_scan = VectorScan(False, n1_own, n1_got, n1_yown, n1_ygot, nz_sem.at[0], ny_sem.at[0])
    grad_norm_scan = VectorScan(True, n2_own, n2_got, n2_yown, n2_ygot, nz_sem.at[1], ny_sem.at[1])
    memory_scan = MemoryScan(
        False, m1_parts, m1_got, m1_inside, m1_yown, m1_ygot, m1_back, m1_full,
        mz_sem.at[0], my_sem.at[0], mb_sem.at[0],
    )
    grad_memory_scan = MemoryScan(
        True, m2_parts, m2_got, m2_inside, m2_yown, m2_ygot, m2_back, m2_full,
        mz_sem.at[1], my_sem.at[1], mb_sem.at[1],
    )
    parts = nz // heads

    def put_parts(target, h, value):
        target[pl.ds(h * parts, parts)] = value.astype(jnp.bfloat16).reshape(parts, dim // parts, dim)

    x_in.wait()
    project(0)

    def key_sums(h):
        n1_own[h] = jnp.sum(feature(kvq[h].astype(jnp.float32)), axis=0, keepdims=True)

    each_head(key_sums)
    pl.semaphore_wait(barrier, len(partners))
    norm_scan.start()
    halo_keys = halo_copy(kvq, prev, 0, after)
    halo_keys.start()
    project(1)

    def write(h):
        phi = feature(kvq[h].astype(jnp.float32)).astype(jnp.bfloat16)
        put_parts(m1_parts, h, dot_tn(phi, kvq[heads + h]))

    each_head(write)
    memory_scan.start()
    halo_values = halo_copy(kvq, prev, 1, after)
    halo_values.start()
    x_out = pair_copy(x_all.at[pl.ds(0, tokens)], x_all.at[pl.ds(tokens, tokens)], 0)
    x_out.start()
    project(2)
    cot_in.wait()
    norm_scan.across_rows()

    def own_part(h):
        query = kvq[2 * heads + h]
        mixing = 1.0 / (1.0 + jnp.exp(-jnp.full((1, dim), gate_ref[h], jnp.float32)))
        upstream = cot[:, columns(h)].astype(jnp.float32)
        local = ((1.0 - mixing) * upstream).astype(jnp.bfloat16)
        grad_local[h] = local
        row = lax.broadcasted_iota(jnp.int32, (tokens, tokens), 0)
        col = lax.broadcasted_iota(jnp.int32, (tokens, tokens), 1)
        scores[h] = jnp.where(col <= row, dot_nt(query, kvq[h]) * score_scale, MASKED)
        soft_grads[h] = dot_nt(local, kvq[heads + h])

    each_head(own_part)
    norms[...] = norm_scan.result()

    def memory_gradient(h):
        mixing = 1.0 / (1.0 + jnp.exp(-jnp.full((1, dim), gate_ref[h], jnp.float32)))
        phi = feature(kvq[2 * heads + h].astype(jnp.float32))
        divisor = jnp.sum(phi * norms[h], axis=1, keepdims=True) + 1.0
        den[h] = divisor
        grad_ret = mixing * cot[:, columns(h)].astype(jnp.float32)
        number = (grad_ret / divisor).astype(jnp.bfloat16)
        grad_num[h] = number
        put_parts(m2_parts, h, dot_tn(phi.astype(jnp.bfloat16), number))

    each_head(memory_gradient)
    grad_memory_scan.start()
    memory_scan.across_rows()

    bias = jnp.where(y * nz + z > 0, 0.0, MASKED)
    halo_keys.wait_recv()
    halo_values.wait_recv()
    memory_scan.give_back()

    def attend(h):
        query, key, value = kvq[2 * heads + h], kvq[h], kvq[heads + h]
        key_prev, value_prev, local = prev[h], prev[heads + h], grad_local[h]
        s_own = scores[h]
        s_prev = dot_nt(query, key_prev) * score_scale + bias
        top = jnp.maximum(jnp.max(s_own, axis=1, keepdims=True), jnp.max(s_prev, axis=1, keepdims=True))
        e_own, e_prev = jnp.exp(s_own - top), jnp.exp(s_prev - top)
        inverse = 1.0 / (jnp.sum(e_own, axis=1, keepdims=True) + jnp.sum(e_prev, axis=1, keepdims=True))
        p_own, p_prev = e_own * inverse, e_prev * inverse
        b_own, b_prev = p_own.astype(jnp.bfloat16), p_prev.astype(jnp.bfloat16)
        local_out[h] = dot_nn(b_own, value) + dot_nn(b_prev, value_prev)
        g_own, g_prev = soft_grads[h], dot_nt(local, value_prev)
        row_dot = jnp.sum(p_own * g_own, axis=1, keepdims=True) + jnp.sum(p_prev * g_prev, axis=1, keepdims=True)
        d_own = (p_own * (g_own - row_dot) * score_scale).astype(jnp.bfloat16)
        d_prev = (p_prev * (g_prev - row_dot) * score_scale).astype(jnp.bfloat16)
        halo_out[h] = dot_tn(d_prev, query).astype(jnp.bfloat16)
        halo_out[heads + h] = dot_tn(b_prev, local).astype(jnp.bfloat16)
        own_grads[h] = dot_tn(d_own, query)
        own_grads[heads + h] = dot_tn(b_own, local)
        dq_att[h] = dot_nn(d_own, key) + dot_nn(d_prev, key_prev)

    each_head(attend)
    back_keys, back_values = (halo_copy(halo_out, halo_in, slot, ahead_of) for slot in (2, 3))
    back_keys.start()
    back_values.start()
    grad_memory_scan.across_rows()
    memory_scan.finish()

    def retrieve(h):
        mixing = 1.0 / (1.0 + jnp.exp(-jnp.full((1, dim), gate_ref[h], jnp.float32)))
        query = kvq[2 * heads + h].astype(jnp.float32)
        phi = feature(query)
        memory = memory_scan.head(h, heads)
        retrieved = dot_nn(phi.astype(jnp.bfloat16), memory) / den[h]
        blended_ref[:, columns(h)] = (mixing * retrieved + (1.0 - mixing) * local_out[h]).astype(jnp.bfloat16)
        grad_ret = mixing * cot[:, columns(h)].astype(jnp.float32)
        grad_den = -jnp.sum(grad_ret * retrieved, axis=1, keepdims=True) / den[h]
        n2_own[h] = jnp.sum(grad_den * phi, axis=0, keepdims=True)
        grad_phi = dot_nt(grad_num[h], memory) + grad_den * norms[h]
        grads[h, :, :dim] = (dq_att[h] + grad_phi * feature_slope(query)).astype(jnp.bfloat16)

    each_head(retrieve)
    grad_norm_scan.start()
    grad_memory_scan.give_back()
    grad_norm_scan.across_rows()
    norms[...] = grad_norm_scan.result()
    back_keys.wait_recv()
    back_values.wait_recv()
    grad_memory_scan.finish()

    def write_back(h):
        key = kvq[h].astype(jnp.float32)
        grad_memory = grad_memory_scan.head(h, heads)
        grad_phi = dot_nt(kvq[heads + h], grad_memory) + norms[h]
        grad_key = own_grads[h] + halo_in[h].astype(jnp.float32) + grad_phi * feature_slope(key)
        grads[h, :, dim:2 * dim] = grad_key.astype(jnp.bfloat16)
        grad_value = dot_nn(feature(key).astype(jnp.bfloat16), grad_memory)
        grad_value = own_grads[heads + h] + halo_in[heads + h].astype(jnp.float32) + grad_value
        grads[h, :, 2 * dim:] = grad_value.astype(jnp.bfloat16)

    each_head(write_back)

    g_out = pair_copy(grads.at[1 - dp], g_all.at[pl.ds(tokens, tokens)], 1)
    g_out.start()
    g_all[pl.ds(0, tokens), :] = grads[dp]
    x_out.wait_recv()
    g_out.wait_recv()
    tile = min(wide, 256)

    def products(target):
        def body(i, carry):
            start = pl.multiple_of(target * wide + i * tile, 128)
            dw[target, pl.ds(pl.multiple_of(i * tile, 8), tile), :] = dot_tn(x_all[:, pl.ds(start, tile)], g_all[...])
            return carry
        lax.fori_loop(0, wide // tile, body, 0)

    def a1_mine(target, sub):
        return dw[:, pl.ds(pl.multiple_of(target * block + sub * rows, 8), rows), :half]

    def b1_mine(target, sub):
        return dw[target, sub * (wide // 2):(sub + 1) * (wide // 2), half:]

    def b2_mine(target, sub):
        return b_sum[pl.ds(pl.multiple_of(target * block + sub * rows, 8), rows), :]

    a1 = RingSum("z", a1_mine, a1_send, a1_recv, z1_sem.at[0], z1_sem.at[1])
    b1 = RingSum("y", b1_mine, b1_send, b1_recv, y1_sem.at[0], y1_sem.at[1])
    a2 = RingSum("y", lambda k, sub: a_sum[sub, k], a2_send, a2_recv, y2_sem.at[0], y2_sem.at[1])
    b2 = RingSum("z", b2_mine, b2_send, b2_recv, z2_sem.at[0], z2_sem.at[1])

    for step in range(ny):
        ahead = ny // 2 - step
        products(lax.rem(y + ahead + ny, ny))
        b1.step(0, ahead)
    a1.step(0)
    a1.step(1)
    b1.step(1)
    for t in range(2, nz // 2):
        a1.step(t)
    for sub in (0, 1):
        b_sum[sub * (wide // 2):(sub + 1) * (wide // 2), :] = b1.total(sub)
    b2.step(0)
    for sub in (0, 1):
        a_sum[sub] = a1.total(sub)
    for t in range(max(ny, nz) // 2):
        a2.step(t)
        b2.step(t + 1)
    for sub in (0, 1):
        fin[sub, :, :half] = a2.total(sub) * scale
        fin[sub, :, half:] = b2.total(sub) * scale
    swap_out = pair_copy(fin.at[1 - dp], swap, 2)
    swap_out.start()
    out_ref[dp] = fin[dp]
    for sent in (
        a1, b1, a2, b2, norm_scan, grad_norm_scan, memory_scan, grad_memory_scan,
    ):
        sent.drain()
    for copy in (halo_keys, halo_values, back_keys, back_values, x_out, g_out):
        copy.wait_send()
    swap_out.wait()
    out_ref[1 - dp] = swap[...]


def layer(x, wq, wk, wv, gate, cot, scale):
    tokens, depth = x.shape
    heads = gate.shape[0]
    dim = wq.shape[1] // heads
    cols = 3 * dim
    ny, nz = lax.axis_size("y"), lax.axis_size("z")
    wide = depth // ny
    rows = wide // nz // 2
    half = cols // 2
    zs, ys = 2 * (nz - 1), 2 * (ny - 1)
    wire = lambda *shape: pltpu.VMEM(shape, jnp.bfloat16)
    real = lambda *shape: pltpu.VMEM(shape, jnp.float32)
    dma = lambda *shape: pltpu.SemaphoreType.DMA(shape)
    a1, b1, last = (zs, ny, rows, half), (ys, wide // 2, half), (rows, half)
    part = (heads * dim // nz, dim)
    vectors = [real(heads, 1, dim), real(nz, heads, 1, dim), real(heads, 1, dim), real(ny, heads, 1, dim)]
    scan = [
        wire(nz, *part), wire(nz, *part), real(nz, *part), real(*part), real(ny, *part), wire(nz, *part),
        wire(nz, *part),
    ]
    pair = (2 * heads, tokens, dim)
    anywhere = pl.BlockSpec(memory_space=pl.ANY)
    return pl.pallas_call(
        functools.partial(layer_kernel, scale),
        out_shape=(
            jax.ShapeDtypeStruct((tokens, heads * dim), jnp.bfloat16),
            jax.ShapeDtypeStruct((2, rows, cols), jnp.float32),
        ),
        in_specs=[anywhere] * 4 + [pl.BlockSpec(memory_space=pltpu.SMEM), anywhere],
        out_specs=(pl.BlockSpec(memory_space=pltpu.VMEM),) * 2,
        scratch_shapes=[
            wire(2 * tokens, depth), wire(3 * heads, depth, dim), wire(tokens, heads * dim),
            wire(3 * heads, tokens, dim), wire(*pair), wire(*pair), wire(*pair), real(*pair),
            real(heads, tokens, dim), real(heads, tokens, dim),
            real(heads, tokens, tokens), real(heads, tokens, tokens), wire(heads, tokens, dim),
            wire(heads, tokens, dim), real(heads, tokens, 1), wire(heads, tokens, cols), wire(2 * tokens, cols),
            *vectors, *vectors, real(heads, 1, dim), *scan, *scan,
            real(ny, wide, cols), real(2, ny, rows, half), real(wide, half), real(2, rows, cols), real(rows, cols),
            wire(*a1), wire(*a1), wire(*b1), wire(*b1),
            wire(ys, *last), wire(ys, *last), wire(zs, *last), wire(zs, *last),
            dma(2 + 3 * heads), dma(2, 4), dma(2, 3), dma(2, 2, nz), dma(2, 2, ny),
            dma(2, 2, nz), dma(2, 2, ny), dma(2, 2, nz), dma(2, zs), dma(2, ys), dma(2, ys), dma(2, zs),
        ],
        compiler_params=pltpu.CompilerParams(
            collective_id=1, has_side_effects=True, vmem_limit_bytes=63 * 1024 * 1024
        ),
    )(x, wq, wk, wv, gate, cot)


def local(inputs, w_query, w_key, w_value, gate_bias, cotangent):
    tokens = inputs[0]
    seg_len = tokens.shape[0]
    columns = w_query.shape[1]
    head_dim = columns // gate_bias.shape[0]
    scale = 1.0 / math.sqrt(lax.axis_size(SEQ) * lax.axis_size("dp") * seg_len)
    blended, summed = layer(tokens, w_query, w_key, w_value, gate_bias, cotangent[0], scale)
    rows = summed.shape[1]
    grad_weights = summed.reshape(2, rows, 3, head_dim).transpose(1, 2, 0, 3).reshape(rows, 3, columns)
    return (blended[None], grad_weights)


def solution(mesh):
    finer = Mesh(
        mesh.devices.reshape(4, 8, mesh.shape["dp"], mesh.shape["head"]),
        ("y", "z", "dp", "head"),
    )
    placed = (
        P("dp", SEQ, None),
        P(None, "head"),
        P(None, "head"),
        P(None, "head"),
        P("head"),
        P("dp", SEQ, "head"),
    )
    return jax.shard_map(
        local,
        mesh=finer,
        in_specs=placed,
        out_specs=(P("dp", SEQ, "head"), P(SEQ_DP, None, "head")),
        check_vma=False,
    )
```

```python
import functools
import math

import jax
import jax.numpy as jnp
from jax import lax
from jax.experimental import pallas as pl
from jax.experimental.pallas import tpu as pltpu
from jax.sharding import Mesh
from jax.sharding import PartitionSpec as P

SEQ = ("y", "z")
SEQ_DP = ("y", "z", "dp")
MESH = pl.DeviceIdType.MESH
MASKED = -1e30


def feature(u):
    return jnp.where(u > 0, u + 1.0, jnp.exp(jnp.minimum(u, 0.0)))


def feature_slope(u):
    return jnp.where(u > 0, 1.0, jnp.exp(jnp.minimum(u, 0.0)))


def contract(a, b, over_a, over_b):
    return lax.dot_general(
        a, b, (((over_a,), (over_b,)), ((), ())), preferred_element_type=jnp.float32
    )


def dot_nn(a, b):
    return contract(a, b, 1, 0)


def dot_nt(a, b):
    return contract(a, b, 1, 1)


def dot_tn(a, b):
    return contract(a, b, 0, 0)


def ring_chains(n):
    chains, first = [], 0
    for sub in (0, 1):
        for way in (1, -1):
            length = n // 2 if (way > 0) == (sub == 0) else n - 1 - n // 2
            chains.append((sub, way, length, first))
            first += length
    return chains


class RingSum:
    def __init__(self, axis, mine, send, recv, send_sem, recv_sem):
        self.axis, self.mine = axis, mine
        self.n, self.position = lax.axis_size(axis), lax.axis_index(axis)
        self.send, self.recv, self.send_sem, self.recv_sem = send, recv, send_sem, recv_sem
        self.chains = ring_chains(self.n)

    def copy(self, slot, way):
        return pltpu.make_async_remote_copy(
            src_ref=self.send.at[slot],
            dst_ref=self.recv.at[slot],
            send_sem=self.send_sem.at[slot],
            recv_sem=self.recv_sem.at[slot],
            device_id={self.axis: lax.rem(self.position + way + self.n, self.n)},
            device_id_type=MESH,
        )

    def step(self, t, ahead=None):
        for sub, way, length, first in self.chains:
            if t >= length:
                continue
            if ahead is not None and (way * (length - t)) % self.n != ahead % self.n:
                continue
            target = lax.rem(self.position + way * (length - t) + self.n, self.n)
            value = self.mine(target, sub)
            if t:
                self.copy(first + t - 1, way).wait_recv()
                value = value + self.recv[first + t - 1].astype(jnp.float32)
            self.send[first + t] = value.astype(jnp.bfloat16)
            self.copy(first + t, way).start()

    def total(self, sub):
        value = self.mine(self.position, sub)
        for chain_sub, way, length, first in self.chains:
            if chain_sub == sub and length:
                self.copy(first + length - 1, way).wait_recv()
                value = value + self.recv[first + length - 1].astype(jnp.float32)
        return value

    def drain(self):
        for _, way, length, first in self.chains:
            for t in range(length):
                self.copy(first + t, way).wait_send()


class Spread:
    def __init__(self, axis, got, sem):
        self.axis, self.got, self.sem = axis, got, sem
        self.n, self.position = lax.axis_size(axis), lax.axis_index(axis)

    def copy(self, src, j):
        return pltpu.make_async_remote_copy(
            src_ref=src,
            dst_ref=self.got.at[j],
            send_sem=self.sem.at[0, j],
            recv_sem=self.sem.at[1, j],
            device_id={self.axis: lax.rem(self.position + j, self.n)},
            device_id_type=MESH,
        )

    def start(self, src):
        self.src = src
        for j in range(1, self.n):
            self.copy(src, j).start()

    def sums(self, own, reverse):
        passed, total = jnp.zeros_like(own), own
        for j in range(1, self.n):
            self.copy(self.src, j).wait_recv()
            value = self.got[j]
            earlier = self.position < j if reverse else self.position >= j
            passed = passed + value * jnp.where(earlier, 1.0, 0.0)
            total = total + value
        return passed, total

    def drain(self):
        for j in range(1, self.n):
            self.copy(self.src, j).wait_send()


class VectorScan:
    def __init__(self, reverse, own, z_got, y_own, y_got, z_sem, y_sem):
        self.reverse, self.own, self.y_own = reverse, own, y_own
        self.z, self.y = Spread("z", z_got, z_sem), Spread("y", y_got, y_sem)

    def start(self):
        self.z.start(self.own)

    def across_rows(self):
        self.inside, total = self.z.sums(self.own[...], self.reverse)
        self.y_own[...] = total
        self.y.start(self.y_own)

    def result(self):
        passed, _ = self.y.sums(self.y_own[...], self.reverse)
        return passed + self.inside

    def drain(self):
        self.z.drain()
        self.y.drain()


class MemoryScan:
    def __init__(self, reverse, parts, got, inside, y_own, y_got, back, result, z_sem, y_sem, back_sem):
        self.reverse, self.parts, self.got, self.inside, self.y_own = reverse, parts, got, inside, y_own
        self.back, self.full, self.z_sem, self.back_sem = back, result, z_sem, back_sem
        self.n, self.position = lax.axis_size("z"), lax.axis_index("z")
        self.y = Spread("y", y_got, y_sem)

    def out_copy(self, j):
        target = lax.rem(self.position + j, self.n)
        return pltpu.make_async_remote_copy(
            src_ref=self.parts.at[target],
            dst_ref=self.got.at[j],
            send_sem=self.z_sem.at[0, j],
            recv_sem=self.z_sem.at[1, j],
            device_id={"z": target},
            device_id_type=MESH,
        )

    def back_copy(self, j):
        target = lax.rem(self.position + j, self.n)
        return pltpu.make_async_remote_copy(
            src_ref=self.back.at[target],
            dst_ref=self.full.at[self.position],
            send_sem=self.back_sem.at[0, j],
            recv_sem=self.back_sem.at[1, j],
            device_id={"z": target},
            device_id_type=MESH,
        )

    def start(self):
        for j in range(1, self.n):
            self.out_copy(j).start()

    def across_rows(self):
        for j in range(1, self.n):
            self.out_copy(j).wait_recv()
        self.got[0] = self.parts[self.position]
        run = jnp.zeros(self.y_own.shape, jnp.float32)
        for k in reversed(range(self.n)) if self.reverse else range(self.n):
            self.inside[k] = run
            run = run + self.got[lax.rem(self.position - k + self.n, self.n)].astype(jnp.float32)
        self.y_own[...] = run
        self.y.start(self.y_own)

    def give_back(self):
        passed, _ = self.y.sums(self.y_own[...], self.reverse)
        for k in range(self.n):
            self.back[k] = (self.inside[k] + passed).astype(jnp.bfloat16)
        for j in range(1, self.n):
            self.back_copy(j).start()
        self.full[self.position] = self.back[self.position]

    def finish(self):
        for j in range(1, self.n):
            self.back_copy(j).wait_recv()

    def head(self, h, heads):
        parts = self.n // heads
        block = self.full[pl.ds(h * parts, parts)]
        return block.reshape(parts * block.shape[1], block.shape[2])

    def drain(self):
        self.y.drain()
        for j in range(1, self.n):
            self.out_copy(j).wait_send()
            self.back_copy(j).wait_send()


def layer_kernel(
    scale, x_ref, wq_ref, wk_ref, wv_ref, gate_ref, cot_ref, blended_ref, out_ref,
    x_all, w_all, cot, kvq, prev, after_in, own_grads, dq_ret, ret_mix,
    scores, soft_grads, grad_local, grad_num, den, stats, stats_in, grads, g_all,
    n1_own, n1_got, n1_yown, n1_ygot, n2_own, n2_got, n2_yown, n2_ygot, norms,
    m1_parts, m1_got, m1_inside, m1_yown, m1_ygot, m1_back, m1_full,
    m2_parts, m2_got, m2_inside, m2_yown, m2_ygot, m2_back, m2_full,
    dw, a_sum, b_sum, q_sum, fin, swap,
    a1_send, a1_recv, b1_send, b1_recv, q1_send, q1_recv, a2_send, a2_recv, b2_send, b2_recv, q2_send, q2_recv,
    local_sem, halo_sem, pair_sem, nz_sem, ny_sem, mz_sem, my_sem, mb_sem, z1_sem, y1_sem, yq_sem, y2_sem, z2_sem, zq_sem,
):
    ny, nz = lax.axis_size("y"), lax.axis_size("z")
    y, z, dp = lax.axis_index("y"), lax.axis_index("z"), lax.axis_index("dp")
    other = {"dp": 1 - dp}
    tokens = x_ref.shape[0]
    heads, dim = kvq.shape[0] // 3, kvq.shape[2]
    wide = dw.shape[2]
    block = wide // nz
    rows = block // 2
    up, down = z == nz - 1, z == 0
    after = {
        "y": lax.rem(y + jnp.where(up, 1, 0), ny), "z": lax.rem(z + 1, nz),
    }
    ahead_of = {
        "y": lax.rem(y - jnp.where(down, 1, 0) + ny, ny), "z": lax.rem(z - 1 + nz, nz),
    }
    score_scale = dim ** (-0.5)

    barrier = pltpu.get_barrier_semaphore()
    partners = [other, after, ahead_of]
    partners += [{"z": lax.rem(z + j, nz)} for j in range(1, nz)]
    partners += [{"y": lax.rem(y + j, ny)} for j in range(1, ny)]
    for device in partners:
        pl.semaphore_signal(barrier, inc=1, device_id=device, device_id_type=MESH)

    x_in = pltpu.make_async_copy(x_ref, x_all.at[pl.ds(0, tokens)], local_sem.at[0])
    cot_in = pltpu.make_async_copy(cot_ref, cot, local_sem.at[1])
    w_in = [
        pltpu.make_async_copy(w.at[:, pl.ds(h * dim, dim)], w_all.at[at * heads + h], local_sem.at[2 + at * heads + h])
        for at, w in enumerate((wk_ref, wv_ref, wq_ref)) for h in range(heads)
    ]
    x_in.start()
    for copy in w_in[:heads]:
        copy.start()
    cot_in.start()
    for copy in w_in[heads:]:
        copy.start()

    def project(at):
        for h in range(heads):
            w_in[at * heads + h].wait()
        def body(h, carry):
            c = at * heads + h
            kvq[c] = dot_nn(x_all[pl.ds(0, tokens), :], w_all[c]).astype(jnp.bfloat16)
            return carry
        lax.fori_loop(0, heads, body, 0)

    def halo_copy(src, dst, slot, device):
        return pltpu.make_async_remote_copy(
            src_ref=src, dst_ref=dst, send_sem=halo_sem.at[0, slot], recv_sem=halo_sem.at[1, slot],
            device_id=device, device_id_type=MESH,
        )

    key_out = [halo_copy(kvq.at[h], prev.at[h], h, after) for h in range(heads)]
    value_out = halo_copy(kvq.at[pl.ds(heads, heads)], prev.at[pl.ds(heads, heads)], heads, after)
    local_out = [
        halo_copy(grad_local.at[h], after_in.at[heads + h], heads + 1 + h, ahead_of) for h in range(heads)
    ]
    query_out = halo_copy(kvq.at[pl.ds(2 * heads, heads)], after_in.at[pl.ds(0, heads)], 2 * heads + 1, ahead_of)
    stats_out = halo_copy(stats, stats_in, 2 * heads + 2, ahead_of)

    def pair_copy(src, dst, slot):
        return pltpu.make_async_remote_copy(
            src_ref=src, dst_ref=dst, send_sem=pair_sem.at[0, slot], recv_sem=pair_sem.at[1, slot],
            device_id=other, device_id_type=MESH,
        )

    def each_head(body):
        def step(h, carry):
            body(h)
            return carry
        lax.fori_loop(0, heads, step, 0)

    def columns(h):
        return pl.ds(pl.multiple_of(h * dim, dim), dim)

    norm_scan = VectorScan(False, n1_own, n1_got, n1_yown, n1_ygot, nz_sem.at[0], ny_sem.at[0])
    grad_norm_scan = VectorScan(True, n2_own, n2_got, n2_yown, n2_ygot, nz_sem.at[1], ny_sem.at[1])
    memory_scan = MemoryScan(
        False, m1_parts, m1_got, m1_inside, m1_yown, m1_ygot, m1_back, m1_full,
        mz_sem.at[0], my_sem.at[0], mb_sem.at[0],
    )
    grad_memory_scan = MemoryScan(
        True, m2_parts, m2_got, m2_inside, m2_yown, m2_ygot, m2_back, m2_full,
        mz_sem.at[1], my_sem.at[1], mb_sem.at[1],
    )
    parts = nz // heads

    def put_parts(target, h, value):
        target[pl.ds(h * parts, parts)] = value.astype(jnp.bfloat16).reshape(parts, dim // parts, dim)

    def mixing_of(h):
        return 1.0 / (1.0 + jnp.exp(-jnp.full((1, dim), gate_ref[h], jnp.float32)))

    x_in.wait()
    project(0)

    def key_sums(h):
        n1_own[h] = jnp.sum(feature(kvq[h].astype(jnp.float32)), axis=0, keepdims=True)

    each_head(key_sums)
    cot_in.wait()

    def local_gradient(h):
        upstream = cot[:, columns(h)].astype(jnp.float32)
        grad_local[h] = ((1.0 - mixing_of(h)) * upstream).astype(jnp.bfloat16)

    each_head(local_gradient)
    pl.semaphore_wait(barrier, len(partners))
    norm_scan.start()
    key_out[0].start()
    local_out[0].start()
    x_out = pair_copy(x_all.at[pl.ds(0, tokens)], x_all.at[pl.ds(tokens, tokens)], 0)
    x_out.start()
    project(1)

    def write(h):
        phi = feature(kvq[h].astype(jnp.float32)).astype(jnp.bfloat16)
        put_parts(m1_parts, h, dot_tn(phi, kvq[heads + h]))

    each_head(write)
    memory_scan.start()
    project(2)
    norm_scan.across_rows()

    def own_part(h):
        row = lax.broadcasted_iota(jnp.int32, (tokens, tokens), 0)
        col = lax.broadcasted_iota(jnp.int32, (tokens, tokens), 1)
        scores[h] = jnp.where(col <= row, dot_nt(kvq[2 * heads + h], kvq[h]) * score_scale, MASKED)
        soft_grads[h] = dot_nt(grad_local[h], kvq[heads + h])

    each_head(own_part)
    norms[0] = norm_scan.result()

    def memory_gradient(h):
        phi = feature(kvq[2 * heads + h].astype(jnp.float32))
        divisor = jnp.sum(phi * norms[0, h], axis=1, keepdims=True) + 1.0
        den[h] = divisor
        grad_ret = mixing_of(h) * cot[:, columns(h)].astype(jnp.float32)
        number = (grad_ret / divisor).astype(jnp.bfloat16)
        grad_num[h] = number
        put_parts(m2_parts, h, dot_tn(phi.astype(jnp.bfloat16), number))

    each_head(memory_gradient)
    grad_memory_scan.start()
    for h in range(1, heads):
        key_out[h].start()
        local_out[h].start()
    memory_scan.across_rows()
    memory_scan.give_back()
    value_out.start()
    query_out.start()
    grad_memory_scan.across_rows()

    x_out.wait_recv()
    spans = 2 * tokens // dim
    tile = min(wide, 256)

    def turn(i, carry):
        at = pl.ds(pl.multiple_of(i * tile, 128), tile)
        for c in range(spans):
            w_all[c, at, :] = x_all[c * dim:(c + 1) * dim, at].T
        return carry

    lax.fori_loop(0, x_all.shape[1] // tile, turn, 0)
    memory_scan.finish()

    def retrieve(h):
        mixing = mixing_of(h)
        query = kvq[2 * heads + h].astype(jnp.float32)
        phi = feature(query)
        memory = memory_scan.head(h, heads)
        retrieved = dot_nn(phi.astype(jnp.bfloat16), memory) / den[h]
        ret_mix[h] = mixing * retrieved
        grad_ret = mixing * cot[:, columns(h)].astype(jnp.float32)
        grad_den = -jnp.sum(grad_ret * retrieved, axis=1, keepdims=True) / den[h]
        n2_own[h] = jnp.sum(grad_den * phi, axis=0, keepdims=True)
        grad_phi = dot_nt(grad_num[h], memory) + grad_den * norms[0, h]
        dq_ret[h] = grad_phi * feature_slope(query)

    each_head(retrieve)
    grad_norm_scan.start()
    grad_memory_scan.give_back()

    segment, last = y * nz + z, ny * nz - 1
    bias = jnp.where(segment > 0, 0.0, MASKED)
    bias_after = jnp.where(segment < last, 0.0, MASKED)
    for copy in key_out:
        copy.wait_recv()
    value_out.wait_recv()

    def as_row(column):
        return jnp.broadcast_to(column, (tokens, 128)).T[:1]

    def attend(h):
        query, key, value = kvq[2 * heads + h], kvq[h], kvq[heads + h]
        key_prev, value_prev, local = prev[h], prev[heads + h], grad_local[h]
        s_own = scores[h]
        s_prev = dot_nt(query, key_prev) * score_scale + bias
        top = jnp.maximum(jnp.max(s_own, axis=1, keepdims=True), jnp.max(s_prev, axis=1, keepdims=True))
        e_own, e_prev = jnp.exp(s_own - top), jnp.exp(s_prev - top)
        inverse = 1.0 / (jnp.sum(e_own, axis=1, keepdims=True) + jnp.sum(e_prev, axis=1, keepdims=True))
        p_own, p_prev = e_own * inverse, e_prev * inverse
        b_own, b_prev = p_own.astype(jnp.bfloat16), p_prev.astype(jnp.bfloat16)
        near = dot_nn(b_own, value) + dot_nn(b_prev, value_prev)
        blended_ref[:, columns(h)] = (ret_mix[h] + (1.0 - mixing_of(h)) * near).astype(jnp.bfloat16)
        g_own, g_prev = soft_grads[h], dot_nt(local, value_prev)
        row_dot = jnp.sum(p_own * g_own, axis=1, keepdims=True) + jnp.sum(p_prev * g_prev, axis=1, keepdims=True)
        stats[h, 0:1] = as_row(top)
        stats[h, 1:2] = as_row(inverse)
        stats[h, 2:3] = as_row(row_dot)
        d_own = (p_own * (g_own - row_dot) * score_scale).astype(jnp.bfloat16)
        d_prev = (p_prev * (g_prev - row_dot) * score_scale).astype(jnp.bfloat16)
        own_grads[h] = dot_tn(d_own, query)
        own_grads[heads + h] = dot_tn(b_own, local)
        dq_att = dot_nn(d_own, key) + dot_nn(d_prev, key_prev)
        grads[0, h] = (dq_att + dq_ret[h]).astype(jnp.bfloat16)

    for h in range(heads):
        stats[h] = jnp.zeros(stats.shape[1:], jnp.float32)
    each_head(attend)
    stats_out.start()

    def pair_grads(m):
        return pair_copy(grads.at[m, 1 - dp], g_all.at[m, pl.ds(tokens, tokens)], 1 + m)

    def keep_grads(m):
        g_all[m, pl.ds(0, tokens), :] = grads[m, dp]

    def products(m, target):
        def body(i, carry):
            at = pl.multiple_of(target * wide + i * tile, 128)
            total = dot_nn(w_all[0, pl.ds(at, tile), :], g_all[m, 0:dim, :])
            for c in range(1, spans):
                total = total + dot_nn(w_all[c, pl.ds(at, tile), :], g_all[m, c * dim:(c + 1) * dim, :])
            dw[m, target, pl.ds(pl.multiple_of(i * tile, 8), tile), :] = total
            return carry
        lax.fori_loop(0, wide // tile, body, 0)

    def a1_mine(target, sub):
        return dw[1, :, pl.ds(pl.multiple_of(target * block + sub * rows, 8), rows), :]

    def y_first(m):
        return lambda target, sub: dw[m, target, sub * (wide // 2):(sub + 1) * (wide // 2), :]

    def z_second(held):
        return lambda target, sub: held[pl.ds(pl.multiple_of(target * block + sub * rows, 8), rows), :]

    a1 = RingSum("z", a1_mine, a1_send, a1_recv, z1_sem.at[0], z1_sem.at[1])
    b1 = RingSum("y", y_first(2), b1_send, b1_recv, y1_sem.at[0], y1_sem.at[1])
    q1 = RingSum("y", y_first(0), q1_send, q1_recv, yq_sem.at[0], yq_sem.at[1])
    a2 = RingSum("y", lambda k, sub: a_sum[sub, k], a2_send, a2_recv, y2_sem.at[0], y2_sem.at[1])
    b2 = RingSum("z", z_second(b_sum), b2_send, b2_recv, z2_sem.at[0], z2_sem.at[1])
    q2 = RingSum("z", z_second(q_sum), q2_send, q2_recv, zq_sem.at[0], zq_sem.at[1])

    def rows_in(ring, held):
        for sub in (0, 1):
            held[sub * (wide // 2):(sub + 1) * (wide // 2), :] = ring.total(sub)

    query_pair = pair_grads(0)
    query_pair.start()
    keep_grads(0)
    grad_norm_scan.across_rows()
    query_pair.wait_recv()
    for step in range(ny):
        ahead = ny // 2 - step
        products(0, lax.rem(y + ahead + ny, ny))
        q1.step(0, ahead)

    for copy in local_out:
        copy.wait_recv()
    query_out.wait_recv()
    stats_out.wait_recv()

    def serve(h):
        query, local = after_in[h], after_in[heads + h]
        top, inverse, row_dot = stats_in[h, 0:1], stats_in[h, 1:2], stats_in[h, 2:3]
        soft = jnp.exp(dot_nt(kvq[h], query) * score_scale + bias_after - top) * inverse
        given = (soft * (dot_nt(kvq[heads + h], local) - row_dot) * score_scale).astype(jnp.bfloat16)
        own_grads[h] += dot_nn(given, query)
        own_grads[heads + h] += dot_nn(soft.astype(jnp.bfloat16), local)

    each_head(serve)
    norms[1] = grad_norm_scan.result()
    grad_memory_scan.finish()

    def write_back(h):
        key = kvq[h].astype(jnp.float32)
        grad_memory = grad_memory_scan.head(h, heads)
        grad_phi = dot_nt(kvq[heads + h], grad_memory) + norms[1, h]
        grads[1, h] = (own_grads[h] + grad_phi * feature_slope(key)).astype(jnp.bfloat16)
        grad_value = dot_nn(feature(key).astype(jnp.bfloat16), grad_memory)
        grads[2, h] = (own_grads[heads + h] + grad_value).astype(jnp.bfloat16)

    each_head(write_back)
    key_pair, value_pair = pair_grads(1), pair_grads(2)
    key_pair.start()
    value_pair.start()
    keep_grads(1)
    keep_grads(2)
    key_pair.wait_recv()
    for k in range(ny):
        products(1, k)
    a1.step(0)
    value_pair.wait_recv()
    for step in range(ny):
        ahead = ny // 2 - step
        products(2, lax.rem(y + ahead + ny, ny))
        b1.step(0, ahead)
    q1.step(1)
    a1.step(1)
    rows_in(q1, q_sum)
    q2.step(0)
    a1.step(2)
    b1.step(1)
    q2.step(1)
    a1.step(3)
    q2.step(2)
    rows_in(b1, b_sum)
    b2.step(0)
    for sub in (0, 1):
        a_sum[sub] = a1.total(sub)
    a2.step(0)
    q2.step(3)
    b2.step(1)
    a2.step(1)
    for t in range(2, nz // 2):
        b2.step(t)
    for sub in (0, 1):
        for m, ring in enumerate((q2, a2, b2)):
            fin[sub, :, m * dim:(m + 1) * dim] = ring.total(sub) * scale
    swap_out = pair_copy(fin.at[1 - dp], swap, 4)
    swap_out.start()
    for m in range(3):
        out_ref[m, :, columns(dp)] = fin[dp, :, m * dim:(m + 1) * dim]
    for sent in (
        a1, b1, q1, a2, b2, q2, norm_scan, grad_norm_scan, memory_scan, grad_memory_scan,
    ):
        sent.drain()
    for copy in (*key_out, value_out, *local_out, query_out, stats_out, x_out, query_pair, key_pair, value_pair):
        copy.wait_send()
    swap_out.wait()
    for m in range(3):
        out_ref[m, :, columns(1 - dp)] = swap[:, m * dim:(m + 1) * dim]


def layer(x, wq, wk, wv, gate, cot, scale):
    tokens, depth = x.shape
    heads = gate.shape[0]
    dim = wq.shape[1] // heads
    ny, nz = lax.axis_size("y"), lax.axis_size("z")
    wide = depth // ny
    rows = wide // nz // 2
    zs, ys = 2 * (nz - 1), 2 * (ny - 1)
    wire = lambda *shape: pltpu.VMEM(shape, jnp.bfloat16)
    real = lambda *shape: pltpu.VMEM(shape, jnp.float32)
    dma = lambda *shape: pltpu.SemaphoreType.DMA(shape)
    a1, b1, last = (zs, ny, rows, dim), (ys, wide // 2, dim), (rows, dim)
    part = (heads * dim // nz, dim)
    vectors = [real(heads, 1, dim), real(nz, heads, 1, dim), real(heads, 1, dim), real(ny, heads, 1, dim)]
    scan = [
        wire(nz, *part), wire(nz, *part), real(nz, *part), real(*part), real(ny, *part), wire(nz, *part),
        wire(nz, *part),
    ]
    pair = (2 * heads, tokens, dim)
    anywhere = pl.BlockSpec(memory_space=pl.ANY)
    return pl.pallas_call(
        functools.partial(layer_kernel, scale),
        out_shape=(
            jax.ShapeDtypeStruct((tokens, heads * dim), jnp.bfloat16),
            jax.ShapeDtypeStruct((3, rows, heads * dim), jnp.float32),
        ),
        in_specs=[anywhere] * 4 + [pl.BlockSpec(memory_space=pltpu.SMEM), anywhere],
        out_specs=(pl.BlockSpec(memory_space=pltpu.VMEM),) * 2,
        scratch_shapes=[
            wire(2 * tokens, depth), wire(3 * heads, depth, dim), wire(tokens, heads * dim),
            wire(3 * heads, tokens, dim), wire(*pair), wire(*pair), real(*pair),
            real(heads, tokens, dim), real(heads, tokens, dim),
            real(heads, tokens, tokens), real(heads, tokens, tokens), wire(heads, tokens, dim),
            wire(heads, tokens, dim), real(heads, tokens, 1), real(heads, 8, tokens), real(heads, 8, tokens),
            wire(3, heads, tokens, dim), wire(3, 2 * tokens, dim),
            *vectors, *vectors, real(2, heads, 1, dim), *scan, *scan,
            real(3, ny, wide, dim), real(2, ny, rows, dim), real(wide, dim), real(wide, dim),
            real(2, rows, 3 * dim), real(rows, 3 * dim),
            wire(*a1), wire(*a1), wire(*b1), wire(*b1), wire(*b1), wire(*b1),
            wire(ys, *last), wire(ys, *last), wire(zs, *last), wire(zs, *last), wire(zs, *last), wire(zs, *last),
            dma(2 + 3 * heads), dma(2, 2 * heads + 3), dma(2, 5), dma(2, 2, nz), dma(2, 2, ny),
            dma(2, 2, nz), dma(2, 2, ny), dma(2, 2, nz),
            dma(2, zs), dma(2, ys), dma(2, ys), dma(2, ys), dma(2, zs), dma(2, zs),
        ],
        compiler_params=pltpu.CompilerParams(
            collective_id=1, has_side_effects=True, vmem_limit_bytes=63 * 1024 * 1024
        ),
    )(x, wq, wk, wv, gate, cot)


def local(inputs, w_query, w_key, w_value, gate_bias, cotangent):
    tokens = inputs[0]
    seg_len = tokens.shape[0]
    scale = 1.0 / math.sqrt(lax.axis_size(SEQ) * lax.axis_size("dp") * seg_len)
    blended, grad_weights = layer(tokens, w_query, w_key, w_value, gate_bias, cotangent[0], scale)
    return (blended[None], grad_weights.transpose(1, 0, 2))


def solution(mesh):
    finer = Mesh(
        mesh.devices.reshape(4, 8, mesh.shape["dp"], mesh.shape["head"]),
        ("y", "z", "dp", "head"),
    )
    placed = (
        P("dp", SEQ, None),
        P(None, "head"),
        P(None, "head"),
        P(None, "head"),
        P("head"),
        P("dp", SEQ, "head"),
    )
    return jax.shard_map(
        local,
        mesh=finer,
        in_specs=placed,
        out_specs=(P("dp", SEQ, "head"), P(SEQ_DP, None, "head")),
        check_vma=False,
    )
```

```python
import functools
import math

import jax
import jax.numpy as jnp
from jax import lax
from jax.experimental import pallas as pl
from jax.experimental.pallas import tpu as pltpu
from jax.sharding import Mesh
from jax.sharding import PartitionSpec as P

SEQ = ("y", "z")
SEQ_DP = ("y", "z", "dp")
MESH = pl.DeviceIdType.MESH
MASKED = -1e30


def feature(u):
    return jnp.where(u > 0, u + 1.0, jnp.exp(jnp.minimum(u, 0.0)))


def feature_slope(u):
    return jnp.where(u > 0, 1.0, jnp.exp(jnp.minimum(u, 0.0)))


def contract(a, b, over_a, over_b):
    return lax.dot_general(
        a, b, (((over_a,), (over_b,)), ((), ())), preferred_element_type=jnp.float32
    )


def dot_nn(a, b):
    return contract(a, b, 1, 0)


def dot_nt(a, b):
    return contract(a, b, 1, 1)


def dot_tn(a, b):
    return contract(a, b, 0, 0)


def ring_chains(n):
    chains, first = [], 0
    for sub in (0, 1):
        for way in (1, -1):
            length = n // 2 if (way > 0) == (sub == 0) else n - 1 - n // 2
            chains.append((sub, way, length, first))
            first += length
    return chains


class RingSum:
    def __init__(self, axis, mine, send, recv, send_sem, recv_sem):
        self.axis, self.mine = axis, mine
        self.n, self.position = lax.axis_size(axis), lax.axis_index(axis)
        self.send, self.recv, self.send_sem, self.recv_sem = send, recv, send_sem, recv_sem
        self.chains = ring_chains(self.n)

    def copy(self, slot, way):
        return pltpu.make_async_remote_copy(
            src_ref=self.send.at[slot],
            dst_ref=self.recv.at[slot],
            send_sem=self.send_sem.at[slot],
            recv_sem=self.recv_sem.at[slot],
            device_id={self.axis: lax.rem(self.position + way + self.n, self.n)},
            device_id_type=MESH,
        )

    def step(self, t, ahead=None):
        for sub, way, length, first in self.chains:
            if t >= length:
                continue
            if ahead is not None and (way * (length - t)) % self.n != ahead % self.n:
                continue
            target = lax.rem(self.position + way * (length - t) + self.n, self.n)
            value = self.mine(target, sub)
            if t:
                self.copy(first + t - 1, way).wait_recv()
                value = value + self.recv[first + t - 1].astype(jnp.float32)
            self.send[first + t] = value.astype(jnp.bfloat16)
            self.copy(first + t, way).start()

    def total(self, sub):
        value = self.mine(self.position, sub)
        for chain_sub, way, length, first in self.chains:
            if chain_sub == sub and length:
                self.copy(first + length - 1, way).wait_recv()
                value = value + self.recv[first + length - 1].astype(jnp.float32)
        return value

    def drain(self):
        for _, way, length, first in self.chains:
            for t in range(length):
                self.copy(first + t, way).wait_send()


class Spread:
    def __init__(self, axis, got, sem):
        self.axis, self.got, self.sem = axis, got, sem
        self.n, self.position = lax.axis_size(axis), lax.axis_index(axis)

    def copy(self, src, j):
        return pltpu.make_async_remote_copy(
            src_ref=src,
            dst_ref=self.got.at[j],
            send_sem=self.sem.at[0, j],
            recv_sem=self.sem.at[1, j],
            device_id={self.axis: lax.rem(self.position + j, self.n)},
            device_id_type=MESH,
        )

    def start(self, src):
        self.src = src
        for j in range(1, self.n):
            self.copy(src, j).start()

    def sums(self, own, reverse):
        passed, total = jnp.zeros_like(own), own
        for j in range(1, self.n):
            self.copy(self.src, j).wait_recv()
            value = self.got[j]
            earlier = self.position < j if reverse else self.position >= j
            passed = passed + value * jnp.where(earlier, 1.0, 0.0)
            total = total + value
        return passed, total

    def drain(self):
        for j in range(1, self.n):
            self.copy(self.src, j).wait_send()


class VectorScan:
    def __init__(self, reverse, own, z_got, y_own, y_got, z_sem, y_sem):
        self.reverse, self.own, self.y_own = reverse, own, y_own
        self.z, self.y = Spread("z", z_got, z_sem), Spread("y", y_got, y_sem)

    def start(self):
        self.z.start(self.own)

    def across_rows(self):
        self.inside, total = self.z.sums(self.own[...], self.reverse)
        self.y_own[...] = total
        self.y.start(self.y_own)

    def result(self):
        passed, _ = self.y.sums(self.y_own[...], self.reverse)
        return passed + self.inside

    def drain(self):
        self.z.drain()
        self.y.drain()


class MemoryScan:
    def __init__(self, reverse, parts, got, inside, y_own, y_got, back, result, z_sem, y_sem, back_sem):
        self.reverse, self.parts, self.got, self.inside, self.y_own = reverse, parts, got, inside, y_own
        self.back, self.full, self.z_sem, self.back_sem = back, result, z_sem, back_sem
        self.n, self.position = lax.axis_size("z"), lax.axis_index("z")
        self.y = Spread("y", y_got, y_sem)

    def out_copy(self, j):
        target = lax.rem(self.position + j, self.n)
        return pltpu.make_async_remote_copy(
            src_ref=self.parts.at[target],
            dst_ref=self.got.at[j],
            send_sem=self.z_sem.at[0, j],
            recv_sem=self.z_sem.at[1, j],
            device_id={"z": target},
            device_id_type=MESH,
        )

    def back_copy(self, j):
        target = lax.rem(self.position + j, self.n)
        return pltpu.make_async_remote_copy(
            src_ref=self.back.at[target],
            dst_ref=self.full.at[self.position],
            send_sem=self.back_sem.at[0, j],
            recv_sem=self.back_sem.at[1, j],
            device_id={"z": target},
            device_id_type=MESH,
        )

    def start(self):
        for j in range(1, self.n):
            self.out_copy(j).start()

    def across_rows(self):
        for j in range(1, self.n):
            self.out_copy(j).wait_recv()
        self.got[0] = self.parts[self.position]
        run = jnp.zeros(self.y_own.shape, jnp.float32)
        for k in reversed(range(self.n)) if self.reverse else range(self.n):
            self.inside[k] = run
            run = run + self.got[lax.rem(self.position - k + self.n, self.n)].astype(jnp.float32)
        self.y_own[...] = run
        self.y.start(self.y_own)

    def give_back(self):
        passed, _ = self.y.sums(self.y_own[...], self.reverse)
        for k in range(self.n):
            self.back[k] = (self.inside[k] + passed).astype(jnp.bfloat16)
        for j in range(1, self.n):
            self.back_copy(j).start()
        self.full[self.position] = self.back[self.position]

    def finish(self):
        for j in range(1, self.n):
            self.back_copy(j).wait_recv()

    def head(self, h, heads):
        parts = self.n // heads
        block = self.full[pl.ds(h * parts, parts)]
        return block.reshape(parts * block.shape[1], block.shape[2])

    def drain(self):
        self.y.drain()
        for j in range(1, self.n):
            self.out_copy(j).wait_send()
            self.back_copy(j).wait_send()


def layer_kernel(
    scale, x_ref, wq_ref, wk_ref, wv_ref, gate_ref, cot_ref, blended_ref, out_ref,
    x_all, x_turned, w_all, cot, blended, kvq, prev, after_in, own_grads, dq_ret, ret_mix,
    scores, soft_grads, grad_local, grad_num, den, stats, stats_in, grads, g_all,
    n1_own, n1_got, n1_yown, n1_ygot, n2_own, n2_got, n2_yown, n2_ygot, norms,
    m1_parts, m1_got, m1_inside, m1_yown, m1_ygot, m1_back, m1_full,
    m2_parts, m2_got, m2_inside, m2_yown, m2_ygot, m2_back, m2_full,
    dw, a_sum, b_sum, c_sum, d_sum, fin, swap,
    a1_send, a1_recv, b1_send, b1_recv, c1_send, c1_recv, d1_send, d1_recv,
    a2_send, a2_recv, b2_send, b2_recv, c2_send, c2_recv, d2_send, d2_recv,
    local_sem, halo_sem, pair_sem, nz_sem, ny_sem, mz_sem, my_sem, mb_sem, ring_z_sem, ring_y_sem, out_sem,
):
    ny, nz = lax.axis_size("y"), lax.axis_size("z")
    y, z, dp = lax.axis_index("y"), lax.axis_index("z"), lax.axis_index("dp")
    other = {"dp": 1 - dp}
    tokens = x_ref.shape[0]
    heads, dim = kvq.shape[0] // 3, kvq.shape[2]
    wide = dw.shape[2]
    block = wide // nz
    rows = block // 2
    up, down = z == nz - 1, z == 0
    after = {
        "y": lax.rem(y + jnp.where(up, 1, 0), ny), "z": lax.rem(z + 1, nz),
    }
    ahead_of = {
        "y": lax.rem(y - jnp.where(down, 1, 0) + ny, ny), "z": lax.rem(z - 1 + nz, nz),
    }
    score_scale = dim ** (-0.5)

    x_in = pltpu.make_async_copy(x_ref, x_all.at[pl.ds(0, tokens)], local_sem.at[0])
    cot_in = pltpu.make_async_copy(cot_ref, cot, local_sem.at[1])
    w_in = [
        pltpu.make_async_copy(w.at[:, pl.ds(h * dim, dim)], w_all.at[at * heads + h], local_sem.at[2 + at * heads + h])
        for at, w in enumerate((wk_ref, wv_ref, wq_ref)) for h in range(heads)
    ]
    x_in.start()
    for copy in w_in[:heads]:
        copy.start()
    cot_in.start()

    barrier = pltpu.get_barrier_semaphore()
    partners = [other, after, ahead_of]
    partners += [{"z": lax.rem(z + j, nz)} for j in range(1, nz)]
    partners += [{"y": lax.rem(y + j, ny)} for j in range(1, ny)]
    for device in partners:
        pl.semaphore_signal(barrier, inc=1, device_id=device, device_id_type=MESH)

    def project(at):
        for h in range(heads):
            w_in[at * heads + h].wait()
        def body(h, carry):
            c = at * heads + h
            kvq[c] = dot_nn(x_all[pl.ds(0, tokens), :], w_all[c]).astype(jnp.bfloat16)
            return carry
        lax.fori_loop(0, heads, body, 0)

    def halo_copy(src, dst, slot, device):
        return pltpu.make_async_remote_copy(
            src_ref=src, dst_ref=dst, send_sem=halo_sem.at[0, slot], recv_sem=halo_sem.at[1, slot],
            device_id=device, device_id_type=MESH,
        )

    key_out = [halo_copy(kvq.at[h], prev.at[h], h, after) for h in range(heads)]
    value_out = [halo_copy(kvq.at[heads + h], prev.at[heads + h], heads + h, after) for h in range(heads)]
    local_out = [
        halo_copy(grad_local.at[h], after_in.at[heads + h], 2 * heads + h, ahead_of) for h in range(heads)
    ]
    query_out = halo_copy(kvq.at[pl.ds(2 * heads, heads)], after_in.at[pl.ds(0, heads)], 3 * heads, ahead_of)
    stats_out = [halo_copy(stats.at[h], stats_in.at[h], 3 * heads + 1 + h, ahead_of) for h in range(heads)]

    def pair_copy(src, dst, slot):
        return pltpu.make_async_remote_copy(
            src_ref=src, dst_ref=dst, send_sem=pair_sem.at[0, slot], recv_sem=pair_sem.at[1, slot],
            device_id=other, device_id_type=MESH,
        )

    def each_head(body):
        def step(h, carry):
            body(h)
            return carry
        lax.fori_loop(0, heads, step, 0)

    def columns(h):
        return pl.ds(pl.multiple_of(h * dim, dim), dim)

    norm_scan = VectorScan(False, n1_own, n1_got, n1_yown, n1_ygot, nz_sem.at[0], ny_sem.at[0])
    grad_norm_scan = VectorScan(True, n2_own, n2_got, n2_yown, n2_ygot, nz_sem.at[1], ny_sem.at[1])
    memory_scan = MemoryScan(
        False, m1_parts, m1_got, m1_inside, m1_yown, m1_ygot, m1_back, m1_full,
        mz_sem.at[0], my_sem.at[0], mb_sem.at[0],
    )
    grad_memory_scan = MemoryScan(
        True, m2_parts, m2_got, m2_inside, m2_yown, m2_ygot, m2_back, m2_full,
        mz_sem.at[1], my_sem.at[1], mb_sem.at[1],
    )
    parts = nz // heads

    def put_parts(target, h, value):
        target[pl.ds(h * parts, parts)] = value.astype(jnp.bfloat16).reshape(parts, dim // parts, dim)

    def mixing_of(h):
        return 1.0 / (1.0 + jnp.exp(-jnp.full((1, dim), gate_ref[h], jnp.float32)))

    x_in.wait()
    for copy in w_in[heads:]:
        copy.start()
    project(0)

    def key_sums(h):
        n1_own[h] = jnp.sum(feature(kvq[h].astype(jnp.float32)), axis=0, keepdims=True)

    each_head(key_sums)
    cot_in.wait()

    def local_gradient(h):
        upstream = cot[:, columns(h)].astype(jnp.float32)
        grad_local[h] = ((1.0 - mixing_of(h)) * upstream).astype(jnp.bfloat16)

    each_head(local_gradient)
    pl.semaphore_wait(barrier, len(partners))
    norm_scan.start()
    key_out[0].start()
    local_out[0].start()
    x_out = pair_copy(x_all.at[pl.ds(0, tokens)], x_all.at[pl.ds(tokens, tokens)], 0)
    x_out.start()
    project(1)

    def write(h):
        phi = feature(kvq[h].astype(jnp.float32)).astype(jnp.bfloat16)
        put_parts(m1_parts, h, dot_tn(phi, kvq[heads + h]))

    each_head(write)
    memory_scan.start()
    project(2)
    norm_scan.across_rows()

    def own_part(h):
        row = lax.broadcasted_iota(jnp.int32, (tokens, tokens), 0)
        col = lax.broadcasted_iota(jnp.int32, (tokens, tokens), 1)
        scores[h] = jnp.where(col <= row, dot_nt(kvq[2 * heads + h], kvq[h]) * score_scale, MASKED)
        soft_grads[h] = dot_nt(grad_local[h], kvq[heads + h])

    each_head(own_part)
    norms[0] = norm_scan.result()

    def memory_gradient(h):
        phi = feature(kvq[2 * heads + h].astype(jnp.float32))
        divisor = jnp.sum(phi * norms[0, h], axis=1, keepdims=True) + 1.0
        den[h] = divisor
        grad_ret = mixing_of(h) * cot[:, columns(h)].astype(jnp.float32)
        number = (grad_ret / divisor).astype(jnp.bfloat16)
        grad_num[h] = number
        put_parts(m2_parts, h, dot_tn(phi.astype(jnp.bfloat16), number))

    each_head(memory_gradient)
    grad_memory_scan.start()
    for h in range(1, heads):
        key_out[h].start()
        local_out[h].start()
    memory_scan.across_rows()
    memory_scan.give_back()
    for copy in value_out:
        copy.start()
    query_out.start()
    grad_memory_scan.across_rows()

    x_out.wait_recv()
    tile = min(wide, 256)

    def turn(i, carry):
        at = pl.ds(pl.multiple_of(i * tile, 128), tile)
        x_turned[at, :] = x_all[:, at].T
        return carry

    lax.fori_loop(0, x_all.shape[1] // tile, turn, 0)
    memory_scan.finish()

    def retrieve(h):
        mixing = mixing_of(h)
        query = kvq[2 * heads + h].astype(jnp.float32)
        phi = feature(query)
        memory = memory_scan.head(h, heads)
        retrieved = dot_nn(phi.astype(jnp.bfloat16), memory) / den[h]
        ret_mix[h] = mixing * retrieved
        grad_ret = mixing * cot[:, columns(h)].astype(jnp.float32)
        grad_den = -jnp.sum(grad_ret * retrieved, axis=1, keepdims=True) / den[h]
        n2_own[h] = jnp.sum(grad_den * phi, axis=0, keepdims=True)
        grad_phi = dot_nt(grad_num[h], memory) + grad_den * norms[0, h]
        dq_ret[h] = grad_phi * feature_slope(query)

    each_head(retrieve)
    grad_norm_scan.start()

    segment, last = y * nz + z, ny * nz - 1
    bias = jnp.where(segment > 0, 0.0, MASKED)
    bias_after = jnp.where(segment < last, 0.0, MASKED)

    def as_row(column):
        return jnp.broadcast_to(column, (tokens, 128)).T[:1]

    def attend(h):
        query, key, value = kvq[2 * heads + h], kvq[h], kvq[heads + h]
        key_prev, value_prev, local = prev[h], prev[heads + h], grad_local[h]
        s_own = scores[h]
        s_prev = dot_nt(query, key_prev) * score_scale + bias
        top = jnp.maximum(jnp.max(s_own, axis=1, keepdims=True), jnp.max(s_prev, axis=1, keepdims=True))
        e_own, e_prev = jnp.exp(s_own - top), jnp.exp(s_prev - top)
        inverse = 1.0 / (jnp.sum(e_own, axis=1, keepdims=True) + jnp.sum(e_prev, axis=1, keepdims=True))
        p_own, p_prev = e_own * inverse, e_prev * inverse
        b_own, b_prev = p_own.astype(jnp.bfloat16), p_prev.astype(jnp.bfloat16)
        near = dot_nn(b_own, value) + dot_nn(b_prev, value_prev)
        blended[:, columns(h)] = (ret_mix[h] + (1.0 - mixing_of(h)) * near).astype(jnp.bfloat16)
        g_own, g_prev = soft_grads[h], dot_nt(local, value_prev)
        row_dot = jnp.sum(p_own * g_own, axis=1, keepdims=True) + jnp.sum(p_prev * g_prev, axis=1, keepdims=True)
        stats[h, 0:1] = as_row(top)
        stats[h, 1:2] = as_row(inverse)
        stats[h, 2:3] = as_row(row_dot)
        d_own = (p_own * (g_own - row_dot) * score_scale).astype(jnp.bfloat16)
        d_prev = (p_prev * (g_prev - row_dot) * score_scale).astype(jnp.bfloat16)
        own_grads[h] = dot_tn(d_own, query)
        own_grads[heads + h] = dot_tn(b_own, local)
        dq_att = dot_nn(d_own, key) + dot_nn(d_prev, key_prev)
        grads[0, h] = (dq_att + dq_ret[h]).astype(jnp.bfloat16)

    for h in range(heads):
        stats[h] = jnp.zeros(stats.shape[1:], jnp.float32)
    for h in range(heads):
        key_out[h].wait_recv()
        value_out[h].wait_recv()
        attend(h)
        stats_out[h].start()
        if h == 0:
            grad_memory_scan.give_back()
    blended_out = pltpu.make_async_copy(blended, blended_ref, out_sem.at[6])
    blended_out.start()

    def pair_grads(m):
        return pair_copy(grads.at[m, 1 - dp], g_all.at[m, pl.ds(tokens, tokens)], 1 + m)

    def keep_grads(m):
        g_all[m, pl.ds(0, tokens), :] = grads[m, dp]

    def products(m, target):
        at = pl.multiple_of(target * wide, 128)
        dw[m, target] = dot_nn(x_turned[pl.ds(at, wide), :], g_all[m])

    part = dim // 2

    def z_first(m, left, right):
        return lambda target, sub: dw[m, :, pl.ds(pl.multiple_of(target * block + sub * rows, 8), rows), left:right]

    def y_first(m, left, right):
        return lambda target, sub: dw[m, target, sub * (wide // 2):(sub + 1) * (wide // 2), left:right]

    def y_second(held):
        return lambda target, sub: held[sub, target]

    def z_second(held):
        return lambda target, sub: held[pl.ds(pl.multiple_of(target * block + sub * rows, 8), rows), :]

    def ring(axis, slot, mine, send, recv):
        sem = (ring_z_sem if axis == "z" else ring_y_sem).at[slot]
        return RingSum(axis, mine, send, recv, sem.at[0], sem.at[1])

    a1 = ring("z", 0, z_first(1, 0, dim), a1_send, a1_recv)
    b1 = ring("y", 0, y_first(2, 0, dim), b1_send, b1_recv)
    c1 = ring("z", 1, z_first(0, 0, part), c1_send, c1_recv)
    d1 = ring("y", 1, y_first(0, part, dim), d1_send, d1_recv)
    a2 = ring("y", 2, y_second(a_sum), a2_send, a2_recv)
    b2 = ring("z", 2, z_second(b_sum), b2_send, b2_recv)
    c2 = ring("y", 3, y_second(c_sum), c2_send, c2_recv)
    d2 = ring("z", 3, z_second(d_sum), d2_send, d2_recv)

    def columns_in(sums, held):
        for sub in (0, 1):
            held[sub] = sums.total(sub)

    def multiply(m, first):
        products(m, lax.rem(y + ny // 2, ny))
        first.step(0, ny // 2)
        for ahead in range(1, ny):
            products(m, lax.rem(y + ny // 2 + ahead, ny))
        for ahead in range(1, ny):
            first.step(0, ny // 2 + ahead)

    def rows_in(sums, held):
        for sub in (0, 1):
            held[sub * (wide // 2):(sub + 1) * (wide // 2), :] = sums.total(sub)

    query_pair = pair_grads(0)
    query_pair.start()
    keep_grads(0)
    grad_norm_scan.across_rows()

    def serve(h):
        query, local = after_in[h], after_in[heads + h]
        top, inverse, row_dot = stats_in[h, 0:1], stats_in[h, 1:2], stats_in[h, 2:3]
        soft = jnp.exp(dot_nt(kvq[h], query) * score_scale + bias_after - top) * inverse
        given = (soft * (dot_nt(kvq[heads + h], local) - row_dot) * score_scale).astype(jnp.bfloat16)
        own_grads[h] += dot_nn(given, query)
        own_grads[heads + h] += dot_nn(soft.astype(jnp.bfloat16), local)

    query_out.wait_recv()
    for h in range(heads):
        if h == heads - 1:
            query_pair.wait_recv()
            multiply(0, d1)
            c1.step(0)
        local_out[h].wait_recv()
        stats_out[h].wait_recv()
        serve(h)
    norms[1] = grad_norm_scan.result()
    grad_memory_scan.finish()

    def write_back(h):
        key = kvq[h].astype(jnp.float32)
        grad_memory = grad_memory_scan.head(h, heads)
        grad_phi = dot_nt(kvq[heads + h], grad_memory) + norms[1, h]
        grads[1, h] = (own_grads[h] + grad_phi * feature_slope(key)).astype(jnp.bfloat16)
        grad_value = dot_nn(feature(key).astype(jnp.bfloat16), grad_memory)
        grads[2, h] = (own_grads[heads + h] + grad_value).astype(jnp.bfloat16)

    write_back(1 - dp)
    key_pair, value_pair = pair_grads(1), pair_grads(2)
    key_pair.start()
    value_pair.start()
    write_back(dp)
    keep_grads(1)
    keep_grads(2)
    key_pair.wait_recv()
    for k in range(ny):
        products(1, k)
    c1.step(1)
    a1.step(0)
    d1.step(1)
    value_pair.wait_recv()
    multiply(2, b1)
    c1.step(2)
    rows_in(d1, d_sum)
    d2.step(0)
    a1.step(1)
    c1.step(3)
    b1.step(1)
    d2.step(1)
    a1.step(2)
    columns_in(c1, c_sum)
    c2.step(0)
    d2.step(2)
    a1.step(3)
    d2.step(3)
    rows_in(b1, b_sum)
    b2.step(0)
    c2.step(1)
    columns_in(a1, a_sum)
    a2.step(0)
    b2.step(1)
    a2.step(1)
    for t in range(2, nz // 2):
        b2.step(t)
    places = ((c2, 0, part), (d2, part, dim), (a2, dim, 2 * dim), (b2, 2 * dim, 3 * dim))
    for sums, left, right in places:
        for sub in (0, 1):
            fin[sub, :, left:right] = sums.total(sub) * scale
    swap_out = pair_copy(fin.at[1 - dp], swap, 4)
    swap_out.start()

    def put(src, m, place, slot):
        return pltpu.make_async_copy(
            src.at[:, pl.ds(m * dim, dim)], out_ref.at[m, :, columns(place)], out_sem.at[slot]
        )

    own_out = [put(fin.at[dp], m, dp, m) for m in range(3)]
    other_out = [put(swap, m, 1 - dp, 3 + m) for m in range(3)]
    for copy in own_out:
        copy.start()
    for sent in (
        a1, b1, c1, d1, a2, b2, c2, d2, norm_scan, grad_norm_scan, memory_scan, grad_memory_scan,
    ):
        sent.drain()
    for copy in (*key_out, *value_out, *local_out, query_out, *stats_out, x_out, query_pair, key_pair, value_pair):
        copy.wait_send()
    swap_out.wait_recv()
    for copy in other_out:
        copy.start()
    swap_out.wait_send()
    for copy in (*own_out, *other_out, blended_out):
        copy.wait()


def layer(x, wq, wk, wv, gate, cot, scale):
    tokens, depth = x.shape
    heads = gate.shape[0]
    dim = wq.shape[1] // heads
    ny, nz = lax.axis_size("y"), lax.axis_size("z")
    wide = depth // ny
    rows = wide // nz // 2
    zs, ys = 2 * (nz - 1), 2 * (ny - 1)
    wire = lambda *shape: pltpu.VMEM(shape, jnp.bfloat16)
    real = lambda *shape: pltpu.VMEM(shape, jnp.float32)
    dma = lambda *shape: pltpu.SemaphoreType.DMA(shape)
    a1, b1 = (zs, ny, rows), (ys, wide // 2)
    part = (heads * dim // nz, dim)
    vectors = [real(heads, 1, dim), real(nz, heads, 1, dim), real(heads, 1, dim), real(ny, heads, 1, dim)]
    scan = [
        wire(nz, *part), wire(nz, *part), real(nz, *part), real(*part), real(ny, *part), wire(nz, *part),
        wire(nz, *part),
    ]
    pair = (2 * heads, tokens, dim)
    anywhere = pl.BlockSpec(memory_space=pl.ANY)
    return pl.pallas_call(
        functools.partial(layer_kernel, scale),
        out_shape=(
            jax.ShapeDtypeStruct((tokens, heads * dim), jnp.bfloat16),
            jax.ShapeDtypeStruct((3, rows, heads * dim), jnp.float32),
        ),
        in_specs=[anywhere] * 4 + [pl.BlockSpec(memory_space=pltpu.SMEM), anywhere],
        out_specs=(anywhere,) * 2,
        scratch_shapes=[
            wire(2 * tokens, depth), wire(depth, 2 * tokens), wire(3 * heads, depth, dim), wire(tokens, heads * dim), wire(tokens, heads * dim),
            wire(3 * heads, tokens, dim), wire(*pair), wire(*pair), real(*pair),
            real(heads, tokens, dim), real(heads, tokens, dim),
            real(heads, tokens, tokens), real(heads, tokens, tokens), wire(heads, tokens, dim),
            wire(heads, tokens, dim), real(heads, tokens, 1), real(heads, 8, tokens), real(heads, 8, tokens),
            wire(3, heads, tokens, dim), wire(3, 2 * tokens, dim),
            *vectors, *vectors, real(2, heads, 1, dim), *scan, *scan,
            real(3, ny, wide, dim), real(2, ny, rows, dim), real(wide, dim), real(2, ny, rows, dim // 2), real(wide, dim // 2),
            real(2, rows, 3 * dim), real(rows, 3 * dim),
            wire(*a1, dim), wire(*a1, dim), wire(*b1, dim), wire(*b1, dim),
            wire(*a1, dim // 2), wire(*a1, dim // 2), wire(*b1, dim // 2), wire(*b1, dim // 2),
            wire(ys, rows, dim), wire(ys, rows, dim), wire(zs, rows, dim), wire(zs, rows, dim),
            wire(ys, rows, dim // 2), wire(ys, rows, dim // 2), wire(zs, rows, dim // 2), wire(zs, rows, dim // 2),
            dma(2 + 3 * heads), dma(2, 4 * heads + 1), dma(2, 5), dma(2, 2, nz), dma(2, 2, ny),
            dma(2, 2, nz), dma(2, 2, ny), dma(2, 2, nz),
            dma(4, 2, zs), dma(4, 2, ys), dma(7),
        ],
        compiler_params=pltpu.CompilerParams(
            collective_id=1, has_side_effects=True, vmem_limit_bytes=63 * 1024 * 1024
        ),
    )(x, wq, wk, wv, gate, cot)


def hand_on_kernel(a_ref, b_ref, a_out, b_out, a_held, b_held, sem):
    steps = [
        (pltpu.make_async_copy(src, held, sem.at[0, i]), pltpu.make_async_copy(held, dst, sem.at[1, i]))
        for i, (src, held, dst) in enumerate(((a_ref, a_held, a_out), (b_ref, b_held, b_out)))
    ]
    for first, _ in steps:
        first.start()
    for first, second in steps:
        first.wait()
        second.start()
    for _, second in steps:
        second.wait()


def hand_on(a, b):
    anywhere = pl.BlockSpec(memory_space=pl.ANY)
    return pl.pallas_call(
        hand_on_kernel,
        out_shape=tuple(jax.ShapeDtypeStruct(v.shape, v.dtype) for v in (a, b)),
        in_specs=[anywhere] * 2,
        out_specs=(anywhere,) * 2,
        scratch_shapes=[pltpu.VMEM(v.shape, v.dtype) for v in (a, b)] + [pltpu.SemaphoreType.DMA((2, 2))],
    )(a, b)


def local(inputs, w_query, w_key, w_value, gate_bias, cotangent):
    tokens = inputs[0]
    seg_len = tokens.shape[0]
    scale = 1.0 / math.sqrt(lax.axis_size(SEQ) * lax.axis_size("dp") * seg_len)
    blended, grad_weights = layer(tokens, w_query, w_key, w_value, gate_bias, cotangent[0], scale)
    blended, grad_weights = hand_on(blended, grad_weights)
    return (blended[None], grad_weights.transpose(1, 0, 2))


def solution(mesh):
    finer = Mesh(
        mesh.devices.reshape(4, 8, mesh.shape["dp"], mesh.shape["head"]),
        ("y", "z", "dp", "head"),
    )
    placed = (
        P("dp", SEQ, None),
        P(None, "head"),
        P(None, "head"),
        P(None, "head"),
        P("head"),
        P("dp", SEQ, "head"),
    )
    return jax.shard_map(
        local,
        mesh=finer,
        in_specs=placed,
        out_specs=(P("dp", SEQ, "head"), P(SEQ_DP, None, "head")),
        check_vma=False,
    )
```

```python
import functools
import math

import jax
import jax.numpy as jnp
from jax import lax
from jax.experimental import pallas as pl
from jax.experimental.pallas import tpu as pltpu
from jax.sharding import Mesh
from jax.sharding import PartitionSpec as P

SEQ = ("y", "z")
SEQ_DP = ("y", "z", "dp")
MESH = pl.DeviceIdType.MESH
MASKED = -1e30


def feature(u):
    return jnp.where(u > 0, u + 1.0, jnp.exp(jnp.minimum(u, 0.0)))


def feature_slope(u):
    return jnp.where(u > 0, 1.0, jnp.exp(jnp.minimum(u, 0.0)))


def contract(a, b, over_a, over_b):
    return lax.dot_general(
        a, b, (((over_a,), (over_b,)), ((), ())), preferred_element_type=jnp.float32
    )


def dot_nn(a, b):
    return contract(a, b, 1, 0)


def dot_nt(a, b):
    return contract(a, b, 1, 1)


def dot_tn(a, b):
    return contract(a, b, 0, 0)


def ring_chains(n):
    chains, first = [], 0
    for sub in (0, 1):
        for way in (1, -1):
            length = n // 2 if (way > 0) == (sub == 0) else n - 1 - n // 2
            chains.append((sub, way, length, first))
            first += length
    return chains


class RingSum:
    def __init__(self, axis, mine, send, recv, send_sem, recv_sem):
        self.axis, self.mine = axis, mine
        self.n, self.position = lax.axis_size(axis), lax.axis_index(axis)
        self.send, self.recv, self.send_sem, self.recv_sem = send, recv, send_sem, recv_sem
        self.chains = ring_chains(self.n)

    def copy(self, slot, way):
        return pltpu.make_async_remote_copy(
            src_ref=self.send.at[slot],
            dst_ref=self.recv.at[slot],
            send_sem=self.send_sem,
            recv_sem=self.recv_sem.at[slot],
            device_id={self.axis: lax.rem(self.position + way + self.n, self.n)},
            device_id_type=MESH,
        )

    def step(self, t, ahead=None):
        for sub, way, length, first in self.chains:
            if t >= length:
                continue
            if ahead is not None and (way * (length - t)) % self.n != ahead % self.n:
                continue
            target = lax.rem(self.position + way * (length - t) + self.n, self.n)
            value = self.mine(target, sub)
            if t:
                self.copy(first + t - 1, way).wait_recv()
                value = value + self.recv[first + t - 1].astype(jnp.float32)
            self.send[first + t] = value.astype(jnp.bfloat16)
            self.copy(first + t, way).start()

    def total(self, sub):
        value = self.mine(self.position, sub)
        for chain_sub, way, length, first in self.chains:
            if chain_sub == sub and length:
                self.copy(first + length - 1, way).wait_recv()
                value = value + self.recv[first + length - 1].astype(jnp.float32)
        return value

    def drain(self):
        self.all_copy().wait_send()

    def all_copy(self):
        return pltpu.make_async_remote_copy(
            src_ref=self.send, dst_ref=self.recv, send_sem=self.send_sem, recv_sem=self.recv_sem.at[0],
            device_id={self.axis: self.position}, device_id_type=MESH,
        )


class Spread:
    def __init__(self, axis, got, sem):
        self.axis, self.got, self.sem = axis, got, sem
        self.n, self.position = lax.axis_size(axis), lax.axis_index(axis)

    def copy(self, src, j):
        return pltpu.make_async_remote_copy(
            src_ref=src,
            dst_ref=self.got.at[j],
            send_sem=self.sem.at[0],
            recv_sem=self.sem.at[1],
            device_id={self.axis: lax.rem(self.position + j, self.n)},
            device_id_type=MESH,
        )

    def all_copy(self):
        others = self.got.at[pl.ds(1, self.n - 1)]
        return pltpu.make_async_remote_copy(
            src_ref=others, dst_ref=others, send_sem=self.sem.at[0], recv_sem=self.sem.at[1],
            device_id={self.axis: self.position}, device_id_type=MESH,
        )

    def start(self, src):
        for j in range(1, self.n):
            self.copy(src, j).start()

    def sums(self, own, reverse):
        passed, total = jnp.zeros_like(own), own
        self.all_copy().wait_recv()
        for j in range(1, self.n):
            value = self.got[j]
            earlier = self.position < j if reverse else self.position >= j
            passed = passed + value * jnp.where(earlier, 1.0, 0.0)
            total = total + value
        return passed, total

    def drain(self):
        self.all_copy().wait_send()


class VectorScan:
    def __init__(self, reverse, own, z_got, y_own, y_got, z_sem, y_sem):
        self.reverse, self.own, self.y_own = reverse, own, y_own
        self.z, self.y = Spread("z", z_got, z_sem), Spread("y", y_got, y_sem)

    def start(self):
        self.z.start(self.own)

    def across_rows(self):
        self.inside, total = self.z.sums(self.own[...], self.reverse)
        self.y_own[...] = total
        self.y.start(self.y_own)

    def result(self):
        passed, _ = self.y.sums(self.y_own[...], self.reverse)
        return passed + self.inside

    def drain(self):
        self.z.drain()
        self.y.drain()


class MemoryScan:
    def __init__(self, reverse, parts, got, inside, y_own, y_got, back, result, z_sem, y_sem, back_sem):
        self.reverse, self.parts, self.got, self.inside, self.y_own = reverse, parts, got, inside, y_own
        self.back, self.full, self.z_sem, self.back_sem = back, result, z_sem, back_sem
        self.n, self.position = lax.axis_size("z"), lax.axis_index("z")
        self.y = Spread("y", y_got, y_sem)

    def out_copy(self, j):
        target = lax.rem(self.position + j, self.n)
        return pltpu.make_async_remote_copy(
            src_ref=self.parts.at[target],
            dst_ref=self.got.at[j],
            send_sem=self.z_sem.at[0],
            recv_sem=self.z_sem.at[1],
            device_id={"z": target},
            device_id_type=MESH,
        )

    def back_copy(self, j):
        target = lax.rem(self.position + j, self.n)
        return pltpu.make_async_remote_copy(
            src_ref=self.back.at[target],
            dst_ref=self.full.at[self.position],
            send_sem=self.back_sem.at[0],
            recv_sem=self.back_sem.at[1],
            device_id={"z": target},
            device_id_type=MESH,
        )

    def start(self):
        for j in range(1, self.n):
            self.out_copy(j).start()

    def across_rows(self):
        self.all_copy(self.z_sem).wait_recv()
        self.got[0] = self.parts[self.position]
        run = jnp.zeros(self.y_own.shape, jnp.float32)
        for k in reversed(range(self.n)) if self.reverse else range(self.n):
            self.inside[k] = run
            run = run + self.got[lax.rem(self.position - k + self.n, self.n)].astype(jnp.float32)
        self.y_own[...] = run
        self.y.start(self.y_own)

    def give_back(self):
        passed, _ = self.y.sums(self.y_own[...], self.reverse)
        for k in range(self.n):
            self.back[k] = (self.inside[k] + passed).astype(jnp.bfloat16)
        for j in range(1, self.n):
            self.back_copy(j).start()
        self.full[self.position] = self.back[self.position]

    def finish(self):
        self.all_copy(self.back_sem).wait_recv()

    def head(self, h, heads):
        parts = self.n // heads
        block = self.full[pl.ds(h * parts, parts)]
        return block.reshape(parts * block.shape[1], block.shape[2])

    def drain(self):
        self.y.drain()
        self.all_copy(self.z_sem).wait_send()
        self.all_copy(self.back_sem).wait_send()

    def all_copy(self, sem):
        others = self.got.at[pl.ds(1, self.n - 1)]
        return pltpu.make_async_remote_copy(
            src_ref=others, dst_ref=others, send_sem=sem.at[0], recv_sem=sem.at[1],
            device_id={"z": self.position}, device_id_type=MESH,
        )


def layer_kernel(
    scale, x_ref, wq_ref, wk_ref, wv_ref, gate_ref, cot_ref, blended_ref, out_ref,
    x_all, x_turned, w_all, cot, blended, kvq, prev, after_in, own_grads, dq_ret, ret_mix,
    scores, soft_grads, grad_local, grad_num, den, stats, stats_in, grads, g_all,
    n1_own, n1_got, n1_yown, n1_ygot, n2_own, n2_got, n2_yown, n2_ygot, norms,
    m1_parts, m1_got, m1_inside, m1_yown, m1_ygot, m1_back, m1_full,
    m2_parts, m2_got, m2_inside, m2_yown, m2_ygot, m2_back, m2_full,
    dw, a_sum, b_sum, c_sum, d_sum, fin, swap,
    a1_send, a1_recv, b1_send, b1_recv, c1_send, c1_recv, d1_send, d1_recv,
    a2_send, a2_recv, b2_send, b2_recv, c2_send, c2_recv, d2_send, d2_recv,
    local_sem, halo_sem, pair_sem, nz_sem, ny_sem, mz_sem, my_sem, mb_sem, ring_z_sem, ring_y_sem, ring_send_sem, out_sem,
):
    ny, nz = lax.axis_size("y"), lax.axis_size("z")
    y, z, dp = lax.axis_index("y"), lax.axis_index("z"), lax.axis_index("dp")
    other = {"dp": 1 - dp}
    tokens = x_ref.shape[0]
    heads, dim = kvq.shape[0] // 3, kvq.shape[2]
    wide = dw.shape[2]
    block = wide // nz
    rows = block // 2
    up, down = z == nz - 1, z == 0
    after = {
        "y": lax.rem(y + jnp.where(up, 1, 0), ny), "z": lax.rem(z + 1, nz),
    }
    ahead_of = {
        "y": lax.rem(y - jnp.where(down, 1, 0) + ny, ny), "z": lax.rem(z - 1 + nz, nz),
    }
    score_scale = dim ** (-0.5)

    x_in = pltpu.make_async_copy(x_ref, x_all.at[pl.ds(0, tokens)], local_sem.at[0])
    cot_in = pltpu.make_async_copy(cot_ref, cot, local_sem.at[1])
    w_in = [
        pltpu.make_async_copy(w.at[:, pl.ds(h * dim, dim)], w_all.at[at * heads + h], local_sem.at[2 + at * heads + h])
        for at, w in enumerate((wk_ref, wv_ref, wq_ref)) for h in range(heads)
    ]
    x_in.start()
    w_in[0].start()
    cot_in.start()

    barrier = pltpu.get_barrier_semaphore()
    partners = [other, after, ahead_of]
    partners += [{"z": lax.rem(z + j, nz)} for j in range(1, nz)]
    partners += [{"y": lax.rem(y + j, ny)} for j in range(1, ny)]
    for device in partners:
        pl.semaphore_signal(barrier, inc=1, device_id=device, device_id_type=MESH)

    def project(first, last):
        for c in range(first, last):
            w_in[c].wait()
        def body(c, carry):
            kvq[c] = dot_nn(x_all[pl.ds(0, tokens), :], w_all[c]).astype(jnp.bfloat16)
            return carry
        lax.fori_loop(first, last, body, 0)

    def halo_copy(src, dst, slot, device):
        return pltpu.make_async_remote_copy(
            src_ref=src, dst_ref=dst, send_sem=halo_sem.at[0, slot], recv_sem=halo_sem.at[1, slot],
            device_id=device, device_id_type=MESH,
        )

    key_out = [halo_copy(kvq.at[h], prev.at[h], h, after) for h in range(heads)]
    value_out = [halo_copy(kvq.at[heads + h], prev.at[heads + h], heads + h, after) for h in range(heads)]
    local_out = [
        halo_copy(grad_local.at[h], after_in.at[heads + h], 2 * heads + h, ahead_of) for h in range(heads)
    ]
    query_out = halo_copy(kvq.at[pl.ds(2 * heads, heads)], after_in.at[pl.ds(0, heads)], 3 * heads, ahead_of)
    stats_out = [halo_copy(stats.at[h], stats_in.at[h], 3 * heads + 1 + h, ahead_of) for h in range(heads)]

    def pair_copy(src, dst, slot):
        return pltpu.make_async_remote_copy(
            src_ref=src, dst_ref=dst, send_sem=pair_sem.at[0, slot], recv_sem=pair_sem.at[1, slot],
            device_id=other, device_id_type=MESH,
        )

    def each_head(body):
        def step(h, carry):
            body(h)
            return carry
        lax.fori_loop(0, heads, step, 0)

    def columns(h):
        return pl.ds(pl.multiple_of(h * dim, dim), dim)

    norm_scan = VectorScan(False, n1_own, n1_got, n1_yown, n1_ygot, nz_sem.at[0], ny_sem.at[0])
    grad_norm_scan = VectorScan(True, n2_own, n2_got, n2_yown, n2_ygot, nz_sem.at[1], ny_sem.at[1])
    memory_scan = MemoryScan(
        False, m1_parts, m1_got, m1_inside, m1_yown, m1_ygot, m1_back, m1_full,
        mz_sem.at[0], my_sem.at[0], mb_sem.at[0],
    )
    grad_memory_scan = MemoryScan(
        True, m2_parts, m2_got, m2_inside, m2_yown, m2_ygot, m2_back, m2_full,
        mz_sem.at[1], my_sem.at[1], mb_sem.at[1],
    )
    parts = nz // heads

    def put_parts(target, h, value):
        target[pl.ds(h * parts, parts)] = value.astype(jnp.bfloat16).reshape(parts, dim // parts, dim)

    def mixing_of(h):
        return 1.0 / (1.0 + jnp.exp(-jnp.full((1, dim), gate_ref[h], jnp.float32)))

    x_in.wait()
    for copy in w_in[1:]:
        copy.start()
    cot_in.wait()

    def local_gradient(h):
        upstream = cot[:, columns(h)].astype(jnp.float32)
        grad_local[h] = ((1.0 - mixing_of(h)) * upstream).astype(jnp.bfloat16)

    each_head(local_gradient)
    project(0, 1)
    pl.semaphore_wait(barrier, len(partners))
    key_out[0].start()
    local_out[0].start()
    project(1, heads)

    def key_sums(h):
        n1_own[h] = jnp.sum(feature(kvq[h].astype(jnp.float32)), axis=0, keepdims=True)

    each_head(key_sums)
    norm_scan.start()
    x_out = pair_copy(x_all.at[pl.ds(0, tokens)], x_all.at[pl.ds(tokens, tokens)], 0)
    x_out.start()
    project(heads, 2 * heads)

    def write(h):
        phi = feature(kvq[h].astype(jnp.float32)).astype(jnp.bfloat16)
        put_parts(m1_parts, h, dot_tn(phi, kvq[heads + h]))

    each_head(write)
    memory_scan.start()
    for h in range(1, heads):
        key_out[h].start()
        local_out[h].start()
    project(2 * heads, 3 * heads)
    norm_scan.across_rows()

    def own_part(h):
        row = lax.broadcasted_iota(jnp.int32, (tokens, tokens), 0)
        col = lax.broadcasted_iota(jnp.int32, (tokens, tokens), 1)
        scores[h] = jnp.where(col <= row, dot_nt(kvq[2 * heads + h], kvq[h]) * score_scale, MASKED)
        soft_grads[h] = dot_nt(grad_local[h], kvq[heads + h])

    each_head(own_part)
    norms[0] = norm_scan.result()

    def memory_gradient(h):
        phi = feature(kvq[2 * heads + h].astype(jnp.float32))
        divisor = jnp.sum(phi * norms[0, h], axis=1, keepdims=True) + 1.0
        den[h] = divisor
        grad_ret = mixing_of(h) * cot[:, columns(h)].astype(jnp.float32)
        number = (grad_ret / divisor).astype(jnp.bfloat16)
        grad_num[h] = number
        put_parts(m2_parts, h, dot_tn(phi.astype(jnp.bfloat16), number))

    each_head(memory_gradient)
    grad_memory_scan.start()
    memory_scan.across_rows()
    memory_scan.give_back()
    for copy in value_out:
        copy.start()
    query_out.start()

    x_out.wait_recv()
    tile = min(wide, 256)

    def turn(i, carry):
        at = pl.ds(pl.multiple_of(i * tile, 128), tile)
        x_turned[at, :] = x_all[:, at].T
        return carry

    lax.fori_loop(0, x_all.shape[1] // tile, turn, 0)
    grad_memory_scan.across_rows()
    memory_scan.finish()

    def retrieve(h):
        mixing = mixing_of(h)
        query = kvq[2 * heads + h].astype(jnp.float32)
        phi = feature(query)
        memory = memory_scan.head(h, heads)
        retrieved = dot_nn(phi.astype(jnp.bfloat16), memory) / den[h]
        ret_mix[h] = mixing * retrieved
        grad_ret = mixing * cot[:, columns(h)].astype(jnp.float32)
        grad_den = -jnp.sum(grad_ret * retrieved, axis=1, keepdims=True) / den[h]
        n2_own[h] = jnp.sum(grad_den * phi, axis=0, keepdims=True)
        grad_phi = dot_nt(grad_num[h], memory) + grad_den * norms[0, h]
        dq_ret[h] = grad_phi * feature_slope(query)

    each_head(retrieve)
    grad_norm_scan.start()

    segment, last = y * nz + z, ny * nz - 1
    bias = jnp.where(segment > 0, 0.0, MASKED)
    bias_after = jnp.where(segment < last, 0.0, MASKED)

    def as_row(column):
        return jnp.broadcast_to(column, (tokens, 128)).T[:1]

    def attend(h):
        query, key, value = kvq[2 * heads + h], kvq[h], kvq[heads + h]
        key_prev, value_prev, local = prev[h], prev[heads + h], grad_local[h]
        s_own = scores[h]
        s_prev = dot_nt(query, key_prev) * score_scale + bias
        top = jnp.maximum(jnp.max(s_own, axis=1, keepdims=True), jnp.max(s_prev, axis=1, keepdims=True))
        e_own, e_prev = jnp.exp(s_own - top), jnp.exp(s_prev - top)
        inverse = 1.0 / (jnp.sum(e_own, axis=1, keepdims=True) + jnp.sum(e_prev, axis=1, keepdims=True))
        p_own, p_prev = e_own * inverse, e_prev * inverse
        b_own, b_prev = p_own.astype(jnp.bfloat16), p_prev.astype(jnp.bfloat16)
        near = dot_nn(b_own, value) + dot_nn(b_prev, value_prev)
        blended[:, columns(h)] = (ret_mix[h] + (1.0 - mixing_of(h)) * near).astype(jnp.bfloat16)
        g_own, g_prev = soft_grads[h], dot_nt(local, value_prev)
        row_dot = jnp.sum(p_own * g_own, axis=1, keepdims=True) + jnp.sum(p_prev * g_prev, axis=1, keepdims=True)
        stats[h, 0:1] = as_row(top)
        stats[h, 1:2] = as_row(inverse)
        stats[h, 2:3] = as_row(row_dot)
        d_own = (p_own * (g_own - row_dot) * score_scale).astype(jnp.bfloat16)
        d_prev = (p_prev * (g_prev - row_dot) * score_scale).astype(jnp.bfloat16)
        own_grads[h] = dot_tn(d_own, query)
        own_grads[heads + h] = dot_tn(b_own, local)
        dq_att = dot_nn(d_own, key) + dot_nn(d_prev, key_prev)
        grads[0, h] = (dq_att + dq_ret[h]).astype(jnp.bfloat16)

    for h in range(heads):
        stats[h] = jnp.zeros(stats.shape[1:], jnp.float32)
    for h in range(heads):
        key_out[h].wait_recv()
        value_out[h].wait_recv()
        attend(h)
        stats_out[h].start()
        if h == 0:
            grad_memory_scan.give_back()
    blended_out = pltpu.make_async_copy(blended, blended_ref, out_sem.at[2])
    blended_out.start()

    def pair_grads(m):
        return pair_copy(grads.at[m, 1 - dp], g_all.at[m, pl.ds(tokens, tokens)], 1 + m)

    def keep_grads(m):
        g_all[m, pl.ds(0, tokens), :] = grads[m, dp]

    def products(m, target):
        at = pl.multiple_of(target * wide, 128)
        dw[m, target] = dot_nn(x_turned[pl.ds(at, wide), :], g_all[m])

    part = dim // 2

    def z_first(m, left, right):
        return lambda target, sub: dw[m, :, pl.ds(pl.multiple_of(target * block + sub * rows, 8), rows), left:right]

    def y_first(m, left, right):
        return lambda target, sub: dw[m, target, sub * (wide // 2):(sub + 1) * (wide // 2), left:right]

    def y_second(held):
        return lambda target, sub: held[sub, target]

    def z_second(held):
        return lambda target, sub: held[pl.ds(pl.multiple_of(target * block + sub * rows, 8), rows), :]

    def ring(axis, slot, mine, send, recv):
        sem = (ring_z_sem if axis == "z" else ring_y_sem).at[slot]
        at = slot if axis == "z" else 4 + slot
        return RingSum(axis, mine, send, recv, ring_send_sem.at[at], sem)

    a1 = ring("z", 0, z_first(1, 0, dim), a1_send, a1_recv)
    b1 = ring("y", 0, y_first(2, 0, dim), b1_send, b1_recv)
    c1 = ring("z", 1, z_first(0, 0, part), c1_send, c1_recv)
    d1 = ring("y", 1, y_first(0, part, dim), d1_send, d1_recv)
    a2 = ring("y", 2, y_second(a_sum), a2_send, a2_recv)
    b2 = ring("z", 2, z_second(b_sum), b2_send, b2_recv)
    c2 = ring("y", 3, y_second(c_sum), c2_send, c2_recv)
    d2 = ring("z", 3, z_second(d_sum), d2_send, d2_recv)

    def columns_in(sums, held):
        for sub in (0, 1):
            held[sub] = sums.total(sub)

    def multiply(m, first):
        products(m, lax.rem(y + ny // 2, ny))
        first.step(0, ny // 2)
        for ahead in range(1, ny):
            products(m, lax.rem(y + ny // 2 + ahead, ny))
        for ahead in range(1, ny):
            first.step(0, ny // 2 + ahead)

    def rows_in(sums, held):
        for sub in (0, 1):
            held[sub * (wide // 2):(sub + 1) * (wide // 2), :] = sums.total(sub)

    query_pair = pair_grads(0)
    query_pair.start()
    keep_grads(0)
    grad_norm_scan.across_rows()

    def serve(h):
        query, local = after_in[h], after_in[heads + h]
        top, inverse, row_dot = stats_in[h, 0:1], stats_in[h, 1:2], stats_in[h, 2:3]
        soft = jnp.exp(dot_nt(kvq[h], query) * score_scale + bias_after - top) * inverse
        given = (soft * (dot_nt(kvq[heads + h], local) - row_dot) * score_scale).astype(jnp.bfloat16)
        own_grads[h] += dot_nn(given, query)
        own_grads[heads + h] += dot_nn(soft.astype(jnp.bfloat16), local)

    query_out.wait_recv()
    for h in range(heads):
        if h == heads - 1:
            query_pair.wait_recv()
            multiply(0, d1)
            c1.step(0)
        local_out[h].wait_recv()
        stats_out[h].wait_recv()
        serve(h)
    norms[1] = grad_norm_scan.result()
    grad_memory_scan.finish()

    def write_back(h):
        key = kvq[h].astype(jnp.float32)
        grad_memory = grad_memory_scan.head(h, heads)
        grad_phi = dot_nt(kvq[heads + h], grad_memory) + norms[1, h]
        grads[1, h] = (own_grads[h] + grad_phi * feature_slope(key)).astype(jnp.bfloat16)
        grad_value = dot_nn(feature(key).astype(jnp.bfloat16), grad_memory)
        grads[2, h] = (own_grads[heads + h] + grad_value).astype(jnp.bfloat16)

    write_back(1 - dp)
    key_pair, value_pair = pair_grads(1), pair_grads(2)
    key_pair.start()
    value_pair.start()
    write_back(dp)
    keep_grads(1)
    keep_grads(2)
    key_pair.wait_recv()
    for k in range(ny):
        products(1, k)
    c1.step(1)
    a1.step(0)
    d1.step(1)
    value_pair.wait_recv()
    multiply(2, b1)
    c1.step(2)
    rows_in(d1, d_sum)
    d2.step(0)
    a1.step(1)
    b1.step(1)
    c1.step(3)
    d2.step(1)
    a1.step(2)
    columns_in(c1, c_sum)
    c2.step(0)
    d2.step(2)
    rows_in(b1, b_sum)
    b2.step(0)
    a1.step(3)
    d2.step(3)
    b2.step(1)
    c2.step(1)
    columns_in(a1, a_sum)
    a2.step(0)
    b2.step(2)
    a2.step(1)
    b2.step(3)
    places = ((c2, 0, part), (d2, part, dim), (a2, dim, 2 * dim), (b2, 2 * dim, 3 * dim))
    for sums, left, right in places:
        for sub in (0, 1):
            fin[sub, :, left:right] = sums.total(sub) * scale
    swap_out = pair_copy(fin.at[1 - dp], swap, 4)
    swap_out.start()

    def put(src, m, place, slot):
        return pltpu.make_async_copy(
            src.at[:, pl.ds(m * dim, dim)], out_ref.at[m, :, columns(place)], out_sem.at[slot]
        )

    own_out = [put(fin.at[dp], m, dp, 0) for m in range(3)]
    other_out = [put(swap, m, 1 - dp, 1) for m in range(3)]
    for copy in own_out:
        copy.start()
    for sent in (
        a1, b1, c1, d1, a2, b2, c2, d2, norm_scan, grad_norm_scan, memory_scan, grad_memory_scan,
    ):
        sent.drain()
    for copy in (*key_out, *value_out, *local_out, query_out, *stats_out, x_out, query_pair, key_pair, value_pair):
        copy.wait_send()
    swap_out.wait_recv()
    for copy in other_out:
        copy.start()
    swap_out.wait_send()
    blended_out.wait()
    for slot in (0, 1):
        pltpu.make_async_copy(fin.at[slot], swap, out_sem.at[slot]).wait()


def layer(x, wq, wk, wv, gate, cot, scale):
    tokens, depth = x.shape
    heads = gate.shape[0]
    dim = wq.shape[1] // heads
    ny, nz = lax.axis_size("y"), lax.axis_size("z")
    wide = depth // ny
    rows = wide // nz // 2
    zs, ys = 2 * (nz - 1), 2 * (ny - 1)
    wire = lambda *shape: pltpu.VMEM(shape, jnp.bfloat16)
    real = lambda *shape: pltpu.VMEM(shape, jnp.float32)
    dma = lambda *shape: pltpu.SemaphoreType.DMA(shape)
    a1, b1 = (zs, ny, rows), (ys, wide // 2)
    part = (heads * dim // nz, dim)
    vectors = [real(heads, 1, dim), real(nz, heads, 1, dim), real(heads, 1, dim), real(ny, heads, 1, dim)]
    scan = [
        wire(nz, *part), wire(nz, *part), real(nz, *part), real(*part), real(ny, *part), wire(nz, *part),
        wire(nz, *part),
    ]
    pair = (2 * heads, tokens, dim)
    anywhere = pl.BlockSpec(memory_space=pl.ANY)
    return pl.pallas_call(
        functools.partial(layer_kernel, scale),
        out_shape=(
            jax.ShapeDtypeStruct((tokens, heads * dim), jnp.bfloat16),
            jax.ShapeDtypeStruct((3, rows, heads * dim), jnp.float32),
        ),
        in_specs=[anywhere] * 4 + [pl.BlockSpec(memory_space=pltpu.SMEM), anywhere],
        out_specs=(anywhere,) * 2,
        scratch_shapes=[
            wire(2 * tokens, depth), wire(depth, 2 * tokens), wire(3 * heads, depth, dim), wire(tokens, heads * dim), wire(tokens, heads * dim),
            wire(3 * heads, tokens, dim), wire(*pair), wire(*pair), real(*pair),
            real(heads, tokens, dim), real(heads, tokens, dim),
            real(heads, tokens, tokens), real(heads, tokens, tokens), wire(heads, tokens, dim),
            wire(heads, tokens, dim), real(heads, tokens, 1), real(heads, 8, tokens), real(heads, 8, tokens),
            wire(3, heads, tokens, dim), wire(3, 2 * tokens, dim),
            *vectors, *vectors, real(2, heads, 1, dim), *scan, *scan,
            real(3, ny, wide, dim), real(2, ny, rows, dim), real(wide, dim), real(2, ny, rows, dim // 2), real(wide, dim // 2),
            real(2, rows, 3 * dim), real(rows, 3 * dim),
            wire(*a1, dim), wire(*a1, dim), wire(*b1, dim), wire(*b1, dim),
            wire(*a1, dim // 2), wire(*a1, dim // 2), wire(*b1, dim // 2), wire(*b1, dim // 2),
            wire(ys, rows, dim), wire(ys, rows, dim), wire(zs, rows, dim), wire(zs, rows, dim),
            wire(ys, rows, dim // 2), wire(ys, rows, dim // 2), wire(zs, rows, dim // 2), wire(zs, rows, dim // 2),
            dma(2 + 3 * heads), dma(2, 4 * heads + 1), dma(2, 5), dma(2, 2), dma(2, 2),
            dma(2, 2), dma(2, 2), dma(2, 2),
            dma(4, zs), dma(4, ys), dma(8), dma(3),
        ],
        compiler_params=pltpu.CompilerParams(
            collective_id=1, has_side_effects=True, vmem_limit_bytes=63 * 1024 * 1024
        ),
    )(x, wq, wk, wv, gate, cot)


def hand_on_kernel(a_ref, b_ref, a_out, b_out, a_held, b_held, sem):
    steps = [
        (pltpu.make_async_copy(src, held, sem.at[0, i]), pltpu.make_async_copy(held, dst, sem.at[1, i]))
        for i, (src, held, dst) in enumerate(((a_ref, a_held, a_out), (b_ref, b_held, b_out)))
    ]
    for first, _ in steps:
        first.start()
    for first, second in steps:
        first.wait()
        second.start()
    for _, second in steps:
        second.wait()


def hand_on(a, b):
    anywhere = pl.BlockSpec(memory_space=pl.ANY)
    return pl.pallas_call(
        hand_on_kernel,
        out_shape=tuple(jax.ShapeDtypeStruct(v.shape, v.dtype) for v in (a, b)),
        in_specs=[anywhere] * 2,
        out_specs=(anywhere,) * 2,
        scratch_shapes=[pltpu.VMEM(v.shape, v.dtype) for v in (a, b)] + [pltpu.SemaphoreType.DMA((2, 2))],
    )(a, b)


def local(inputs, w_query, w_key, w_value, gate_bias, cotangent):
    tokens = inputs[0]
    seg_len = tokens.shape[0]
    scale = 1.0 / math.sqrt(lax.axis_size(SEQ) * lax.axis_size("dp") * seg_len)
    blended, grad_weights = layer(tokens, w_query, w_key, w_value, gate_bias, cotangent[0], scale)
    blended, grad_weights = hand_on(blended, grad_weights)
    return (blended[None], grad_weights.transpose(1, 0, 2))


def solution(mesh):
    finer = Mesh(
        mesh.devices.reshape(4, 8, mesh.shape["dp"], mesh.shape["head"]),
        ("y", "z", "dp", "head"),
    )
    placed = (
        P("dp", SEQ, None),
        P(None, "head"),
        P(None, "head"),
        P(None, "head"),
        P("head"),
        P("dp", SEQ, "head"),
    )
    return jax.shard_map(
        local,
        mesh=finer,
        in_specs=placed,
        out_specs=(P("dp", SEQ, "head"), P(SEQ_DP, None, "head")),
        check_vma=False,
    )
```

```python
import functools
import math

import jax
import jax.numpy as jnp
from jax import lax
from jax.experimental import pallas as pl
from jax.experimental.pallas import tpu as pltpu
from jax.sharding import Mesh
from jax.sharding import PartitionSpec as P

SEQ = ("y", "z")
SEQ_DP = ("y", "z", "dp")
MESH = pl.DeviceIdType.MESH
MASKED = -1e30
PIECES = 4


def feature(u):
    return jnp.where(u > 0, u + 1.0, jnp.exp(jnp.minimum(u, 0.0)))


def feature_slope(u):
    return jnp.where(u > 0, 1.0, jnp.exp(jnp.minimum(u, 0.0)))


def contract(a, b, over_a, over_b):
    return lax.dot_general(
        a, b, (((over_a,), (over_b,)), ((), ())), preferred_element_type=jnp.float32
    )


def dot_nn(a, b):
    return contract(a, b, 1, 0)


def dot_nt(a, b):
    return contract(a, b, 1, 1)


def dot_tn(a, b):
    return contract(a, b, 0, 0)


def ring_chains(n):
    chains, first = [], 0
    for sub in (0, 1):
        for way in (1, -1):
            length = n // 2 if (way > 0) == (sub == 0) else n - 1 - n // 2
            chains.append((sub, way, length, first))
            first += length
    return chains


class RingSum:
    def __init__(self, axis, mine, send, recv, send_sem, recv_sem):
        self.axis, self.mine = axis, mine
        self.n, self.position = lax.axis_size(axis), lax.axis_index(axis)
        self.send, self.recv, self.send_sem, self.recv_sem = send, recv, send_sem, recv_sem
        self.chains = ring_chains(self.n)

    def copy(self, slot, way):
        return pltpu.make_async_remote_copy(
            src_ref=self.send.at[slot],
            dst_ref=self.recv.at[slot],
            send_sem=self.send_sem,
            recv_sem=self.recv_sem.at[slot],
            device_id={self.axis: lax.rem(self.position + way + self.n, self.n)},
            device_id_type=MESH,
        )

    def step(self, t, ahead=None):
        for sub, way, length, first in self.chains:
            if t >= length:
                continue
            if ahead is not None and (way * (length - t)) % self.n != ahead % self.n:
                continue
            target = lax.rem(self.position + way * (length - t) + self.n, self.n)
            value = self.mine(target, sub)
            if t:
                self.copy(first + t - 1, way).wait_recv()
                value = value + self.recv[first + t - 1].astype(jnp.float32)
            self.send[first + t] = value.astype(jnp.bfloat16)
            self.copy(first + t, way).start()

    def total(self, sub):
        value = self.mine(self.position, sub)
        for chain_sub, way, length, first in self.chains:
            if chain_sub == sub and length:
                self.copy(first + length - 1, way).wait_recv()
                value = value + self.recv[first + length - 1].astype(jnp.float32)
        return value

    def drain(self):
        self.all_copy().wait_send()

    def all_copy(self):
        return pltpu.make_async_remote_copy(
            src_ref=self.send, dst_ref=self.recv, send_sem=self.send_sem, recv_sem=self.recv_sem.at[0],
            device_id={self.axis: self.position}, device_id_type=MESH,
        )


class Spread:
    def __init__(self, axis, got, sem):
        self.axis, self.got, self.sem = axis, got, sem
        self.n, self.position = lax.axis_size(axis), lax.axis_index(axis)

    def copy(self, src, j):
        return pltpu.make_async_remote_copy(
            src_ref=src,
            dst_ref=self.got.at[j],
            send_sem=self.sem.at[0],
            recv_sem=self.sem.at[1],
            device_id={self.axis: lax.rem(self.position + j, self.n)},
            device_id_type=MESH,
        )

    def all_copy(self):
        others = self.got.at[pl.ds(1, self.n - 1)]
        return pltpu.make_async_remote_copy(
            src_ref=others, dst_ref=others, send_sem=self.sem.at[0], recv_sem=self.sem.at[1],
            device_id={self.axis: self.position}, device_id_type=MESH,
        )

    def start(self, src):
        for j in range(1, self.n):
            self.copy(src, j).start()

    def sums(self, own, reverse):
        passed, total = jnp.zeros_like(own), own
        self.all_copy().wait_recv()
        for j in range(1, self.n):
            value = self.got[j]
            earlier = self.position < j if reverse else self.position >= j
            passed = passed + value * jnp.where(earlier, 1.0, 0.0)
            total = total + value
        return passed, total

    def drain(self):
        self.all_copy().wait_send()


class VectorScan:
    def __init__(self, reverse, own, z_got, y_own, y_got, z_sem, y_sem):
        self.reverse, self.own, self.y_own = reverse, own, y_own
        self.z, self.y = Spread("z", z_got, z_sem), Spread("y", y_got, y_sem)

    def start(self):
        self.z.start(self.own)

    def across_rows(self):
        self.inside, total = self.z.sums(self.own[...], self.reverse)
        self.y_own[...] = total
        self.y.start(self.y_own)

    def result(self):
        passed, _ = self.y.sums(self.y_own[...], self.reverse)
        return passed + self.inside

    def drain(self):
        self.z.drain()
        self.y.drain()


class VectorScanDown:
    def __init__(self, reverse, own, y_got, z_own, z_got, y_sem, z_sem):
        self.reverse, self.own, self.z_own = reverse, own, z_own
        self.y, self.z = Spread("y", y_got, y_sem), Spread("z", z_got, z_sem)

    def start(self):
        self.y.start(self.own)

    def across_columns(self):
        passed, _ = self.y.sums(self.own[...], self.reverse)
        self.z_own[0] = self.own[...]
        self.z_own[1] = passed
        self.z.start(self.z_own)

    def result(self):
        passed, total = self.z.sums(self.z_own[...], self.reverse)
        return passed[0] + total[1]

    def drain(self):
        self.y.drain()
        self.z.drain()


class MemoryScan:
    def __init__(self, reverse, parts, got, inside, y_own, y_got, back, result, z_sem, y_sem, back_sem):
        self.reverse, self.parts, self.got, self.inside, self.y_own = reverse, parts, got, inside, y_own
        self.back, self.full, self.z_sem, self.back_sem = back, result, z_sem, back_sem
        self.n, self.position = lax.axis_size("z"), lax.axis_index("z")
        self.y = Spread("y", y_got, y_sem)

    def out_copy(self, j):
        target = lax.rem(self.position + j, self.n)
        return pltpu.make_async_remote_copy(
            src_ref=self.parts.at[target],
            dst_ref=self.got.at[j],
            send_sem=self.z_sem.at[0],
            recv_sem=self.z_sem.at[1],
            device_id={"z": target},
            device_id_type=MESH,
        )

    def back_copy(self, j):
        target = lax.rem(self.position + j, self.n)
        return pltpu.make_async_remote_copy(
            src_ref=self.back.at[target],
            dst_ref=self.full.at[self.position],
            send_sem=self.back_sem.at[0],
            recv_sem=self.back_sem.at[1],
            device_id={"z": target},
            device_id_type=MESH,
        )

    def start(self):
        for j in range(1, self.n):
            self.out_copy(j).start()

    def across_rows(self):
        self.all_copy(self.z_sem).wait_recv()
        self.got[0] = self.parts[self.position]
        run = jnp.zeros(self.y_own.shape, jnp.float32)
        for k in reversed(range(self.n)) if self.reverse else range(self.n):
            self.inside[k] = run
            run = run + self.got[lax.rem(self.position - k + self.n, self.n)].astype(jnp.float32)
        self.y_own[...] = run
        self.y.start(self.y_own)

    def give_back(self):
        passed, _ = self.y.sums(self.y_own[...], self.reverse)
        for k in range(self.n):
            self.back[k] = (self.inside[k] + passed).astype(jnp.bfloat16)
        for j in range(1, self.n):
            self.back_copy(j).start()
        self.full[self.position] = self.back[self.position]

    def finish(self):
        self.all_copy(self.back_sem).wait_recv()

    def head(self, h, heads):
        parts = self.n // heads
        block = self.full[pl.ds(h * parts, parts)]
        return block.reshape(parts * block.shape[1], block.shape[2])

    def drain(self):
        self.y.drain()
        self.all_copy(self.z_sem).wait_send()
        self.all_copy(self.back_sem).wait_send()

    def all_copy(self, sem):
        others = self.got.at[pl.ds(1, self.n - 1)]
        return pltpu.make_async_remote_copy(
            src_ref=others, dst_ref=others, send_sem=sem.at[0], recv_sem=sem.at[1],
            device_id={"z": self.position}, device_id_type=MESH,
        )


def layer_kernel(
    scale, x_ref, wq_ref, wk_ref, wv_ref, gate_ref, cot_ref, blended_ref, out_ref,
    x_all, x_turned, w_all, cot, blended, kvq, prev, after_in, own_grads, dq_att, near_mix,
    scores, soft_grads, grad_local, grad_num, den, stats, stats_in, grads, g_all,
    n1_own, n1_got, n1_yown, n1_ygot, n2_own, n2_ygot, n2_zown, n2_zgot, norms,
    m1_parts, m1_got, m1_inside, m1_yown, m1_ygot, m1_back, m1_full,
    m2_parts, m2_got, m2_inside, m2_yown, m2_ygot, m2_back, m2_full,
    dw, a_sum, b_sum, c_sum, d_sum, fin, swap,
    a1_send, a1_recv, b1_send, b1_recv, c1_send, c1_recv, d1_send, d1_recv,
    a2_send, a2_recv, b2_send, b2_recv, c2_send, c2_recv, d2_send, d2_recv,
    local_sem, halo_sem, pair_sem, nz_sem, ny_sem, mz_sem, my_sem, mb_sem, ring_z_sem, ring_y_sem, ring_send_sem, direct_sem, out_sem,
):
    ny, nz = lax.axis_size("y"), lax.axis_size("z")
    y, z, dp = lax.axis_index("y"), lax.axis_index("z"), lax.axis_index("dp")
    other = {"dp": 1 - dp}
    tokens = x_ref.shape[0]
    heads, dim = kvq.shape[0] // 3, kvq.shape[2]
    wide = dw.shape[2]
    block = wide // nz
    rows = block // 2
    up, down = z == nz - 1, z == 0
    after = {
        "y": lax.rem(y + jnp.where(up, 1, 0), ny), "z": lax.rem(z + 1, nz),
    }
    ahead_of = {
        "y": lax.rem(y - jnp.where(down, 1, 0) + ny, ny), "z": lax.rem(z - 1 + nz, nz),
    }
    score_scale = dim ** (-0.5)

    x_in = pltpu.make_async_copy(x_ref, x_all.at[pl.ds(0, tokens)], local_sem.at[0])
    cot_in = pltpu.make_async_copy(cot_ref, cot, local_sem.at[1])
    w_in = [
        pltpu.make_async_copy(w.at[:, pl.ds(h * dim, dim)], w_all.at[at * heads + h], local_sem.at[2 + at * heads + h])
        for at, w in enumerate((wk_ref, wv_ref, wq_ref)) for h in range(heads)
    ]
    x_in.start()
    w_in[0].start()
    cot_in.start()

    barrier = pltpu.get_barrier_semaphore()
    partners = [other, after, ahead_of]
    partners += [{"z": lax.rem(z + j, nz)} for j in range(1, nz)]
    partners += [{"y": lax.rem(y + j, ny)} for j in range(1, ny)]
    for device in partners:
        pl.semaphore_signal(barrier, inc=1, device_id=device, device_id_type=MESH)

    def project(first, last):
        for c in range(first, last):
            w_in[c].wait()
        def body(c, carry):
            kvq[c] = dot_nn(x_all[pl.ds(0, tokens), :], w_all[c]).astype(jnp.bfloat16)
            return carry
        lax.fori_loop(first, last, body, 0)

    def halo_copy(src, dst, slot, device):
        return pltpu.make_async_remote_copy(
            src_ref=src, dst_ref=dst, send_sem=halo_sem.at[0, slot], recv_sem=halo_sem.at[1, slot],
            device_id=device, device_id_type=MESH,
        )

    key_out = [halo_copy(kvq.at[h], prev.at[h], h, after) for h in range(heads)]
    value_out = [halo_copy(kvq.at[heads + h], prev.at[heads + h], heads + h, after) for h in range(heads)]
    local_out = [
        halo_copy(grad_local.at[h], after_in.at[heads + h], 2 * heads + h, ahead_of) for h in range(heads)
    ]
    query_out = [halo_copy(kvq.at[2 * heads + h], after_in.at[h], 3 * heads + h, ahead_of) for h in range(heads)]
    stats_out = [halo_copy(stats.at[h], stats_in.at[h], 4 * heads + h, ahead_of) for h in range(heads)]

    def pair_copy(src, dst, slot):
        return pltpu.make_async_remote_copy(
            src_ref=src, dst_ref=dst, send_sem=pair_sem.at[0, slot], recv_sem=pair_sem.at[1, slot],
            device_id=other, device_id_type=MESH,
        )

    def each_head(body):
        def step(h, carry):
            body(h)
            return carry
        lax.fori_loop(0, heads, step, 0)

    def columns(h):
        return pl.ds(pl.multiple_of(h * dim, dim), dim)

    norm_scan = VectorScan(False, n1_own, n1_got, n1_yown, n1_ygot, nz_sem.at[0], ny_sem.at[0])
    grad_norm_scan = VectorScanDown(True, n2_own, n2_ygot, n2_zown, n2_zgot, ny_sem.at[1], nz_sem.at[1])
    memory_scan = MemoryScan(
        False, m1_parts, m1_got, m1_inside, m1_yown, m1_ygot, m1_back, m1_full,
        mz_sem.at[0], my_sem.at[0], mb_sem.at[0],
    )
    grad_memory_scan = MemoryScan(
        True, m2_parts, m2_got, m2_inside, m2_yown, m2_ygot, m2_back, m2_full,
        mz_sem.at[1], my_sem.at[1], mb_sem.at[1],
    )
    parts = nz // heads

    def put_parts(target, h, value):
        target[pl.ds(h * parts, parts)] = value.astype(jnp.bfloat16).reshape(parts, dim // parts, dim)

    def mixing_of(h):
        return 1.0 / (1.0 + jnp.exp(-jnp.full((1, dim), gate_ref[h], jnp.float32)))

    x_in.wait()
    for copy in w_in[1:]:
        copy.start()
    cot_in.wait()

    def local_gradient(h):
        upstream = cot[:, columns(h)].astype(jnp.float32)
        grad_local[h] = ((1.0 - mixing_of(h)) * upstream).astype(jnp.bfloat16)

    each_head(local_gradient)
    project(0, 1)
    pl.semaphore_wait(barrier, len(partners))
    key_out[0].start()
    local_out[0].start()
    project(1, heads)

    def key_sums(h):
        n1_own[h] = jnp.sum(feature(kvq[h].astype(jnp.float32)), axis=0, keepdims=True)

    each_head(key_sums)
    norm_scan.start()
    x_out = pair_copy(x_all.at[pl.ds(0, tokens)], x_all.at[pl.ds(tokens, tokens)], 0)
    x_out.start()
    project(heads, 2 * heads)

    def write(h):
        phi = feature(kvq[h].astype(jnp.float32)).astype(jnp.bfloat16)
        put_parts(m1_parts, h, dot_tn(phi, kvq[heads + h]))

    each_head(write)
    memory_scan.start()
    for h in range(1, heads):
        key_out[h].start()
        local_out[h].start()
    project(2 * heads, 3 * heads)
    norm_scan.across_rows()

    def own_part(h):
        row = lax.broadcasted_iota(jnp.int32, (tokens, tokens), 0)
        col = lax.broadcasted_iota(jnp.int32, (tokens, tokens), 1)
        scores[h] = jnp.where(col <= row, dot_nt(kvq[2 * heads + h], kvq[h]) * score_scale, MASKED)
        soft_grads[h] = dot_nt(grad_local[h], kvq[heads + h])

    each_head(own_part)
    norms[0] = norm_scan.result()

    def memory_gradient(h):
        phi = feature(kvq[2 * heads + h].astype(jnp.float32))
        divisor = jnp.sum(phi * norms[0, h], axis=1, keepdims=True) + 1.0
        den[h] = divisor
        grad_ret = mixing_of(h) * cot[:, columns(h)].astype(jnp.float32)
        number = (grad_ret / divisor).astype(jnp.bfloat16)
        grad_num[h] = number
        put_parts(m2_parts, h, dot_tn(phi.astype(jnp.bfloat16), number))

    each_head(memory_gradient)
    grad_memory_scan.start()
    value_out[0].start()
    query_out[0].start()
    memory_scan.across_rows()
    memory_scan.give_back()
    for h in range(1, heads):
        value_out[h].start()
        query_out[h].start()

    x_out.wait_recv()
    tile = min(wide, 256)

    def turn(i, carry):
        at = pl.ds(pl.multiple_of(i * tile, 128), tile)
        x_turned[at, :] = x_all[:, at].T
        return carry

    lax.fori_loop(0, x_all.shape[1] // tile, turn, 0)
    grad_memory_scan.across_rows()

    segment, last = y * nz + z, ny * nz - 1
    bias = jnp.where(segment > 0, 0.0, MASKED)
    bias_after = jnp.where(segment < last, 0.0, MASKED)

    def as_row(column):
        return jnp.broadcast_to(column, (tokens, 128)).T[:1]

    seen = set()

    def join(h, output, grad):
        kind = (h, output is None)
        if kind not in seen:
            seen.add(kind)
            if output is None:
                dq_att[h] = grad
            else:
                near_mix[h] = output
        elif output is None:
            grads[0, h] = (dq_att[h] + grad).astype(jnp.bfloat16)
        else:
            blended[:, columns(h)] = (near_mix[h] + output).astype(jnp.bfloat16)

    def attend(h):
        query, key, value = kvq[2 * heads + h], kvq[h], kvq[heads + h]
        key_prev, value_prev, local = prev[h], prev[heads + h], grad_local[h]
        s_own = scores[h]
        s_prev = dot_nt(query, key_prev) * score_scale + bias
        top = jnp.maximum(jnp.max(s_own, axis=1, keepdims=True), jnp.max(s_prev, axis=1, keepdims=True))
        e_own, e_prev = jnp.exp(s_own - top), jnp.exp(s_prev - top)
        inverse = 1.0 / (jnp.sum(e_own, axis=1, keepdims=True) + jnp.sum(e_prev, axis=1, keepdims=True))
        p_own, p_prev = e_own * inverse, e_prev * inverse
        b_own, b_prev = p_own.astype(jnp.bfloat16), p_prev.astype(jnp.bfloat16)
        near = dot_nn(b_own, value) + dot_nn(b_prev, value_prev)
        join(h, (1.0 - mixing_of(h)) * near, None)
        g_own, g_prev = soft_grads[h], dot_nt(local, value_prev)
        row_dot = jnp.sum(p_own * g_own, axis=1, keepdims=True) + jnp.sum(p_prev * g_prev, axis=1, keepdims=True)
        stats[h, 0:1] = as_row(top)
        stats[h, 1:2] = as_row(inverse)
        stats[h, 2:3] = as_row(row_dot)
        d_own = (p_own * (g_own - row_dot) * score_scale).astype(jnp.bfloat16)
        d_prev = (p_prev * (g_prev - row_dot) * score_scale).astype(jnp.bfloat16)
        own_grads[h] = dot_tn(d_own, query)
        own_grads[heads + h] = dot_tn(b_own, local)
        join(h, None, dot_nn(d_own, key) + dot_nn(d_prev, key_prev))

    for h in range(heads):
        stats[h] = jnp.zeros(stats.shape[1:], jnp.float32)
    def pair_grads(m):
        return pair_copy(grads.at[m, 1 - dp], g_all.at[m, pl.ds(tokens, tokens)], 1 + m)

    def keep_grads(m):
        g_all[m, pl.ds(0, tokens), :] = grads[m, dp]

    def products(m, target):
        at = pl.multiple_of(target * wide, 128)
        dw[m, target] = dot_nn(x_turned[pl.ds(at, wide), :], g_all[m])

    part = dim // 2

    def z_first(m, left, right):
        return lambda target, sub: dw[m, :, pl.ds(pl.multiple_of(target * block + sub * rows, 8), rows), left:right]

    def y_first(m, left, right):
        return lambda target, sub: dw[m, target, sub * (wide // 2):(sub + 1) * (wide // 2), left:right]

    def z_second(held):
        return lambda target, sub: held[pl.ds(pl.multiple_of(target * block + sub * rows, 8), rows), :]

    def ring(axis, slot, mine, send, recv):
        sem = (ring_z_sem if axis == "z" else ring_y_sem).at[slot]
        at = slot if axis == "z" else 4 + slot
        return RingSum(axis, mine, send, recv, ring_send_sem.at[at], sem)

    a1 = ring("z", 0, z_first(1, 0, dim), a1_send, a1_recv)
    b1 = ring("y", 0, y_first(2, 0, dim), b1_send, b1_recv)
    c1 = ring("z", 1, z_first(0, 0, part), c1_send, c1_recv)
    d1 = ring("y", 1, y_first(0, part, dim), d1_send, d1_recv)
    a2 = Spread("y", a2_recv, direct_sem.at[0])
    b2 = ring("z", 2, z_second(b_sum), b2_send, b2_recv)
    c2 = Spread("y", c2_recv, direct_sem.at[1])
    d2 = ring("z", 3, z_second(d_sum), d2_send, d2_recv)

    def columns_in(sums, held):
        for sub in (0, 1):
            held[sub] = sums.total(sub)

    def send_parts(spread, held, parts):
        for j in range(1, ny):
            parts[j] = held[:, lax.rem(y + j, ny)].astype(jnp.bfloat16)
            spread.copy(parts.at[j], j).start()

    def direct_total(spread, held):
        spread.all_copy().wait_recv()
        value = held[:, y]
        for j in range(1, ny):
            value = value + spread.got[j].astype(jnp.float32)
        return value

    def multiply_far(m, first):
        products(m, lax.rem(y + ny // 2, ny))
        first.step(0, ny // 2)

    def multiply_near(m, first):
        for ahead in range(1, ny):
            products(m, lax.rem(y + ny // 2 + ahead, ny))
        for ahead in range(1, ny):
            first.step(0, ny // 2 + ahead)

    def rows_in(sums, held):
        for sub in (0, 1):
            held[sub * (wide // 2):(sub + 1) * (wide // 2), :] = sums.total(sub)

    def serve(h):
        query, local = after_in[h], after_in[heads + h]
        top, inverse, row_dot = stats_in[h, 0:1], stats_in[h, 1:2], stats_in[h, 2:3]
        soft = jnp.exp(dot_nt(kvq[h], query) * score_scale + bias_after - top) * inverse
        given = (soft * (dot_nt(kvq[heads + h], local) - row_dot) * score_scale).astype(jnp.bfloat16)
        own_grads[h] += dot_nn(given, query)
        own_grads[heads + h] += dot_nn(soft.astype(jnp.bfloat16), local)

    def retrieve(h):
        mixing = mixing_of(h)
        query = kvq[2 * heads + h].astype(jnp.float32)
        phi = feature(query)
        memory = memory_scan.head(h, heads)
        retrieved = dot_nn(phi.astype(jnp.bfloat16), memory) / den[h]
        join(h, mixing * retrieved, None)
        grad_ret = mixing * cot[:, columns(h)].astype(jnp.float32)
        grad_den = -jnp.sum(grad_ret * retrieved, axis=1, keepdims=True) / den[h]
        n2_own[h] = jnp.sum(grad_den * phi, axis=0, keepdims=True)
        grad_phi = dot_nt(grad_num[h], memory) + grad_den * norms[0, h]
        join(h, None, grad_phi * feature_slope(query))

    def attend_now(h):
        key_out[h].wait_recv()
        value_out[h].wait_recv()
        attend(h)
        stats_out[h].start()

    def serve_now(h):
        query_out[h].wait_recv()
        local_out[h].wait_recv()
        stats_out[h].wait_recv()
        serve(h)

    for h in range(heads - 1):
        attend_now(h)
    grad_memory_scan.give_back()
    memory_scan.finish()
    for h in range(heads):
        retrieve(h)
    grad_norm_scan.start()
    attend_now(heads - 1)
    query_pair = pair_grads(0)
    query_pair.start()
    keep_grads(0)
    grad_norm_scan.across_columns()
    blended_out = pltpu.make_async_copy(blended, blended_ref, out_sem.at[2])
    blended_out.start()
    for h in range(heads - 1):
        serve_now(h)
    query_pair.wait_recv()
    multiply_far(0, d1)
    multiply_near(0, d1)
    c1.step(0)
    serve_now(heads - 1)
    grad_memory_scan.finish()
    norms[1] = grad_norm_scan.result()

    def write_back(h):
        key = kvq[h].astype(jnp.float32)
        grad_memory = grad_memory_scan.head(h, heads)
        grad_phi = dot_nt(kvq[heads + h], grad_memory) + norms[1, h]
        grads[1, h] = (own_grads[h] + grad_phi * feature_slope(key)).astype(jnp.bfloat16)
        grad_value = dot_nn(feature(key).astype(jnp.bfloat16), grad_memory)
        grads[2, h] = (own_grads[heads + h] + grad_value).astype(jnp.bfloat16)

    key_pair, value_pair = pair_grads(1), pair_grads(2)
    write_back(1 - dp)
    key_pair.start()
    value_pair.start()
    write_back(dp)
    keep_grads(1)
    keep_grads(2)
    key_pair.wait_recv()
    for k in range(ny):
        products(1, k)
    c1.step(1)
    a1.step(0)
    d1.step(1)
    value_pair.wait_recv()
    multiply_far(2, b1)
    multiply_near(2, b1)
    c1.step(2)
    rows_in(d1, d_sum)
    d2.step(0)
    a1.step(1)
    b1.step(1)
    c1.step(3)
    d2.step(1)
    a1.step(2)
    columns_in(c1, c_sum)
    send_parts(c2, c_sum, c2_send)
    d2.step(2)
    rows_in(b1, b_sum)
    b2.step(0)
    a1.step(3)
    d2.step(3)
    b2.step(1)
    columns_in(a1, a_sum)
    send_parts(a2, a_sum, a2_send)
    b2.step(2)

    def put(src, m, place, slot):
        return pltpu.make_async_copy(
            src.at[:, pl.ds(m * dim, dim)], out_ref.at[m, :, columns(place)], out_sem.at[slot]
        )

    swaps = [
        pair_copy(fin.at[1 - dp, :, pl.ds(m * dim, dim)], swap.at[:, pl.ds(m * dim, dim)], 4 + m) for m in range(3)
    ]

    def hand_over(m):
        swaps[m].start()
        put(fin.at[dp], m, dp, 0).start()

    fin[:, :, 0:part] = direct_total(c2, c_sum) * scale
    for sub in (0, 1):
        fin[sub, :, part:dim] = d2.total(sub) * scale
    hand_over(0)
    b2.step(3)
    fin[:, :, dim:2 * dim] = direct_total(a2, a_sum) * scale
    hand_over(1)
    for sub in (0, 1):
        fin[sub, :, 2 * dim:3 * dim] = b2.total(sub) * scale
    hand_over(2)
    for sent in (
        a1, b1, c1, d1, a2, b2, c2, d2, norm_scan, grad_norm_scan, memory_scan, grad_memory_scan,
    ):
        sent.drain()
    for copy in (*key_out, *value_out, *local_out, *query_out, *stats_out, x_out, query_pair, key_pair, value_pair):
        copy.wait_send()
    for m in range(3):
        swaps[m].wait_recv()
        put(swap, m, 1 - dp, 1).start()
    for m in range(3):
        swaps[m].wait_send()
    blended_out.wait()
    for slot in (0, 1):
        pltpu.make_async_copy(fin.at[slot], swap, out_sem.at[slot]).wait()


def layer(x, wq, wk, wv, gate, cot, scale):
    tokens, depth = x.shape
    heads = gate.shape[0]
    dim = wq.shape[1] // heads
    ny, nz = lax.axis_size("y"), lax.axis_size("z")
    wide = depth // ny
    rows = wide // nz // 2
    zs, ys = 2 * (nz - 1), 2 * (ny - 1)
    wire = lambda *shape: pltpu.VMEM(shape, jnp.bfloat16)
    real = lambda *shape: pltpu.VMEM(shape, jnp.float32)
    dma = lambda *shape: pltpu.SemaphoreType.DMA(shape)
    a1, b1 = (zs, ny, rows), (ys, wide // 2)
    part = (heads * dim // nz, dim)
    vectors = [real(heads, 1, dim), real(nz, heads, 1, dim), real(heads, 1, dim), real(ny, heads, 1, dim)]
    scan = [
        wire(nz, *part), wire(nz, *part), real(nz, *part), real(*part), real(ny, *part), wire(nz, *part),
        wire(nz, *part),
    ]
    pair = (2 * heads, tokens, dim)
    anywhere = pl.BlockSpec(memory_space=pl.ANY)
    return pl.pallas_call(
        functools.partial(layer_kernel, scale),
        out_shape=(
            jax.ShapeDtypeStruct((tokens, heads * dim), jnp.bfloat16),
            jax.ShapeDtypeStruct((3, rows, heads * dim), jnp.float32),
        ),
        in_specs=[anywhere] * 4 + [pl.BlockSpec(memory_space=pltpu.SMEM), anywhere],
        out_specs=(anywhere,) * 2,
        scratch_shapes=[
            wire(2 * tokens, depth), wire(depth, 2 * tokens), wire(3 * heads, depth, dim), wire(tokens, heads * dim), wire(tokens, heads * dim),
            wire(3 * heads, tokens, dim), wire(*pair), wire(*pair), real(*pair),
            real(heads, tokens, dim), real(heads, tokens, dim),
            real(heads, tokens, tokens), real(heads, tokens, tokens), wire(heads, tokens, dim),
            wire(heads, tokens, dim), real(heads, tokens, 1), real(heads, 8, tokens), real(heads, 8, tokens),
            wire(3, heads, tokens, dim), wire(3, 2 * tokens, dim),
            *vectors, real(heads, 1, dim), real(ny, heads, 1, dim), real(2, heads, 1, dim), real(nz, 2, heads, 1, dim),
            real(2, heads, 1, dim), *scan, *scan,
            real(3, ny, wide, dim), real(2, ny, rows, dim), real(wide, dim), real(2, ny, rows, dim // 2), real(wide, dim // 2),
            real(2, rows, 3 * dim), real(rows, 3 * dim),
            wire(*a1, dim), wire(*a1, dim), wire(*b1, dim), wire(*b1, dim),
            wire(*a1, dim // 2), wire(*a1, dim // 2), wire(*b1, dim // 2), wire(*b1, dim // 2),
            wire(ny, 2, rows, dim), wire(ny, 2, rows, dim), wire(zs, rows, dim), wire(zs, rows, dim),
            wire(ny, 2, rows, dim // 2), wire(ny, 2, rows, dim // 2), wire(zs, rows, dim // 2), wire(zs, rows, dim // 2),
            dma(2 + 3 * heads), dma(2, 5 * heads), dma(2, 7), dma(2, 2), dma(2, 2),
            dma(2, 2), dma(2, 2), dma(2, 2),
            dma(4, zs), dma(2, ys), dma(8), dma(2, 2), dma(3),
        ],
        compiler_params=pltpu.CompilerParams(
            collective_id=1, has_side_effects=True, vmem_limit_bytes=63 * 1024 * 1024
        ),
    )(x, wq, wk, wv, gate, cot)


def hand_on_kernel(a_ref, b_ref, a_out, b_out, a_held, b_held, sem):
    size = a_ref.shape[0] // PIECES
    whole = [(b_ref.at[m], b_held.at[m], b_out.at[m]) for m in range(b_ref.shape[0])]
    whole += [tuple(ref.at[pl.ds(i * size, size)] for ref in (a_ref, a_held, a_out)) for i in range(PIECES)]
    reads = [pltpu.make_async_copy(src, held, sem.at[0, i]) for i, (src, held, _) in enumerate(whole)]
    writes = [pltpu.make_async_copy(held, dst, sem.at[1, i]) for i, (_, held, dst) in enumerate(whole)]
    for read in reads:
        read.start()
    for read, write in zip(reads, writes):
        read.wait()
        write.start()
    for write in writes:
        write.wait()


def hand_on(a, b):
    anywhere = pl.BlockSpec(memory_space=pl.ANY)
    return pl.pallas_call(
        hand_on_kernel,
        out_shape=tuple(jax.ShapeDtypeStruct(v.shape, v.dtype) for v in (a, b)),
        in_specs=[anywhere] * 2,
        out_specs=(anywhere,) * 2,
        scratch_shapes=[pltpu.VMEM(v.shape, v.dtype) for v in (a, b)]
        + [pltpu.SemaphoreType.DMA((2, PIECES + b.shape[0]))],
    )(a, b)


def local(inputs, w_query, w_key, w_value, gate_bias, cotangent):
    tokens = inputs[0]
    seg_len = tokens.shape[0]
    scale = 1.0 / math.sqrt(lax.axis_size(SEQ) * lax.axis_size("dp") * seg_len)
    blended, grad_weights = layer(tokens, w_query, w_key, w_value, gate_bias, cotangent[0], scale)
    blended, grad_weights = hand_on(blended, grad_weights)
    return (blended[None], grad_weights.transpose(1, 0, 2))


def solution(mesh):
    finer = Mesh(
        mesh.devices.reshape(4, 8, mesh.shape["dp"], mesh.shape["head"]),
        ("y", "z", "dp", "head"),
    )
    placed = (
        P("dp", SEQ, None),
        P(None, "head"),
        P(None, "head"),
        P(None, "head"),
        P("head"),
        P("dp", SEQ, "head"),
    )
    return jax.shard_map(
        local,
        mesh=finer,
        in_specs=placed,
        out_specs=(P("dp", SEQ, "head"), P(SEQ_DP, None, "head")),
        check_vma=False,
    )
```

```python
import functools
import math

import jax
import jax.numpy as jnp
from jax import lax
from jax.experimental import pallas as pl
from jax.experimental.pallas import tpu as pltpu
from jax.sharding import Mesh
from jax.sharding import PartitionSpec as P

SEQ = ("y", "z")
SEQ_DP = ("y", "z", "dp")
MESH = pl.DeviceIdType.MESH
MASKED = -1e30
PIECES = 4


def feature(u):
    return jnp.where(u > 0, u + 1.0, jnp.exp(jnp.minimum(u, 0.0)))


def feature_slope(u):
    return jnp.where(u > 0, 1.0, jnp.exp(jnp.minimum(u, 0.0)))


def contract(a, b, over_a, over_b):
    return lax.dot_general(
        a, b, (((over_a,), (over_b,)), ((), ())), preferred_element_type=jnp.float32
    )


def dot_nn(a, b):
    return contract(a, b, 1, 0)


def dot_nt(a, b):
    return contract(a, b, 1, 1)


def dot_tn(a, b):
    return contract(a, b, 0, 0)


def ring_chains(n):
    chains, first = [], 0
    for sub in (0, 1):
        for way in (1, -1):
            length = n // 2 if (way > 0) == (sub == 0) else n - 1 - n // 2
            chains.append((sub, way, length, first))
            first += length
    return chains


class RingSum:
    def __init__(self, axis, mine, send, recv, send_sem, recv_sem):
        self.axis, self.mine = axis, mine
        self.n, self.position = lax.axis_size(axis), lax.axis_index(axis)
        self.send, self.recv, self.send_sem, self.recv_sem = send, recv, send_sem, recv_sem
        self.chains = ring_chains(self.n)

    def copy(self, slot, way):
        return pltpu.make_async_remote_copy(
            src_ref=self.send.at[slot],
            dst_ref=self.recv.at[slot],
            send_sem=self.send_sem,
            recv_sem=self.recv_sem.at[slot],
            device_id={self.axis: lax.rem(self.position + way + self.n, self.n)},
            device_id_type=MESH,
        )

    def step(self, t, ahead=None):
        for sub, way, length, first in self.chains:
            if t >= length:
                continue
            if ahead is not None and (way * (length - t)) % self.n != ahead % self.n:
                continue
            target = lax.rem(self.position + way * (length - t) + self.n, self.n)
            value = self.mine(target, sub)
            if t:
                self.copy(first + t - 1, way).wait_recv()
                value = value + self.recv[first + t - 1].astype(jnp.float32)
            self.send[first + t] = value.astype(jnp.bfloat16)
            self.copy(first + t, way).start()

    def total(self, sub):
        value = self.mine(self.position, sub)
        for chain_sub, way, length, first in self.chains:
            if chain_sub == sub and length:
                self.copy(first + length - 1, way).wait_recv()
                value = value + self.recv[first + length - 1].astype(jnp.float32)
        return value

    def drain(self):
        self.all_copy().wait_send()

    def all_copy(self):
        return pltpu.make_async_remote_copy(
            src_ref=self.send, dst_ref=self.recv, send_sem=self.send_sem, recv_sem=self.recv_sem.at[0],
            device_id={self.axis: self.position}, device_id_type=MESH,
        )


class Spread:
    def __init__(self, axis, got, sem):
        self.axis, self.got, self.sem = axis, got, sem
        self.n, self.position = lax.axis_size(axis), lax.axis_index(axis)

    def copy(self, src, j):
        return pltpu.make_async_remote_copy(
            src_ref=src,
            dst_ref=self.got.at[j],
            send_sem=self.sem.at[0],
            recv_sem=self.sem.at[1],
            device_id={self.axis: lax.rem(self.position + j, self.n)},
            device_id_type=MESH,
        )

    def all_copy(self):
        others = self.got.at[pl.ds(1, self.n - 1)]
        return pltpu.make_async_remote_copy(
            src_ref=others, dst_ref=others, send_sem=self.sem.at[0], recv_sem=self.sem.at[1],
            device_id={self.axis: self.position}, device_id_type=MESH,
        )

    def start(self, src):
        for j in range(1, self.n):
            self.copy(src, j).start()

    def sums(self, own, reverse):
        passed, total = jnp.zeros_like(own), own
        self.all_copy().wait_recv()
        for j in range(1, self.n):
            value = self.got[j]
            earlier = self.position < j if reverse else self.position >= j
            passed = passed + value * jnp.where(earlier, 1.0, 0.0)
            total = total + value
        return passed, total

    def drain(self):
        self.all_copy().wait_send()


class VectorScan:
    def __init__(self, reverse, own, z_got, y_own, y_got, z_sem, y_sem):
        self.reverse, self.own, self.y_own = reverse, own, y_own
        self.z, self.y = Spread("z", z_got, z_sem), Spread("y", y_got, y_sem)

    def start(self):
        self.z.start(self.own)

    def across_rows(self):
        self.inside, total = self.z.sums(self.own[...], self.reverse)
        self.y_own[...] = total
        self.y.start(self.y_own)

    def result(self):
        passed, _ = self.y.sums(self.y_own[...], self.reverse)
        return passed + self.inside

    def drain(self):
        self.z.drain()
        self.y.drain()


class VectorScanDown:
    def __init__(self, reverse, own, y_got, z_own, z_got, y_sem, z_sem):
        self.reverse, self.own, self.z_own = reverse, own, z_own
        self.y, self.z = Spread("y", y_got, y_sem), Spread("z", z_got, z_sem)

    def start(self):
        self.y.start(self.own)

    def across_columns(self):
        passed, _ = self.y.sums(self.own[...], self.reverse)
        self.z_own[0] = self.own[...]
        self.z_own[1] = passed
        self.z.start(self.z_own)

    def result(self):
        passed, total = self.z.sums(self.z_own[...], self.reverse)
        return passed[0] + total[1]

    def drain(self):
        self.y.drain()
        self.z.drain()


class MemoryScan:
    def __init__(self, reverse, parts, got, inside, y_own, y_got, back, result, z_sem, y_sem, back_sem):
        self.reverse, self.parts, self.got, self.inside, self.y_own = reverse, parts, got, inside, y_own
        self.back, self.full, self.z_sem, self.back_sem = back, result, z_sem, back_sem
        self.n, self.position = lax.axis_size("z"), lax.axis_index("z")
        self.y = Spread("y", y_got, y_sem)

    def out_copy(self, j):
        target = lax.rem(self.position + j, self.n)
        return pltpu.make_async_remote_copy(
            src_ref=self.parts.at[target],
            dst_ref=self.got.at[j],
            send_sem=self.z_sem.at[0],
            recv_sem=self.z_sem.at[1],
            device_id={"z": target},
            device_id_type=MESH,
        )

    def back_copy(self, j):
        target = lax.rem(self.position + j, self.n)
        return pltpu.make_async_remote_copy(
            src_ref=self.back.at[target],
            dst_ref=self.full.at[self.position],
            send_sem=self.back_sem.at[0],
            recv_sem=self.back_sem.at[1],
            device_id={"z": target},
            device_id_type=MESH,
        )

    def start(self):
        for j in range(1, self.n):
            self.out_copy(j).start()

    def across_rows(self):
        self.all_copy(self.z_sem).wait_recv()
        self.got[0] = self.parts[self.position]
        run = jnp.zeros(self.y_own.shape, jnp.float32)
        for k in reversed(range(self.n)) if self.reverse else range(self.n):
            self.inside[k] = run
            run = run + self.got[lax.rem(self.position - k + self.n, self.n)].astype(jnp.float32)
        self.y_own[...] = run
        self.y.start(self.y_own)

    def give_back(self):
        passed, _ = self.y.sums(self.y_own[...], self.reverse)
        for k in range(self.n):
            self.back[k] = (self.inside[k] + passed).astype(jnp.bfloat16)
        for j in range(1, self.n):
            self.back_copy(j).start()
        self.full[self.position] = self.back[self.position]

    def finish(self):
        self.all_copy(self.back_sem).wait_recv()

    def head(self, h, heads):
        parts = self.n // heads
        block = self.full[pl.ds(h * parts, parts)]
        return block.reshape(parts * block.shape[1], block.shape[2])

    def drain(self):
        self.y.drain()
        self.all_copy(self.z_sem).wait_send()
        self.all_copy(self.back_sem).wait_send()

    def all_copy(self, sem):
        others = self.got.at[pl.ds(1, self.n - 1)]
        return pltpu.make_async_remote_copy(
            src_ref=others, dst_ref=others, send_sem=sem.at[0], recv_sem=sem.at[1],
            device_id={"z": self.position}, device_id_type=MESH,
        )


def layer_kernel(
    scale, x_ref, wq_ref, wk_ref, wv_ref, gate_ref, cot_ref, blended_ref, out_ref,
    x_all, x_turned, w_all, cot, blended, kvq, prev, after_in, own_grads, dq_att, near_mix,
    scores, soft_grads, grad_local, grad_num, den, stats, stats_in, grads, g_all,
    n1_own, n1_got, n1_yown, n1_ygot, n2_own, n2_ygot, n2_zown, n2_zgot, norms,
    m1_parts, m1_got, m1_inside, m1_yown, m1_ygot, m1_back, m1_full,
    m2_parts, m2_got, m2_inside, m2_yown, m2_ygot, m2_back, m2_full,
    dw, a_sum, b_sum, c_sum, d_sum, fin, swap,
    a1_send, a1_recv, b1_send, b1_recv, c1_send, c1_recv, d1_send, d1_recv,
    a2_send, a2_recv, b2_send, b2_recv, c2_send, c2_recv, d2_send, d2_recv,
    local_sem, halo_sem, pair_sem, nz_sem, ny_sem, mz_sem, my_sem, mb_sem, ring_z_sem, ring_y_sem, ring_send_sem, direct_sem, out_sem,
):
    ny, nz = lax.axis_size("y"), lax.axis_size("z")
    y, z, dp = lax.axis_index("y"), lax.axis_index("z"), lax.axis_index("dp")
    other = {"dp": 1 - dp}
    tokens = x_ref.shape[0]
    heads, dim = kvq.shape[0] // 3, kvq.shape[2]
    wide = dw.shape[2]
    block = wide // nz
    rows = block // 2
    up, down = z == nz - 1, z == 0
    after = {
        "y": lax.rem(y + jnp.where(up, 1, 0), ny), "z": lax.rem(z + 1, nz),
    }
    ahead_of = {
        "y": lax.rem(y - jnp.where(down, 1, 0) + ny, ny), "z": lax.rem(z - 1 + nz, nz),
    }
    score_scale = dim ** (-0.5)

    x_in = pltpu.make_async_copy(x_ref, x_all.at[pl.ds(0, tokens)], local_sem.at[0])
    cot_in = pltpu.make_async_copy(cot_ref, cot, local_sem.at[1])
    w_in = [
        pltpu.make_async_copy(w.at[:, pl.ds(h * dim, dim)], w_all.at[at * heads + h], local_sem.at[2 + at * heads + h])
        for at, w in enumerate((wk_ref, wv_ref, wq_ref)) for h in range(heads)
    ]
    x_in.start()
    w_in[0].start()
    cot_in.start()

    barrier = pltpu.get_barrier_semaphore()
    partners = [other, after, ahead_of]
    partners += [{"z": lax.rem(z + j, nz)} for j in range(1, nz)]
    partners += [{"y": lax.rem(y + j, ny)} for j in range(1, ny)]
    for device in partners:
        pl.semaphore_signal(barrier, inc=1, device_id=device, device_id_type=MESH)

    def project(first, last):
        for c in range(first, last):
            w_in[c].wait()
        def body(c, carry):
            kvq[c] = dot_nn(x_all[pl.ds(0, tokens), :], w_all[c]).astype(jnp.bfloat16)
            return carry
        lax.fori_loop(first, last, body, 0)

    def halo_copy(src, dst, slot, device):
        return pltpu.make_async_remote_copy(
            src_ref=src, dst_ref=dst, send_sem=halo_sem.at[0, slot], recv_sem=halo_sem.at[1, slot],
            device_id=device, device_id_type=MESH,
        )

    key_out = [halo_copy(kvq.at[h], prev.at[h], h, after) for h in range(heads)]
    value_out = [halo_copy(kvq.at[heads + h], prev.at[heads + h], heads + h, after) for h in range(heads)]
    local_out = [
        halo_copy(grad_local.at[h], after_in.at[heads + h], 2 * heads + h, ahead_of) for h in range(heads)
    ]
    query_out = [halo_copy(kvq.at[2 * heads + h], after_in.at[h], 3 * heads + h, ahead_of) for h in range(heads)]
    stats_out = [halo_copy(stats.at[h], stats_in.at[h], 4 * heads + h, ahead_of) for h in range(heads)]

    def pair_copy(src, dst, slot):
        return pltpu.make_async_remote_copy(
            src_ref=src, dst_ref=dst, send_sem=pair_sem.at[0, slot], recv_sem=pair_sem.at[1, slot],
            device_id=other, device_id_type=MESH,
        )

    def each_head(body):
        def step(h, carry):
            body(h)
            return carry
        lax.fori_loop(0, heads, step, 0)

    def columns(h):
        return pl.ds(pl.multiple_of(h * dim, dim), dim)

    norm_scan = VectorScan(False, n1_own, n1_got, n1_yown, n1_ygot, nz_sem.at[0], ny_sem.at[0])
    grad_norm_scan = VectorScanDown(True, n2_own, n2_ygot, n2_zown, n2_zgot, ny_sem.at[1], nz_sem.at[1])
    memory_scan = MemoryScan(
        False, m1_parts, m1_got, m1_inside, m1_yown, m1_ygot, m1_back, m1_full,
        mz_sem.at[0], my_sem.at[0], mb_sem.at[0],
    )
    grad_memory_scan = MemoryScan(
        True, m2_parts, m2_got, m2_inside, m2_yown, m2_ygot, m2_back, m2_full,
        mz_sem.at[1], my_sem.at[1], mb_sem.at[1],
    )
    parts = nz // heads

    def put_parts(target, h, value):
        target[pl.ds(h * parts, parts)] = value.astype(jnp.bfloat16).reshape(parts, dim // parts, dim)

    def mixing_of(h):
        return 1.0 / (1.0 + jnp.exp(-jnp.full((1, dim), gate_ref[h], jnp.float32)))

    x_in.wait()
    for copy in w_in[1:]:
        copy.start()
    cot_in.wait()

    def local_gradient(h):
        upstream = cot[:, columns(h)].astype(jnp.float32)
        grad_local[h] = ((1.0 - mixing_of(h)) * upstream).astype(jnp.bfloat16)

    each_head(local_gradient)
    project(0, 1)
    pl.semaphore_wait(barrier, len(partners))
    key_out[0].start()
    local_out[0].start()
    project(1, heads)

    def key_sums(h):
        n1_own[h] = jnp.sum(feature(kvq[h].astype(jnp.float32)), axis=0, keepdims=True)

    each_head(key_sums)
    norm_scan.start()
    x_out = pair_copy(x_all.at[pl.ds(0, tokens)], x_all.at[pl.ds(tokens, tokens)], 0)
    x_out.start()
    project(heads, 2 * heads)

    def write(h):
        phi = feature(kvq[h].astype(jnp.float32)).astype(jnp.bfloat16)
        put_parts(m1_parts, h, dot_tn(phi, kvq[heads + h]))

    each_head(write)
    memory_scan.start()
    for h in range(1, heads):
        key_out[h].start()
        local_out[h].start()
    project(2 * heads, 3 * heads)
    norm_scan.across_rows()

    def own_part(h):
        row = lax.broadcasted_iota(jnp.int32, (tokens, tokens), 0)
        col = lax.broadcasted_iota(jnp.int32, (tokens, tokens), 1)
        scores[h] = jnp.where(col <= row, dot_nt(kvq[2 * heads + h], kvq[h]) * score_scale, MASKED)
        soft_grads[h] = dot_nt(grad_local[h], kvq[heads + h])

    each_head(own_part)
    norms[0] = norm_scan.result()

    def memory_gradient(h):
        phi = feature(kvq[2 * heads + h].astype(jnp.float32))
        divisor = jnp.sum(phi * norms[0, h], axis=1, keepdims=True) + 1.0
        den[h] = divisor
        grad_ret = mixing_of(h) * cot[:, columns(h)].astype(jnp.float32)
        number = (grad_ret / divisor).astype(jnp.bfloat16)
        grad_num[h] = number
        put_parts(m2_parts, h, dot_tn(phi.astype(jnp.bfloat16), number))

    each_head(memory_gradient)
    grad_memory_scan.start()
    value_out[0].start()
    query_out[0].start()
    memory_scan.across_rows()
    memory_scan.give_back()
    for h in range(1, heads):
        value_out[h].start()
        query_out[h].start()

    x_out.wait_recv()
    tile = min(wide, 256)

    def turn(i, carry):
        at = pl.ds(pl.multiple_of(i * tile, 128), tile)
        x_turned[at, :] = x_all[:, at].T
        return carry

    lax.fori_loop(0, x_all.shape[1] // tile, turn, 0)
    grad_memory_scan.across_rows()

    segment, last = y * nz + z, ny * nz - 1
    bias = jnp.where(segment > 0, 0.0, MASKED)
    bias_after = jnp.where(segment < last, 0.0, MASKED)

    def as_row(column):
        return jnp.broadcast_to(column, (tokens, 128)).T[:1]

    seen = set()

    def join(h, output, grad):
        kind = (h, output is None)
        if kind not in seen:
            seen.add(kind)
            if output is None:
                dq_att[h] = grad
            else:
                near_mix[h] = output
        elif output is None:
            grads[0, h] = (dq_att[h] + grad).astype(jnp.bfloat16)
        else:
            blended[:, columns(h)] = (near_mix[h] + output).astype(jnp.bfloat16)

    def attend(h):
        query, key, value = kvq[2 * heads + h], kvq[h], kvq[heads + h]
        key_prev, value_prev, local = prev[h], prev[heads + h], grad_local[h]
        s_own = scores[h]
        s_prev = dot_nt(query, key_prev) * score_scale + bias
        top = jnp.maximum(jnp.max(s_own, axis=1, keepdims=True), jnp.max(s_prev, axis=1, keepdims=True))
        e_own, e_prev = jnp.exp(s_own - top), jnp.exp(s_prev - top)
        inverse = 1.0 / (jnp.sum(e_own, axis=1, keepdims=True) + jnp.sum(e_prev, axis=1, keepdims=True))
        p_own, p_prev = e_own * inverse, e_prev * inverse
        b_own, b_prev = p_own.astype(jnp.bfloat16), p_prev.astype(jnp.bfloat16)
        near = dot_nn(b_own, value) + dot_nn(b_prev, value_prev)
        join(h, (1.0 - mixing_of(h)) * near, None)
        g_own, g_prev = soft_grads[h], dot_nt(local, value_prev)
        row_dot = jnp.sum(p_own * g_own, axis=1, keepdims=True) + jnp.sum(p_prev * g_prev, axis=1, keepdims=True)
        stats[h, 0:1] = as_row(top)
        stats[h, 1:2] = as_row(inverse)
        stats[h, 2:3] = as_row(row_dot)
        d_own = (p_own * (g_own - row_dot) * score_scale).astype(jnp.bfloat16)
        d_prev = (p_prev * (g_prev - row_dot) * score_scale).astype(jnp.bfloat16)
        own_grads[h] = dot_tn(d_own, query)
        own_grads[heads + h] = dot_tn(b_own, local)
        join(h, None, dot_nn(d_own, key) + dot_nn(d_prev, key_prev))

    for h in range(heads):
        stats[h] = jnp.zeros(stats.shape[1:], jnp.float32)
    def pair_grads(m):
        return pair_copy(grads.at[m, 1 - dp], g_all.at[m, pl.ds(tokens, tokens)], 1 + m)

    def keep_grads(m):
        g_all[m, pl.ds(0, tokens), :] = grads[m, dp]

    def products(m, target):
        at = pl.multiple_of(target * wide, 128)
        dw[m, target] = dot_nn(x_turned[pl.ds(at, wide), :], g_all[m])

    part = dim // 2

    def z_first(m, left, right):
        return lambda target, sub: dw[m, :, pl.ds(pl.multiple_of(target * block + sub * rows, 8), rows), left:right]

    def y_first(m, left, right):
        return lambda target, sub: dw[m, target, sub * (wide // 2):(sub + 1) * (wide // 2), left:right]

    def z_second(held):
        return lambda target, sub: held[pl.ds(pl.multiple_of(target * block + sub * rows, 8), rows), :]

    def ring(axis, slot, mine, send, recv):
        sem = (ring_z_sem if axis == "z" else ring_y_sem).at[slot]
        at = slot if axis == "z" else 4 + slot
        return RingSum(axis, mine, send, recv, ring_send_sem.at[at], sem)

    a1 = ring("z", 0, z_first(1, 0, dim), a1_send, a1_recv)
    b1 = ring("y", 0, y_first(2, 0, dim), b1_send, b1_recv)
    c1 = ring("z", 1, z_first(0, 0, part), c1_send, c1_recv)
    d1 = ring("y", 1, y_first(0, part, dim), d1_send, d1_recv)
    a2 = Spread("y", a2_recv, direct_sem.at[0])
    b2 = ring("z", 2, z_second(b_sum), b2_send, b2_recv)
    c2 = Spread("y", c2_recv, direct_sem.at[1])
    d2 = ring("z", 3, z_second(d_sum), d2_send, d2_recv)

    def columns_in(sums, held):
        for sub in (0, 1):
            held[sub] = sums.total(sub)

    def send_parts(spread, held, parts):
        for j in range(1, ny):
            parts[j] = held[:, lax.rem(y + j, ny)].astype(jnp.bfloat16)
            spread.copy(parts.at[j], j).start()

    def direct_total(spread, held):
        spread.all_copy().wait_recv()
        value = held[:, y]
        for j in range(1, ny):
            value = value + spread.got[j].astype(jnp.float32)
        return value

    def multiply(m):
        for k in range(ny):
            products(m, k)

    def first_hop(sums):
        for ahead in range(ny):
            sums.step(0, ny // 2 + ahead)


    def rows_in(sums, held):
        for sub in (0, 1):
            held[sub * (wide // 2):(sub + 1) * (wide // 2), :] = sums.total(sub)

    def serve(h):
        query, local = after_in[h], after_in[heads + h]
        top, inverse, row_dot = stats_in[h, 0:1], stats_in[h, 1:2], stats_in[h, 2:3]
        soft = jnp.exp(dot_nt(kvq[h], query) * score_scale + bias_after - top) * inverse
        given = (soft * (dot_nt(kvq[heads + h], local) - row_dot) * score_scale).astype(jnp.bfloat16)
        own_grads[h] += dot_nn(given, query)
        own_grads[heads + h] += dot_nn(soft.astype(jnp.bfloat16), local)

    def retrieve(h):
        mixing = mixing_of(h)
        query = kvq[2 * heads + h].astype(jnp.float32)
        phi = feature(query)
        memory = memory_scan.head(h, heads)
        retrieved = dot_nn(phi.astype(jnp.bfloat16), memory) / den[h]
        join(h, mixing * retrieved, None)
        grad_ret = mixing * cot[:, columns(h)].astype(jnp.float32)
        grad_den = -jnp.sum(grad_ret * retrieved, axis=1, keepdims=True) / den[h]
        n2_own[h] = jnp.sum(grad_den * phi, axis=0, keepdims=True)
        grad_phi = dot_nt(grad_num[h], memory) + grad_den * norms[0, h]
        join(h, None, grad_phi * feature_slope(query))

    def attend_now(h):
        key_out[h].wait_recv()
        value_out[h].wait_recv()
        attend(h)
        stats_out[h].start()

    def serve_now(h):
        query_out[h].wait_recv()
        local_out[h].wait_recv()
        stats_out[h].wait_recv()
        serve(h)

    for h in range(heads - 1):
        attend_now(h)
    grad_memory_scan.give_back()
    memory_scan.finish()
    for h in range(heads):
        retrieve(h)
    grad_norm_scan.start()
    attend_now(heads - 1)
    query_pair = pair_grads(0)
    query_pair.start()
    keep_grads(0)
    grad_norm_scan.across_columns()
    blended_out = pltpu.make_async_copy(blended, blended_ref, out_sem.at[2])
    blended_out.start()
    for h in range(heads - 1):
        serve_now(h)
    query_pair.wait_recv()
    multiply(0)
    c1.step(0)
    first_hop(d1)
    serve_now(heads - 1)
    grad_memory_scan.finish()
    norms[1] = grad_norm_scan.result()

    def write_key(h):
        grad_phi = dot_nt(kvq[heads + h], grad_memory_scan.head(h, heads)) + norms[1, h]
        slope = feature_slope(kvq[h].astype(jnp.float32))
        grads[1, h] = (own_grads[h] + grad_phi * slope).astype(jnp.bfloat16)

    def write_value(h):
        phi = feature(kvq[h].astype(jnp.float32)).astype(jnp.bfloat16)
        grads[2, h] = (own_grads[heads + h] + dot_nn(phi, grad_memory_scan.head(h, heads))).astype(jnp.bfloat16)

    key_pair, value_pair = pair_grads(1), pair_grads(2)
    write_key(1 - dp)
    key_pair.start()
    write_key(dp)
    write_value(1 - dp)
    value_pair.start()
    write_value(dp)
    keep_grads(1)
    keep_grads(2)
    c1.step(1)
    d1.step(1)
    key_pair.wait_recv()
    multiply(1)
    a1.step(0)
    value_pair.wait_recv()
    multiply(2)
    first_hop(b1)
    c1.step(2)
    rows_in(d1, d_sum)
    d2.step(0)
    a1.step(1)
    b1.step(1)
    c1.step(3)
    d2.step(1)
    a1.step(2)
    columns_in(c1, c_sum)
    send_parts(c2, c_sum, c2_send)
    d2.step(2)
    rows_in(b1, b_sum)
    b2.step(0)
    a1.step(3)
    d2.step(3)
    b2.step(1)
    columns_in(a1, a_sum)
    send_parts(a2, a_sum, a2_send)
    b2.step(2)

    def put(src, m, place, slot):
        return pltpu.make_async_copy(
            src.at[:, pl.ds(m * dim, dim)], out_ref.at[m, :, columns(place)], out_sem.at[slot]
        )

    swaps = [
        pair_copy(fin.at[1 - dp, :, pl.ds(m * dim, dim)], swap.at[:, pl.ds(m * dim, dim)], 4 + m) for m in range(3)
    ]

    def hand_over(m):
        swaps[m].start()
        put(fin.at[dp], m, dp, 0).start()

    fin[:, :, 0:part] = direct_total(c2, c_sum) * scale
    for sub in (0, 1):
        fin[sub, :, part:dim] = d2.total(sub) * scale
    hand_over(0)
    b2.step(3)
    fin[:, :, dim:2 * dim] = direct_total(a2, a_sum) * scale
    hand_over(1)
    for sub in (0, 1):
        fin[sub, :, 2 * dim:3 * dim] = b2.total(sub) * scale
    hand_over(2)
    for sent in (
        a1, b1, c1, d1, a2, b2, c2, d2, norm_scan, grad_norm_scan, memory_scan, grad_memory_scan,
    ):
        sent.drain()
    for copy in (*key_out, *value_out, *local_out, *query_out, *stats_out, x_out, query_pair, key_pair, value_pair):
        copy.wait_send()
    for m in range(3):
        swaps[m].wait_recv()
        put(swap, m, 1 - dp, 1).start()
    for m in range(3):
        swaps[m].wait_send()
    blended_out.wait()
    for slot in (0, 1):
        pltpu.make_async_copy(fin.at[slot], swap, out_sem.at[slot]).wait()


def layer(x, wq, wk, wv, gate, cot, scale):
    tokens, depth = x.shape
    heads = gate.shape[0]
    dim = wq.shape[1] // heads
    ny, nz = lax.axis_size("y"), lax.axis_size("z")
    wide = depth // ny
    rows = wide // nz // 2
    zs, ys = 2 * (nz - 1), 2 * (ny - 1)
    wire = lambda *shape: pltpu.VMEM(shape, jnp.bfloat16)
    real = lambda *shape: pltpu.VMEM(shape, jnp.float32)
    dma = lambda *shape: pltpu.SemaphoreType.DMA(shape)
    a1, b1 = (zs, ny, rows), (ys, wide // 2)
    part = (heads * dim // nz, dim)
    vectors = [real(heads, 1, dim), real(nz, heads, 1, dim), real(heads, 1, dim), real(ny, heads, 1, dim)]
    scan = [
        wire(nz, *part), wire(nz, *part), real(nz, *part), real(*part), real(ny, *part), wire(nz, *part),
        wire(nz, *part),
    ]
    pair = (2 * heads, tokens, dim)
    anywhere = pl.BlockSpec(memory_space=pl.ANY)
    return pl.pallas_call(
        functools.partial(layer_kernel, scale),
        out_shape=(
            jax.ShapeDtypeStruct((tokens, heads * dim), jnp.bfloat16),
            jax.ShapeDtypeStruct((3, rows, heads * dim), jnp.float32),
        ),
        in_specs=[anywhere] * 4 + [pl.BlockSpec(memory_space=pltpu.SMEM), anywhere],
        out_specs=(anywhere,) * 2,
        scratch_shapes=[
            wire(2 * tokens, depth), wire(depth, 2 * tokens), wire(3 * heads, depth, dim), wire(tokens, heads * dim), wire(tokens, heads * dim),
            wire(3 * heads, tokens, dim), wire(*pair), wire(*pair), real(*pair),
            real(heads, tokens, dim), real(heads, tokens, dim),
            real(heads, tokens, tokens), real(heads, tokens, tokens), wire(heads, tokens, dim),
            wire(heads, tokens, dim), real(heads, tokens, 1), real(heads, 8, tokens), real(heads, 8, tokens),
            wire(3, heads, tokens, dim), wire(3, 2 * tokens, dim),
            *vectors, real(heads, 1, dim), real(ny, heads, 1, dim), real(2, heads, 1, dim), real(nz, 2, heads, 1, dim),
            real(2, heads, 1, dim), *scan, *scan,
            real(3, ny, wide, dim), real(2, ny, rows, dim), real(wide, dim), real(2, ny, rows, dim // 2), real(wide, dim // 2),
            real(2, rows, 3 * dim), real(rows, 3 * dim),
            wire(*a1, dim), wire(*a1, dim), wire(*b1, dim), wire(*b1, dim),
            wire(*a1, dim // 2), wire(*a1, dim // 2), wire(*b1, dim // 2), wire(*b1, dim // 2),
            wire(ny, 2, rows, dim), wire(ny, 2, rows, dim), wire(zs, rows, dim), wire(zs, rows, dim),
            wire(ny, 2, rows, dim // 2), wire(ny, 2, rows, dim // 2), wire(zs, rows, dim // 2), wire(zs, rows, dim // 2),
            dma(2 + 3 * heads), dma(2, 5 * heads), dma(2, 7), dma(2, 2), dma(2, 2),
            dma(2, 2), dma(2, 2), dma(2, 2),
            dma(4, zs), dma(2, ys), dma(8), dma(2, 2), dma(3),
        ],
        compiler_params=pltpu.CompilerParams(
            collective_id=1, has_side_effects=True, vmem_limit_bytes=63 * 1024 * 1024
        ),
    )(x, wq, wk, wv, gate, cot)


def hand_on_kernel(a_ref, b_ref, a_out, b_out, a_held, b_held, sem):
    size = a_ref.shape[0] // PIECES
    whole = [(b_ref.at[m], b_held.at[m], b_out.at[m]) for m in range(b_ref.shape[0])]
    whole += [tuple(ref.at[pl.ds(i * size, size)] for ref in (a_ref, a_held, a_out)) for i in range(PIECES)]
    reads = [pltpu.make_async_copy(src, held, sem.at[0, i]) for i, (src, held, _) in enumerate(whole)]
    writes = [pltpu.make_async_copy(held, dst, sem.at[1, i]) for i, (_, held, dst) in enumerate(whole)]
    for read in reads:
        read.start()
    for read, write in zip(reads, writes):
        read.wait()
        write.start()
    for write in writes:
        write.wait()


def hand_on(a, b):
    anywhere = pl.BlockSpec(memory_space=pl.ANY)
    return pl.pallas_call(
        hand_on_kernel,
        out_shape=tuple(jax.ShapeDtypeStruct(v.shape, v.dtype) for v in (a, b)),
        in_specs=[anywhere] * 2,
        out_specs=(anywhere,) * 2,
        scratch_shapes=[pltpu.VMEM(v.shape, v.dtype) for v in (a, b)]
        + [pltpu.SemaphoreType.DMA((2, PIECES + b.shape[0]))],
    )(a, b)


def local(inputs, w_query, w_key, w_value, gate_bias, cotangent):
    tokens = inputs[0]
    seg_len = tokens.shape[0]
    scale = 1.0 / math.sqrt(lax.axis_size(SEQ) * lax.axis_size("dp") * seg_len)
    blended, grad_weights = layer(tokens, w_query, w_key, w_value, gate_bias, cotangent[0], scale)
    blended, grad_weights = hand_on(blended, grad_weights)
    return (blended[None], grad_weights.transpose(1, 0, 2))


def solution(mesh):
    finer = Mesh(
        mesh.devices.reshape(4, 8, mesh.shape["dp"], mesh.shape["head"]),
        ("y", "z", "dp", "head"),
    )
    placed = (
        P("dp", SEQ, None),
        P(None, "head"),
        P(None, "head"),
        P(None, "head"),
        P("head"),
        P("dp", SEQ, "head"),
    )
    return jax.shard_map(
        local,
        mesh=finer,
        in_specs=placed,
        out_specs=(P("dp", SEQ, "head"), P(SEQ_DP, None, "head")),
        check_vma=False,
    )
```

```python
import functools
import math

import jax
import jax.numpy as jnp
from jax import lax
from jax.experimental import pallas as pl
from jax.experimental.pallas import tpu as pltpu
from jax.sharding import Mesh
from jax.sharding import PartitionSpec as P

SEQ = ("y", "z")
SEQ_DP = ("y", "z", "dp")
MESH = pl.DeviceIdType.MESH
MASKED = -1e30
PIECES = 4


def feature(u):
    return jnp.where(u > 0, u + 1.0, jnp.exp(jnp.minimum(u, 0.0)))


def feature_slope(u):
    return jnp.where(u > 0, 1.0, jnp.exp(jnp.minimum(u, 0.0)))


def contract(a, b, over_a, over_b):
    return lax.dot_general(
        a, b, (((over_a,), (over_b,)), ((), ())), preferred_element_type=jnp.float32
    )


def dot_nn(a, b):
    return contract(a, b, 1, 0)


def dot_nt(a, b):
    return contract(a, b, 1, 1)


def dot_tn(a, b):
    return contract(a, b, 0, 0)


def ring_chains(n):
    chains, first = [], 0
    for sub in (0, 1):
        for way in (1, -1):
            length = n // 2 if (way > 0) == (sub == 0) else n - 1 - n // 2
            chains.append((sub, way, length, first))
            first += length
    return chains


class RingSum:
    def __init__(self, axis, mine, send, recv, send_sem, recv_sem):
        self.axis, self.mine = axis, mine
        self.n, self.position = lax.axis_size(axis), lax.axis_index(axis)
        self.send, self.recv, self.send_sem, self.recv_sem = send, recv, send_sem, recv_sem
        self.chains = ring_chains(self.n)

    def copy(self, slot, way):
        return pltpu.make_async_remote_copy(
            src_ref=self.send.at[slot],
            dst_ref=self.recv.at[slot],
            send_sem=self.send_sem,
            recv_sem=self.recv_sem.at[slot],
            device_id={self.axis: lax.rem(self.position + way + self.n, self.n)},
            device_id_type=MESH,
        )

    def step(self, t, ahead=None):
        for sub, way, length, first in self.chains:
            if t >= length:
                continue
            if ahead is not None and (way * (length - t)) % self.n != ahead % self.n:
                continue
            target = lax.rem(self.position + way * (length - t) + self.n, self.n)
            value = self.mine(target, sub)
            if t:
                self.copy(first + t - 1, way).wait_recv()
                value = value + self.recv[first + t - 1].astype(jnp.float32)
            self.send[first + t] = value.astype(jnp.bfloat16)
            self.copy(first + t, way).start()

    def total(self, sub):
        value = self.mine(self.position, sub)
        for chain_sub, way, length, first in self.chains:
            if chain_sub == sub and length:
                self.copy(first + length - 1, way).wait_recv()
                value = value + self.recv[first + length - 1].astype(jnp.float32)
        return value

    def drain(self):
        self.all_copy().wait_send()

    def all_copy(self):
        return pltpu.make_async_remote_copy(
            src_ref=self.send, dst_ref=self.recv, send_sem=self.send_sem, recv_sem=self.recv_sem.at[0],
            device_id={self.axis: self.position}, device_id_type=MESH,
        )


class Spread:
    def __init__(self, axis, got, sem):
        self.axis, self.got, self.sem = axis, got, sem
        self.n, self.position = lax.axis_size(axis), lax.axis_index(axis)

    def copy(self, src, j):
        return pltpu.make_async_remote_copy(
            src_ref=src,
            dst_ref=self.got.at[j],
            send_sem=self.sem.at[0],
            recv_sem=self.sem.at[1],
            device_id={self.axis: lax.rem(self.position + j, self.n)},
            device_id_type=MESH,
        )

    def all_copy(self):
        others = self.got.at[pl.ds(1, self.n - 1)]
        return pltpu.make_async_remote_copy(
            src_ref=others, dst_ref=others, send_sem=self.sem.at[0], recv_sem=self.sem.at[1],
            device_id={self.axis: self.position}, device_id_type=MESH,
        )

    def start(self, src):
        for j in range(1, self.n):
            self.copy(src, j).start()

    def sums(self, own, reverse):
        passed, total = jnp.zeros_like(own), own
        self.all_copy().wait_recv()
        for j in range(1, self.n):
            value = self.got[j]
            earlier = self.position < j if reverse else self.position >= j
            passed = passed + value * jnp.where(earlier, 1.0, 0.0)
            total = total + value
        return passed, total

    def drain(self):
        self.all_copy().wait_send()


class VectorScan:
    def __init__(self, reverse, own, z_got, y_own, y_got, z_sem, y_sem):
        self.reverse, self.own, self.y_own = reverse, own, y_own
        self.z, self.y = Spread("z", z_got, z_sem), Spread("y", y_got, y_sem)

    def start(self):
        self.z.start(self.own)

    def across_rows(self):
        self.inside, total = self.z.sums(self.own[...], self.reverse)
        self.y_own[...] = total
        self.y.start(self.y_own)

    def result(self):
        passed, _ = self.y.sums(self.y_own[...], self.reverse)
        return passed + self.inside

    def drain(self):
        self.z.drain()
        self.y.drain()


class VectorScanDown:
    def __init__(self, reverse, own, y_got, z_own, z_got, y_sem, z_sem):
        self.reverse, self.own, self.z_own = reverse, own, z_own
        self.y, self.z = Spread("y", y_got, y_sem), Spread("z", z_got, z_sem)

    def start(self):
        self.y.start(self.own)

    def across_columns(self):
        passed, _ = self.y.sums(self.own[...], self.reverse)
        self.z_own[0] = self.own[...]
        self.z_own[1] = passed
        self.z.start(self.z_own)

    def result(self):
        passed, total = self.z.sums(self.z_own[...], self.reverse)
        return passed[0] + total[1]

    def drain(self):
        self.y.drain()
        self.z.drain()


class MemoryScan:
    def __init__(self, reverse, parts, got, inside, y_own, y_got, back, result, z_sem, y_sem, back_sem):
        self.reverse, self.parts, self.got, self.inside, self.y_own = reverse, parts, got, inside, y_own
        self.back, self.full, self.z_sem, self.back_sem = back, result, z_sem, back_sem
        self.n, self.position = lax.axis_size("z"), lax.axis_index("z")
        self.y = Spread("y", y_got, y_sem)

    def out_copy(self, j):
        target = lax.rem(self.position + j, self.n)
        return pltpu.make_async_remote_copy(
            src_ref=self.parts.at[target],
            dst_ref=self.got.at[j],
            send_sem=self.z_sem.at[0],
            recv_sem=self.z_sem.at[1],
            device_id={"z": target},
            device_id_type=MESH,
        )

    def back_copy(self, j):
        target = lax.rem(self.position + j, self.n)
        return pltpu.make_async_remote_copy(
            src_ref=self.back.at[target],
            dst_ref=self.full.at[self.position],
            send_sem=self.back_sem.at[0],
            recv_sem=self.back_sem.at[1],
            device_id={"z": target},
            device_id_type=MESH,
        )

    def start(self):
        for j in range(1, self.n):
            self.out_copy(j).start()

    def across_rows(self):
        self.all_copy(self.z_sem).wait_recv()
        self.got[0] = self.parts[self.position]
        run = jnp.zeros(self.y_own.shape, jnp.float32)
        for k in reversed(range(self.n)) if self.reverse else range(self.n):
            self.inside[k] = run
            run = run + self.got[lax.rem(self.position - k + self.n, self.n)].astype(jnp.float32)
        self.y_own[...] = run
        self.y.start(self.y_own)

    def give_back(self):
        passed, _ = self.y.sums(self.y_own[...], self.reverse)
        for k in range(self.n):
            self.back[k] = (self.inside[k] + passed).astype(jnp.bfloat16)
        for j in range(1, self.n):
            self.back_copy(j).start()
        self.full[self.position] = self.back[self.position]

    def finish(self):
        self.all_copy(self.back_sem).wait_recv()

    def head(self, h, heads):
        parts = self.n // heads
        block = self.full[pl.ds(h * parts, parts)]
        return block.reshape(parts * block.shape[1], block.shape[2])

    def drain(self):
        self.y.drain()
        self.all_copy(self.z_sem).wait_send()
        self.all_copy(self.back_sem).wait_send()

    def all_copy(self, sem):
        others = self.got.at[pl.ds(1, self.n - 1)]
        return pltpu.make_async_remote_copy(
            src_ref=others, dst_ref=others, send_sem=sem.at[0], recv_sem=sem.at[1],
            device_id={"z": self.position}, device_id_type=MESH,
        )


def layer_kernel(
    scale, x_ref, wq_ref, wk_ref, wv_ref, gate_ref, cot_ref, blended_ref, out_ref,
    x_all, x_turned, w_all, cot, blended, kvq, prev, after_in, own_grads, dq_att, near_mix,
    scores, soft_grads, grad_local, grad_num, den, stats, stats_in, grads, g_all,
    n1_own, n1_got, n1_yown, n1_ygot, n2_own, n2_ygot, n2_zown, n2_zgot, norms,
    m1_parts, m1_got, m1_inside, m1_yown, m1_ygot, m1_back, m1_full,
    m2_parts, m2_got, m2_inside, m2_yown, m2_ygot, m2_back, m2_full,
    dw, a_sum, b_sum, c_sum, d_sum, fin, swap,
    a1_send, a1_recv, b1_send, b1_recv, c1_send, c1_recv, d1_send, d1_recv,
    a2_send, a2_recv, b2_send, b2_recv, c2_send, c2_recv, d2_send, d2_recv,
    local_sem, halo_sem, pair_sem, nz_sem, ny_sem, mz_sem, my_sem, mb_sem, ring_z_sem, ring_y_sem, ring_send_sem, direct_sem, out_sem,
):
    ny, nz = lax.axis_size("y"), lax.axis_size("z")
    y, z, dp = lax.axis_index("y"), lax.axis_index("z"), lax.axis_index("dp")
    other = {"dp": 1 - dp}
    tokens = x_ref.shape[0]
    heads, dim = kvq.shape[0] // 3, kvq.shape[2]
    wide = dw.shape[2]
    block = wide // nz
    rows = block // 2
    up, down = z == nz - 1, z == 0
    after = {
        "y": lax.rem(y + jnp.where(up, 1, 0), ny), "z": lax.rem(z + 1, nz),
    }
    ahead_of = {
        "y": lax.rem(y - jnp.where(down, 1, 0) + ny, ny), "z": lax.rem(z - 1 + nz, nz),
    }
    score_scale = dim ** (-0.5)

    x_in = pltpu.make_async_copy(x_ref, x_all.at[pl.ds(0, tokens)], local_sem.at[0])
    cot_in = pltpu.make_async_copy(cot_ref, cot, local_sem.at[1])
    w_in = [
        pltpu.make_async_copy(w.at[:, pl.ds(h * dim, dim)], w_all.at[at * heads + h], local_sem.at[2 + at * heads + h])
        for at, w in enumerate((wk_ref, wv_ref, wq_ref)) for h in range(heads)
    ]
    x_in.start()
    w_in[0].start()
    cot_in.start()

    barrier = pltpu.get_barrier_semaphore()
    partners = [other, after, ahead_of]
    partners += [{"z": lax.rem(z + j, nz)} for j in range(1, nz)]
    partners += [{"y": lax.rem(y + j, ny)} for j in range(1, ny)]
    for device in partners:
        pl.semaphore_signal(barrier, inc=1, device_id=device, device_id_type=MESH)

    def project(first, last):
        for c in range(first, last):
            w_in[c].wait()
        def body(c, carry):
            kvq[c] = dot_nn(x_all[pl.ds(0, tokens), :], w_all[c]).astype(jnp.bfloat16)
            return carry
        lax.fori_loop(first, last, body, 0)

    def halo_copy(src, dst, slot, device):
        return pltpu.make_async_remote_copy(
            src_ref=src, dst_ref=dst, send_sem=halo_sem.at[0, slot], recv_sem=halo_sem.at[1, slot],
            device_id=device, device_id_type=MESH,
        )

    key_out = [halo_copy(kvq.at[h], prev.at[h], h, after) for h in range(heads)]
    value_out = [halo_copy(kvq.at[heads + h], prev.at[heads + h], heads + h, after) for h in range(heads)]
    local_out = [
        halo_copy(grad_local.at[h], after_in.at[heads + h], 2 * heads + h, ahead_of) for h in range(heads)
    ]
    query_out = [halo_copy(kvq.at[2 * heads + h], after_in.at[h], 3 * heads + h, ahead_of) for h in range(heads)]
    stats_out = [halo_copy(stats.at[h], stats_in.at[h], 4 * heads + h, ahead_of) for h in range(heads)]

    def pair_copy(src, dst, slot):
        return pltpu.make_async_remote_copy(
            src_ref=src, dst_ref=dst, send_sem=pair_sem.at[0, slot], recv_sem=pair_sem.at[1, slot],
            device_id=other, device_id_type=MESH,
        )

    def each_head(body):
        def step(h, carry):
            body(h)
            return carry
        lax.fori_loop(0, heads, step, 0)

    def columns(h):
        return pl.ds(pl.multiple_of(h * dim, dim), dim)

    norm_scan = VectorScan(False, n1_own, n1_got, n1_yown, n1_ygot, nz_sem.at[0], ny_sem.at[0])
    grad_norm_scan = VectorScanDown(True, n2_own, n2_ygot, n2_zown, n2_zgot, ny_sem.at[1], nz_sem.at[1])
    memory_scan = MemoryScan(
        False, m1_parts, m1_got, m1_inside, m1_yown, m1_ygot, m1_back, m1_full,
        mz_sem.at[0], my_sem.at[0], mb_sem.at[0],
    )
    grad_memory_scan = MemoryScan(
        True, m2_parts, m2_got, m2_inside, m2_yown, m2_ygot, m2_back, m2_full,
        mz_sem.at[1], my_sem.at[1], mb_sem.at[1],
    )
    parts = nz // heads

    def put_parts(target, h, value):
        target[pl.ds(h * parts, parts)] = value.astype(jnp.bfloat16).reshape(parts, dim // parts, dim)

    def mixing_of(h):
        return 1.0 / (1.0 + jnp.exp(-jnp.full((1, dim), gate_ref[h], jnp.float32)))

    x_in.wait()
    for copy in w_in[1:]:
        copy.start()
    cot_in.wait()

    def local_gradient(h):
        upstream = cot[:, columns(h)].astype(jnp.float32)
        grad_local[h] = ((1.0 - mixing_of(h)) * upstream).astype(jnp.bfloat16)

    each_head(local_gradient)
    project(0, 1)
    pl.semaphore_wait(barrier, len(partners))
    key_out[0].start()
    local_out[0].start()
    project(1, heads)

    def key_sums(h):
        n1_own[h] = jnp.sum(feature(kvq[h].astype(jnp.float32)), axis=0, keepdims=True)

    each_head(key_sums)
    norm_scan.start()
    x_out = pair_copy(x_all.at[pl.ds(0, tokens)], x_all.at[pl.ds(tokens, tokens)], 0)
    x_out.start()
    project(heads, 2 * heads)

    def write(h):
        phi = feature(kvq[h].astype(jnp.float32)).astype(jnp.bfloat16)
        put_parts(m1_parts, h, dot_tn(phi, kvq[heads + h]))

    each_head(write)
    memory_scan.start()
    for h in range(1, heads):
        key_out[h].start()
        local_out[h].start()
    project(2 * heads, 3 * heads)
    norm_scan.across_rows()

    def own_part(h):
        row = lax.broadcasted_iota(jnp.int32, (tokens, tokens), 0)
        col = lax.broadcasted_iota(jnp.int32, (tokens, tokens), 1)
        scores[h] = jnp.where(col <= row, dot_nt(kvq[2 * heads + h], kvq[h]) * score_scale, MASKED)
        soft_grads[h] = dot_nt(grad_local[h], kvq[heads + h])

    each_head(own_part)
    norms[0] = norm_scan.result()

    def memory_gradient(h):
        phi = feature(kvq[2 * heads + h].astype(jnp.float32))
        divisor = jnp.sum(phi * norms[0, h], axis=1, keepdims=True) + 1.0
        den[h] = divisor
        grad_ret = mixing_of(h) * cot[:, columns(h)].astype(jnp.float32)
        number = (grad_ret / divisor).astype(jnp.bfloat16)
        grad_num[h] = number
        put_parts(m2_parts, h, dot_tn(phi.astype(jnp.bfloat16), number))

    each_head(memory_gradient)
    grad_memory_scan.start()
    value_out[0].start()
    query_out[0].start()
    memory_scan.across_rows()
    memory_scan.give_back()
    for h in range(1, heads):
        value_out[h].start()
        query_out[h].start()

    x_out.wait_recv()
    tile = min(wide, 256)

    def turn(i, carry):
        at = pl.ds(pl.multiple_of(i * tile, 128), tile)
        x_turned[at, :] = x_all[:, at].T
        return carry

    lax.fori_loop(0, x_all.shape[1] // tile, turn, 0)
    grad_memory_scan.across_rows()

    segment, last = y * nz + z, ny * nz - 1
    bias = jnp.where(segment > 0, 0.0, MASKED)
    bias_after = jnp.where(segment < last, 0.0, MASKED)

    def as_row(column):
        return jnp.broadcast_to(column, (tokens, 128)).T[:1]

    seen = set()

    def join(h, output, grad):
        kind = (h, output is None)
        if kind not in seen:
            seen.add(kind)
            if output is None:
                dq_att[h] = grad
            else:
                near_mix[h] = output
        elif output is None:
            grads[0, h] = (dq_att[h] + grad).astype(jnp.bfloat16)
        else:
            blended[:, columns(h)] = (near_mix[h] + output).astype(jnp.bfloat16)

    def attend(h):
        query, key, value = kvq[2 * heads + h], kvq[h], kvq[heads + h]
        key_prev, value_prev, local = prev[h], prev[heads + h], grad_local[h]
        s_own = scores[h]
        s_prev = dot_nt(query, key_prev) * score_scale + bias
        top = jnp.maximum(jnp.max(s_own, axis=1, keepdims=True), jnp.max(s_prev, axis=1, keepdims=True))
        e_own, e_prev = jnp.exp(s_own - top), jnp.exp(s_prev - top)
        inverse = 1.0 / (jnp.sum(e_own, axis=1, keepdims=True) + jnp.sum(e_prev, axis=1, keepdims=True))
        p_own, p_prev = e_own * inverse, e_prev * inverse
        b_own, b_prev = p_own.astype(jnp.bfloat16), p_prev.astype(jnp.bfloat16)
        near = dot_nn(b_own, value) + dot_nn(b_prev, value_prev)
        join(h, (1.0 - mixing_of(h)) * near, None)
        g_own, g_prev = soft_grads[h], dot_nt(local, value_prev)
        row_dot = jnp.sum(p_own * g_own, axis=1, keepdims=True) + jnp.sum(p_prev * g_prev, axis=1, keepdims=True)
        stats[h, 0:1] = as_row(top)
        stats[h, 1:2] = as_row(inverse)
        stats[h, 2:3] = as_row(row_dot)
        d_own = (p_own * (g_own - row_dot) * score_scale).astype(jnp.bfloat16)
        d_prev = (p_prev * (g_prev - row_dot) * score_scale).astype(jnp.bfloat16)
        own_grads[h] = dot_tn(d_own, query)
        own_grads[heads + h] = dot_tn(b_own, local)
        join(h, None, dot_nn(d_own, key) + dot_nn(d_prev, key_prev))

    for h in range(heads):
        stats[h] = jnp.zeros(stats.shape[1:], jnp.float32)
    def pair_grads(m):
        return pair_copy(grads.at[m, 1 - dp], g_all.at[m, pl.ds(tokens, tokens)], 1 + m)

    def keep_grads(m):
        g_all[m, pl.ds(0, tokens), :] = grads[m, dp]

    def products(m, target):
        at = pl.multiple_of(target * wide, 128)
        dw[m, target] = dot_nn(x_turned[pl.ds(at, wide), :], g_all[m])

    part = dim // 2

    def z_first(m, left, right):
        return lambda target, sub: dw[m, :, pl.ds(pl.multiple_of(target * block + sub * rows, 8), rows), left:right]

    def y_first(m, left, right):
        return lambda target, sub: dw[m, target, sub * (wide // 2):(sub + 1) * (wide // 2), left:right]

    def z_second(held):
        return lambda target, sub: held[pl.ds(pl.multiple_of(target * block + sub * rows, 8), rows), :]

    def ring(axis, slot, mine, send, recv):
        sem = (ring_z_sem if axis == "z" else ring_y_sem).at[slot]
        at = slot if axis == "z" else 4 + slot
        return RingSum(axis, mine, send, recv, ring_send_sem.at[at], sem)

    a1 = ring("z", 0, z_first(1, 0, dim), a1_send, a1_recv)
    b1 = ring("y", 0, y_first(2, 0, dim), b1_send, b1_recv)
    c1 = ring("z", 1, z_first(0, 0, part), c1_send, c1_recv)
    d1 = ring("y", 1, y_first(0, part, dim), d1_send, d1_recv)
    a2 = Spread("y", a2_recv, direct_sem.at[0])
    b2 = ring("z", 2, z_second(b_sum), b2_send, b2_recv)
    c2 = Spread("y", c2_recv, direct_sem.at[1])
    d2 = ring("z", 3, z_second(d_sum), d2_send, d2_recv)

    def columns_in(sums, held):
        for sub in (0, 1):
            held[sub] = sums.total(sub)

    def send_parts(spread, held, parts):
        for j in range(1, ny):
            parts[j] = held[:, lax.rem(y + j, ny)].astype(jnp.bfloat16)
            spread.copy(parts.at[j], j).start()

    def direct_total(spread, held):
        spread.all_copy().wait_recv()
        value = held[:, y]
        for j in range(1, ny):
            value = value + spread.got[j].astype(jnp.float32)
        return value

    def multiply(m):
        for k in range(ny):
            products(m, k)

    def first_hop(sums):
        for ahead in range(ny):
            sums.step(0, ny // 2 + ahead)


    def rows_in(sums, held):
        for sub in (0, 1):
            held[sub * (wide // 2):(sub + 1) * (wide // 2), :] = sums.total(sub)

    def serve(h):
        query, local = after_in[h], after_in[heads + h]
        top, inverse, row_dot = stats_in[h, 0:1], stats_in[h, 1:2], stats_in[h, 2:3]
        soft = jnp.exp(dot_nt(kvq[h], query) * score_scale + bias_after - top) * inverse
        given = (soft * (dot_nt(kvq[heads + h], local) - row_dot) * score_scale).astype(jnp.bfloat16)
        own_grads[h] += dot_nn(given, query)
        own_grads[heads + h] += dot_nn(soft.astype(jnp.bfloat16), local)

    def retrieve(h):
        mixing = mixing_of(h)
        query = kvq[2 * heads + h].astype(jnp.float32)
        phi = feature(query)
        memory = memory_scan.head(h, heads)
        retrieved = dot_nn(phi.astype(jnp.bfloat16), memory) / den[h]
        join(h, mixing * retrieved, None)
        grad_ret = mixing * cot[:, columns(h)].astype(jnp.float32)
        grad_den = -jnp.sum(grad_ret * retrieved, axis=1, keepdims=True) / den[h]
        n2_own[h] = jnp.sum(grad_den * phi, axis=0, keepdims=True)
        grad_phi = dot_nt(grad_num[h], memory) + grad_den * norms[0, h]
        join(h, None, grad_phi * feature_slope(query))

    def attend_now(h):
        key_out[h].wait_recv()
        value_out[h].wait_recv()
        attend(h)
        stats_out[h].start()

    def serve_now(h):
        query_out[h].wait_recv()
        local_out[h].wait_recv()
        stats_out[h].wait_recv()
        serve(h)

    for h in range(heads - 1):
        attend_now(h)
    grad_memory_scan.give_back()
    memory_scan.finish()
    for h in range(heads):
        retrieve(h)
    grad_norm_scan.start()
    attend_now(heads - 1)
    query_pair = pair_grads(0)
    query_pair.start()
    keep_grads(0)
    grad_norm_scan.across_columns()
    blended_out = pltpu.make_async_copy(blended, blended_ref, out_sem.at[2])
    blended_out.start()
    for h in range(heads - 1):
        serve_now(h)
    query_pair.wait_recv()
    multiply(0)
    c1.step(0)
    first_hop(d1)
    serve_now(heads - 1)
    grad_memory_scan.finish()
    norms[1] = grad_norm_scan.result()

    def write_key(h):
        grad_phi = dot_nt(kvq[heads + h], grad_memory_scan.head(h, heads)) + norms[1, h]
        slope = feature_slope(kvq[h].astype(jnp.float32))
        grads[1, h] = (own_grads[h] + grad_phi * slope).astype(jnp.bfloat16)

    def write_value(h):
        phi = feature(kvq[h].astype(jnp.float32)).astype(jnp.bfloat16)
        grads[2, h] = (own_grads[heads + h] + dot_nn(phi, grad_memory_scan.head(h, heads))).astype(jnp.bfloat16)

    key_pair, value_pair = pair_grads(1), pair_grads(2)
    write_key(1 - dp)
    key_pair.start()
    write_key(dp)
    write_value(1 - dp)
    value_pair.start()
    write_value(dp)
    keep_grads(1)
    keep_grads(2)
    c1.step(1)
    d1.step(1)
    key_pair.wait_recv()
    multiply(1)
    a1.step(0)
    value_pair.wait_recv()
    multiply(2)
    first_hop(b1)
    c1.step(2)
    a1.step(1)
    rows_in(d1, d_sum)
    b1.step(1)
    c1.step(3)
    d2.step(0)
    a1.step(2)
    columns_in(c1, c_sum)
    send_parts(c2, c_sum, c2_send)
    d2.step(1)
    rows_in(b1, b_sum)
    b2.step(0)
    a1.step(3)
    d2.step(2)
    b2.step(1)
    columns_in(a1, a_sum)
    send_parts(a2, a_sum, a2_send)
    b2.step(2)
    d2.step(3)

    def put(src, m, place, slot):
        return pltpu.make_async_copy(
            src.at[:, pl.ds(m * dim, dim)], out_ref.at[m, :, columns(place)], out_sem.at[slot]
        )

    swaps = [
        pair_copy(fin.at[1 - dp, :, pl.ds(m * dim, dim)], swap.at[:, pl.ds(m * dim, dim)], 4 + m) for m in range(3)
    ]

    def hand_over(m):
        swaps[m].start()
        put(fin.at[dp], m, dp, 0).start()

    b2.step(3)
    fin[:, :, 0:part] = direct_total(c2, c_sum) * scale
    for sub in (0, 1):
        fin[sub, :, part:dim] = d2.total(sub) * scale
    hand_over(0)
    fin[:, :, dim:2 * dim] = direct_total(a2, a_sum) * scale
    hand_over(1)
    for sub in (0, 1):
        fin[sub, :, 2 * dim:3 * dim] = b2.total(sub) * scale
    hand_over(2)
    for sent in (
        a1, b1, c1, d1, a2, b2, c2, d2, norm_scan, grad_norm_scan, memory_scan, grad_memory_scan,
    ):
        sent.drain()
    for copy in (*key_out, *value_out, *local_out, *query_out, *stats_out, x_out, query_pair, key_pair, value_pair):
        copy.wait_send()
    for m in range(3):
        swaps[m].wait_recv()
        put(swap, m, 1 - dp, 1).start()
    for m in range(3):
        swaps[m].wait_send()
    blended_out.wait()
    for slot in (0, 1):
        pltpu.make_async_copy(fin.at[slot], swap, out_sem.at[slot]).wait()


def layer(x, wq, wk, wv, gate, cot, scale):
    tokens, depth = x.shape
    heads = gate.shape[0]
    dim = wq.shape[1] // heads
    ny, nz = lax.axis_size("y"), lax.axis_size("z")
    wide = depth // ny
    rows = wide // nz // 2
    zs, ys = 2 * (nz - 1), 2 * (ny - 1)
    wire = lambda *shape: pltpu.VMEM(shape, jnp.bfloat16)
    real = lambda *shape: pltpu.VMEM(shape, jnp.float32)
    dma = lambda *shape: pltpu.SemaphoreType.DMA(shape)
    a1, b1 = (zs, ny, rows), (ys, wide // 2)
    part = (heads * dim // nz, dim)
    vectors = [real(heads, 1, dim), real(nz, heads, 1, dim), real(heads, 1, dim), real(ny, heads, 1, dim)]
    scan = [
        wire(nz, *part), wire(nz, *part), real(nz, *part), real(*part), real(ny, *part), wire(nz, *part),
        wire(nz, *part),
    ]
    pair = (2 * heads, tokens, dim)
    anywhere = pl.BlockSpec(memory_space=pl.ANY)
    return pl.pallas_call(
        functools.partial(layer_kernel, scale),
        out_shape=(
            jax.ShapeDtypeStruct((tokens, heads * dim), jnp.bfloat16),
            jax.ShapeDtypeStruct((3, rows, heads * dim), jnp.float32),
        ),
        in_specs=[anywhere] * 4 + [pl.BlockSpec(memory_space=pltpu.SMEM), anywhere],
        out_specs=(anywhere,) * 2,
        scratch_shapes=[
            wire(2 * tokens, depth), wire(depth, 2 * tokens), wire(3 * heads, depth, dim), wire(tokens, heads * dim), wire(tokens, heads * dim),
            wire(3 * heads, tokens, dim), wire(*pair), wire(*pair), real(*pair),
            real(heads, tokens, dim), real(heads, tokens, dim),
            real(heads, tokens, tokens), real(heads, tokens, tokens), wire(heads, tokens, dim),
            wire(heads, tokens, dim), real(heads, tokens, 1), real(heads, 8, tokens), real(heads, 8, tokens),
            wire(3, heads, tokens, dim), wire(3, 2 * tokens, dim),
            *vectors, real(heads, 1, dim), real(ny, heads, 1, dim), real(2, heads, 1, dim), real(nz, 2, heads, 1, dim),
            real(2, heads, 1, dim), *scan, *scan,
            real(3, ny, wide, dim), real(2, ny, rows, dim), real(wide, dim), real(2, ny, rows, dim // 2), real(wide, dim // 2),
            real(2, rows, 3 * dim), real(rows, 3 * dim),
            wire(*a1, dim), wire(*a1, dim), wire(*b1, dim), wire(*b1, dim),
            wire(*a1, dim // 2), wire(*a1, dim // 2), wire(*b1, dim // 2), wire(*b1, dim // 2),
            wire(ny, 2, rows, dim), wire(ny, 2, rows, dim), wire(zs, rows, dim), wire(zs, rows, dim),
            wire(ny, 2, rows, dim // 2), wire(ny, 2, rows, dim // 2), wire(zs, rows, dim // 2), wire(zs, rows, dim // 2),
            dma(2 + 3 * heads), dma(2, 5 * heads), dma(2, 7), dma(2, 2), dma(2, 2),
            dma(2, 2), dma(2, 2), dma(2, 2),
            dma(4, zs), dma(2, ys), dma(8), dma(2, 2), dma(3),
        ],
        compiler_params=pltpu.CompilerParams(
            collective_id=1, has_side_effects=True, vmem_limit_bytes=63 * 1024 * 1024
        ),
    )(x, wq, wk, wv, gate, cot)


def hand_on_kernel(a_ref, b_ref, a_out, b_out, a_held, b_held, sem):
    size = a_ref.shape[0] // PIECES
    whole = [(b_ref.at[m], b_held.at[m], b_out.at[m]) for m in range(b_ref.shape[0])]
    whole += [tuple(ref.at[pl.ds(i * size, size)] for ref in (a_ref, a_held, a_out)) for i in range(PIECES)]
    reads = [pltpu.make_async_copy(src, held, sem.at[0, i]) for i, (src, held, _) in enumerate(whole)]
    writes = [pltpu.make_async_copy(held, dst, sem.at[1, i]) for i, (_, held, dst) in enumerate(whole)]
    for read in reads:
        read.start()
    for read, write in zip(reads, writes):
        read.wait()
        write.start()
    for write in writes:
        write.wait()


def hand_on(a, b):
    anywhere = pl.BlockSpec(memory_space=pl.ANY)
    return pl.pallas_call(
        hand_on_kernel,
        out_shape=tuple(jax.ShapeDtypeStruct(v.shape, v.dtype) for v in (a, b)),
        in_specs=[anywhere] * 2,
        out_specs=(anywhere,) * 2,
        scratch_shapes=[pltpu.VMEM(v.shape, v.dtype) for v in (a, b)]
        + [pltpu.SemaphoreType.DMA((2, PIECES + b.shape[0]))],
    )(a, b)


def local(inputs, w_query, w_key, w_value, gate_bias, cotangent):
    tokens = inputs[0]
    seg_len = tokens.shape[0]
    scale = 1.0 / math.sqrt(lax.axis_size(SEQ) * lax.axis_size("dp") * seg_len)
    blended, grad_weights = layer(tokens, w_query, w_key, w_value, gate_bias, cotangent[0], scale)
    blended, grad_weights = hand_on(blended, grad_weights)
    return (blended[None], grad_weights.transpose(1, 0, 2))


def solution(mesh):
    finer = Mesh(
        mesh.devices.reshape(4, 8, mesh.shape["dp"], mesh.shape["head"]),
        ("y", "z", "dp", "head"),
    )
    placed = (
        P("dp", SEQ, None),
        P(None, "head"),
        P(None, "head"),
        P(None, "head"),
        P("head"),
        P("dp", SEQ, "head"),
    )
    return jax.shard_map(
        local,
        mesh=finer,
        in_specs=placed,
        out_specs=(P("dp", SEQ, "head"), P(SEQ_DP, None, "head")),
        check_vma=False,
    )
```
